32 devices in a mesh: seq: 8 (over z, x), head: 4 (over y, core).
Axes of the slice: x: 2, y: 2, z: 4, core: 2. Of those that a mesh axis runs over, the one named last changes fastest.
Arguments:
- query_rows: bfloat16 [1, 2048, 2048], P(None, 'seq', 'head'), may hold values from -28 to 28
- key_rows: bfloat16 [1, 2048, 2048], P(None, 'seq', 'head'), may hold values from -4 to 4
- value_rows: bfloat16 [1, 2048, 2048], P(None, 'seq', 'head'), may hold values from -6 to 6
- grad_out: bfloat16 [1, 2048, 2048], P(None, 'seq', 'head'), may hold values from -6 to 6
- rand_blocks: int32 [1, 16, 32, 3], P(None, 'head'), may hold values from 0 to 31, as said below
- global_pos: int32 [128], replicated, may hold values from 0 to 2047, as said below
Outputs:
- attended: bfloat16 [1, 2048, 2048], P(None, 'seq', 'head')
- grad_query: bfloat16 [1, 2048, 2048], P(None, 'seq', 'head')
- grad_key: bfloat16 [1, 2048, 2048], P(None, 'seq', 'head')
- grad_value: bfloat16 [1, 2048, 2048], P(None, 'seq', 'head')
The draws below stay inside these ranges and needn't reach their ends.
Inputs may be any that keep to these rules, and one draw needn't show every extreme that they name: `rand_blocks`: for each run of 4 query blocks and each run of 4 heads that start at multiples of these counts, taking the one sequence and all 3 picks together, at most 6 picks name a block of any one run of 4 key blocks that starts at a multiple of 4; in each such run of query blocks and heads some run of key blocks is named exactly 6 times. `global_pos`: distinct positions; the first and the last token of the sequence are among them.
All inputs are finite; a program needn't handle non-finite values.
Results may differ from the reference program's by a relative error of at most 0.006.
The reference program's roundings to bfloat16 on the way (of `weights_b` and `dscore_b`) count: a program that leaves them out, or rounds other values in their place, can miss the bound.
Values may be sent and summed in bfloat16 or wider, within the bound.
No kernel may reach another device: no remote copies, remote signals or barrier semaphores. Data moves between devices by JAX's collectives and lax.ppermute only.
A program may use at most 64 MiB of HBM per device.

```python
from functools import partial
import jax
import jax.numpy as jnp
from jax import lax

HEADS = 16
HEAD_DIM = 128
BLOCK = 64
RAND = 3
GLOBALS = 128
BATCH = 1
BLK_DEV = 4
HEAD_DEV = 4
NBLOCKS = 32
SEQ = 2048
NKEYS = 512


def attention_pair(key):
    base_key = jax.random.fold_in(key, 11)
    first_key, second_key = jax.random.split(base_key, 2)
    dims_all = (BATCH, SEQ, HEADS, HEAD_DIM)
    query_part = jnp.clip(jax.random.normal(first_key, dims_all, jnp.float32), -4.0, 4.0)
    key_part = jnp.clip(jax.random.normal(second_key, dims_all, jnp.float32), -4.0, 4.0)
    return (query_part.reshape(BATCH, SEQ, HEADS * HEAD_DIM), key_part.reshape(BATCH, SEQ, HEADS * HEAD_DIM))


def draw_query_rows(key, part):
    return attention_pair(key)[0].astype(jnp.bfloat16)


def draw_key_rows(key, part):
    return attention_pair(key)[1].astype(jnp.bfloat16)


def draw_rand_blocks(key, part):
    groups = NBLOCKS // BLK_DEV
    head_groups = HEADS // HEAD_DEV
    slot_count = BATCH * HEAD_DEV * BLK_DEV * RAND
    most = (slot_count + groups - 1) // groups

    def one_group(group_key):
        hold_key, place_key = jax.random.split(group_key)
        holders = jax.random.permutation(hold_key, jnp.arange(groups * most, dtype=jnp.int32) % groups)[:slot_count]
        local_block = jax.random.randint(place_key, (slot_count,), 0, BLK_DEV, dtype=jnp.int32)
        return holders * BLK_DEV + local_block
    table = jax.vmap(one_group)(jax.random.split(key, groups * head_groups))
    table = table.reshape(groups, head_groups, BATCH, HEAD_DEV, BLK_DEV, RAND).transpose(2, 1, 3, 0, 4, 5)
    return table.reshape(BATCH, HEADS, NBLOCKS, RAND).astype(jnp.int32)


def draw_global_pos(key, part):
    middle = jax.random.permutation(key, SEQ - 2)[:GLOBALS - 2].astype(jnp.int32) + 1
    return jnp.concatenate([jnp.zeros((1,), jnp.int32), middle, jnp.full((1,), SEQ - 1, jnp.int32)])


def block_scale(own_key, extent, cuts, smallest, high):
    level = 1.0
    for axis_at, parts in cuts:
        heights = jax.random.uniform(jax.random.fold_in(jax.random.fold_in(own_key, 6), axis_at), (parts,), jnp.float32, smallest / len(cuts), high / len(cuts))
        level = level * jnp.repeat(jnp.exp(heights), extent[axis_at] // parts).reshape((-1,) + (1,) * (len(extent) - 1 - axis_at))
    return level


def centred(own_key, dims, scale, most, shards=(), kind=jnp.bfloat16):
    factor_of = block_scale(own_key, dims, shards, -0.22, 0.18) if shards else 1.0
    result = jax.random.normal(own_key, dims, jnp.float32) * scale * factor_of
    return jnp.minimum(jnp.maximum(result, -most), most).astype(kind)


def setup_inputs(seed: int = 0) -> dict:
    streams_of = jax.random.split(jax.random.key(seed), 7)
    query_rows = draw_query_rows(jax.random.fold_in(streams_of[6], 71), 0)
    key_rows = draw_key_rows(jax.random.fold_in(streams_of[6], 71), 0)
    value_rows = centred(streams_of[2], (BATCH, SEQ, HEADS * HEAD_DIM), 1.0, 6.0, ((1, 8), (2, 4)))
    grad_out = centred(streams_of[3], (BATCH, SEQ, HEADS * HEAD_DIM), 1.0, 6.0, ((1, 8), (2, 4)))
    rand_blocks = draw_rand_blocks(jax.random.fold_in(streams_of[6], 71), 0)
    global_pos = draw_global_pos(jax.random.fold_in(streams_of[6], 71), 0)
    return {"query_rows": query_rows, "key_rows": key_rows, "value_rows": value_rows, "grad_out": grad_out, "rand_blocks": rand_blocks, "global_pos": global_pos}


def rounded(values):
    return lax.optimization_barrier(values.astype(jnp.bfloat16)).astype(jnp.float32)


def one_head(operands, global_pos):
    query_one, key_one, value_one, grad_one, table_one = operands
    score_scale = HEAD_DIM ** -0.5
    query_blocks = query_one.astype(jnp.float32).reshape(NBLOCKS, BLOCK, HEAD_DIM)
    grad_blocks = grad_one.astype(jnp.float32).reshape(NBLOCKS, BLOCK, HEAD_DIM)

    def key_list(token_rows):
        token_rows = token_rows.astype(jnp.float32)
        blocks = token_rows.reshape(NBLOCKS, BLOCK, HEAD_DIM)
        empty = jnp.zeros((1, BLOCK, HEAD_DIM), jnp.float32)
        padded = jnp.concatenate([empty, blocks, empty], axis=0)
        window_part = jnp.concatenate([padded[:-2], padded[1:-1], padded[2:]], axis=1)
        random_part = blocks[table_one].reshape(NBLOCKS, RAND * BLOCK, HEAD_DIM)
        global_part = jnp.broadcast_to(token_rows[global_pos][None], (NBLOCKS, GLOBALS, HEAD_DIM))
        return jnp.concatenate([window_part, random_part, global_part], axis=1)

    key_lists = key_list(key_one)
    value_lists = key_list(value_one)
    block_ids = jnp.arange(NBLOCKS)
    column_ids = jnp.arange(NKEYS)[None, :]
    middle_ok = jnp.where((column_ids >= 2 * BLOCK) & (column_ids < 3 * BLOCK), (block_ids < NBLOCKS - 1)[:, None], True)
    valid_mask = jnp.where(column_ids < BLOCK, (block_ids > 0)[:, None], middle_ok)
    scores = jnp.einsum('jqd,jkd->jqk', query_blocks, key_lists) * score_scale
    scores = jnp.where(valid_mask[:, None, :], scores, -1e30)
    row_max = jnp.max(scores, axis=-1, keepdims=True)
    log_total = row_max + jnp.log(jnp.sum(jnp.exp(scores - row_max), axis=-1, keepdims=True))
    weights = jnp.exp(scores - log_total)
    weights_b = rounded(weights)
    mixed_rows = jnp.einsum('jqk,jkd->jqd', weights_b, value_lists)
    row_delta = jnp.sum(grad_blocks * mixed_rows, axis=-1, keepdims=True)
    grad_probs = jnp.einsum('jqd,jkd->jqk', grad_blocks, value_lists)
    dscore_b = rounded(weights * (grad_probs - row_delta))
    grad_query = jnp.einsum('jqk,jkd->jqd', dscore_b, key_lists) * score_scale
    key_terms = jnp.einsum('jqk,jqd->jkd', dscore_b, query_blocks) * score_scale
    value_terms = jnp.einsum('jqk,jqd->jkd', weights_b, grad_blocks)

    def collect(terms):
        window_terms = terms[:, :3 * BLOCK].reshape(NBLOCKS, 3, BLOCK, HEAD_DIM)
        padded = jnp.zeros((NBLOCKS + 2, BLOCK, HEAD_DIM), jnp.float32)
        padded = padded.at[0:NBLOCKS].add(window_terms[:, 0])
        padded = padded.at[1:NBLOCKS + 1].add(window_terms[:, 1])
        padded = padded.at[2:NBLOCKS + 2].add(window_terms[:, 2])
        blocks = padded[1:-1]
        random_terms = terms[:, 3 * BLOCK:(3 + RAND) * BLOCK].reshape(NBLOCKS, RAND, BLOCK, HEAD_DIM)
        blocks = blocks.at[table_one].add(random_terms)
        token_rows = blocks.reshape(SEQ, HEAD_DIM)
        return token_rows.at[global_pos].add(jnp.sum(terms[:, (3 + RAND) * BLOCK:], axis=0))

    return (mixed_rows.reshape(SEQ, HEAD_DIM).astype(jnp.bfloat16),
            grad_query.reshape(SEQ, HEAD_DIM).astype(jnp.bfloat16),
            collect(key_terms).astype(jnp.bfloat16),
            collect(value_terms).astype(jnp.bfloat16))


def heads_first(array):
    return array.reshape(BATCH, SEQ, HEADS, HEAD_DIM).transpose(0, 2, 1, 3).reshape(BATCH * HEADS, SEQ, HEAD_DIM)


def heads_back(array):
    return array.reshape(BATCH, HEADS, SEQ, HEAD_DIM).transpose(0, 2, 1, 3).reshape(BATCH, SEQ, HEADS * HEAD_DIM)


def reference(query_rows, key_rows, value_rows, grad_out, rand_blocks, global_pos):
    operands = (heads_first(query_rows), heads_first(key_rows), heads_first(value_rows),
                heads_first(grad_out), rand_blocks.reshape(BATCH * HEADS, NBLOCKS, RAND))
    results = lax.map(partial(one_head, global_pos=global_pos), operands)
    return (heads_back(results[0]), heads_back(results[1]), heads_back(results[2]), heads_back(results[3]))
```

```python
import functools

import jax
import jax.numpy as jnp
from jax import lax
from jax.experimental import pallas as pl
from jax.experimental.pallas import tpu as pltpu
from jax.sharding import PartitionSpec as P

BLOCK = 64
AXES = ("seq", "head")
GROUPS = 2
VMEM = pl.BlockSpec(memory_space=pltpu.VMEM)
SMEM = pl.BlockSpec(memory_space=pltpu.SMEM)
ANY = pl.BlockSpec(memory_space=pl.ANY)
F32 = jnp.float32
BF16 = jnp.bfloat16


def dot(a, b, dims):
    return lax.dot_general(a, b, (dims, ((), ())), preferred_element_type=F32)


def round_pairs(seq_count, head_count, i):
    rounds = seq_count // 2
    pairs = []
    for s in range(seq_count):
        for head in range(head_count):
            y, c = head // 2, head % 2
            k = rounds * c + (s + i) % rounds
            pairs.append((s * head_count + head, k * head_count + 2 * y + s // rounds))
    return pairs


def pack_kernel(rounds, width, pos_ref, a_ref, b_ref, *rest):
    outs, (buf, in_sem, out_sem) = rest[:rounds], rest[rounds:]
    s = pos_ref[0]
    loads = []
    for i in range(rounds):
        col = pl.multiple_of(lax.rem(s + i, rounds) * width, width)
        for n, ref in enumerate((a_ref, b_ref)):
            copy = pltpu.make_async_copy(
                ref.at[0, :, pl.ds(col, width)], buf.at[i, n], in_sem.at[i, n]
            )
            copy.start()
            loads.append(copy)
    stores = []
    for i in range(rounds):
        loads[2 * i].wait()
        loads[2 * i + 1].wait()
        copy = pltpu.make_async_copy(buf.at[i], outs[i], out_sem.at[i])
        copy.start()
        stores.append(copy)
    for copy in stores:
        copy.wait()


def pack(where, a, b, rounds):
    _, tokens, columns = a.shape
    width = columns // rounds
    out = jax.ShapeDtypeStruct((2, tokens, width), a.dtype)
    return pl.pallas_call(
        functools.partial(pack_kernel, rounds, width),
        out_shape=[out] * rounds,
        in_specs=[SMEM, ANY, ANY],
        out_specs=[ANY] * rounds,
        scratch_shapes=[
            pltpu.VMEM((rounds, 2, tokens, width), a.dtype),
            pltpu.SemaphoreType.DMA((rounds, 2)),
            pltpu.SemaphoreType.DMA((rounds,)),
        ],
        cost_estimate=pl.CostEstimate(
            flops=0, transcendentals=0, bytes_accessed=8 * tokens * columns
        ),
        name="pack",
    )(where, a, b)


def unpack_kernel(rounds, width, pos_ref, *rest):
    ins, outs, (buf, in_sem, out_sem) = rest[:rounds], rest[rounds : rounds + 2], rest[rounds + 2 :]
    s = pos_ref[0]
    loads = []
    for i in range(rounds):
        copy = pltpu.make_async_copy(ins[i], buf.at[i], in_sem.at[i])
        copy.start()
        loads.append(copy)
    stores = []
    for i in range(rounds):
        loads[i].wait()
        col = pl.multiple_of(lax.rem(s + i, rounds) * width, width)
        for n in range(2):
            copy = pltpu.make_async_copy(
                buf.at[i, n], outs[n].at[0, :, pl.ds(col, width)], out_sem.at[i, n]
            )
            copy.start()
            stores.append(copy)
    for copy in stores:
        copy.wait()


def unpack(where, parts):
    rounds = len(parts)
    _, tokens, width = parts[0].shape
    out = jax.ShapeDtypeStruct((1, tokens, rounds * width), parts[0].dtype)
    return pl.pallas_call(
        functools.partial(unpack_kernel, rounds, width),
        out_shape=[out] * 2,
        in_specs=[SMEM] + [ANY] * rounds,
        out_specs=[ANY] * 2,
        scratch_shapes=[
            pltpu.VMEM((rounds, 2, tokens, width), parts[0].dtype),
            pltpu.SemaphoreType.DMA((rounds,)),
            pltpu.SemaphoreType.DMA((rounds, 2)),
        ],
        cost_estimate=pl.CostEstimate(
            flops=0, transcendentals=0, bytes_accessed=8 * rounds * tokens * width
        ),
        name="unpack",
    )(where, *parts)


def slot_of(run, k, h, rounds):
    half = run // rounds
    turn = lax.rem(k - lax.rem(run, rounds) + 2 * rounds, rounds)
    return jnp.where(half == h, 0, rounds) + turn


def gather_kernel(rounds, pos_ref, global_ref, *rest):
    parts, (all_ref, picked_ref, sem) = rest[: 2 * rounds], rest[2 * rounds :]
    k, h = pos_ref[0], pos_ref[1]
    tokens = all_ref.shape[1] // (2 * rounds)
    copies = []
    for n in range(2 * rounds):
        copy = pltpu.make_async_copy(
            parts[n], all_ref.at[:, pl.ds(n * tokens, tokens), :], sem.at[n]
        )
        copy.start()
        copies.append(copy)
    place = global_ref[...]
    row = slot_of(place // tokens, k, h, rounds) * tokens + lax.rem(place, tokens)
    ids = lax.broadcasted_iota(jnp.int32, (row.shape[0], all_ref.shape[1]), 1)
    hot = jnp.where(ids == row, 1.0, 0.0).astype(BF16)
    for copy in copies:
        copy.wait()
    for n in range(2):
        picked_ref[n] = dot(hot, all_ref[n], ((1,), (0,))).astype(BF16)


def gather(where, global_pos, own, other):
    rounds = len(own)
    _, tokens, width = own[0].shape
    count = global_pos.shape[0]
    return pl.pallas_call(
        functools.partial(gather_kernel, rounds),
        out_shape=[
            jax.ShapeDtypeStruct((2, 2 * rounds * tokens, width), BF16),
            jax.ShapeDtypeStruct((2, count, width), BF16),
        ],
        in_specs=[SMEM, VMEM] + [ANY] * (2 * rounds),
        out_specs=[VMEM, VMEM],
        scratch_shapes=[pltpu.SemaphoreType.DMA((2 * rounds,))],
        cost_estimate=pl.CostEstimate(
            flops=8 * count * rounds * tokens * width,
            transcendentals=0,
            bytes_accessed=16 * rounds * tokens * width,
        ),
        name="gather",
    )(where, global_pos.reshape(count, 1), *own, *other)


def key_rows_of(pos_ref, table_ref, rounds, run_blocks, turn, block, picks):
    k, h = pos_ref[0], pos_ref[1]
    total = 2 * rounds * run_blocks
    run = h * rounds + lax.rem(k - turn + 2 * rounds, rounds)
    query_block = run * run_blocks + block

    def row(key_block):
        slot = slot_of(key_block // run_blocks, k, h, rounds)
        return pl.multiple_of(
            (slot * run_blocks + lax.rem(key_block, run_blocks)) * BLOCK, BLOCK
        )

    rows = [
        row(jnp.clip(query_block + step, 0, total - 1)) for step in (-1, 0, 1)
    ] + [row(table_ref[query_block * picks + n]) for n in range(picks)]
    return query_block, rows


def attend_kernel(rounds, run_blocks, picks, turns, pos_ref, table_ref, all_ref, picked_ref, *rest):
    count = len(turns)
    sides, outs = rest[:count], rest[count:]
    mixes, keeps = outs[:count], outs[count:]
    total = 2 * rounds * run_blocks
    width = all_ref.shape[2]
    scale = width**-0.5
    for n, turn in enumerate(turns):
        for block in range(run_blocks):
            query_block, rows = key_rows_of(
                pos_ref, table_ref, rounds, run_blocks, turn, block, picks
            )
            mine = slice(block * BLOCK, (block + 1) * BLOCK)
            query = sides[n][0, mine]
            grad = sides[n][1, mine]
            keys = jnp.concatenate(
                [all_ref[0, pl.ds(r, BLOCK)] for r in rows] + [picked_ref[0]], axis=0
            )
            values = jnp.concatenate(
                [all_ref[1, pl.ds(r, BLOCK)] for r in rows] + [picked_ref[1]], axis=0
            )
            scores = dot(query, keys, ((1,), (1,))) * scale
            column = lax.broadcasted_iota(jnp.int32, (1, keys.shape[0]), 1)
            first = (column < BLOCK) & (query_block == 0)
            last = (
                (column >= 2 * BLOCK) & (column < 3 * BLOCK) & (query_block == total - 1)
            )
            scores = jnp.where(first | last, -1e30, scores)
            peak = jnp.max(scores, axis=1, keepdims=True)
            powers = jnp.exp(scores - peak)
            weights = powers * (1.0 / jnp.sum(powers, axis=1, keepdims=True))
            weights_b = weights.astype(BF16)
            mixed = dot(weights_b, values, ((1,), (0,)))
            delta = jnp.sum(grad.astype(F32) * mixed, axis=1, keepdims=True)
            probs = dot(grad, values, ((1,), (1,)))
            dscore_b = (weights * (probs - delta)).astype(BF16)
            grad_query = dot(dscore_b, keys, ((1,), (0,))) * scale
            mixes[n][0, mine] = mixed.astype(BF16)
            mixes[n][1, mine] = grad_query.astype(BF16)
            keeps[n][0, mine] = dscore_b
            keeps[n][1, mine] = weights_b


def attend(where, table, all_kv, picked, sides, turns, rounds, picks):
    _, tokens, width = sides[0].shape
    run_blocks = tokens // BLOCK
    entries = (3 + picks) * BLOCK + picked.shape[1]
    count = len(turns)
    outs = pl.pallas_call(
        functools.partial(attend_kernel, rounds, run_blocks, picks, turns),
        out_shape=[jax.ShapeDtypeStruct((2, tokens, width), BF16)] * count
        + [jax.ShapeDtypeStruct((2, tokens, entries), BF16)] * count,
        in_specs=[SMEM, SMEM, VMEM, VMEM] + [VMEM] * count,
        out_specs=[VMEM] * (2 * count),
        cost_estimate=pl.CostEstimate(
            flops=8 * count * tokens * entries * width,
            transcendentals=count * tokens * entries,
            bytes_accessed=4 * all_kv.size,
        ),
        name="attend",
    )(where, table, all_kv, picked, *sides)
    return outs[:count], outs[count:]


def key_grads_kernel(rounds, run_blocks, picks, pos_ref, table_ref, *rest):
    sides, keeps, (own_ref, other_ref, acc) = (
        rest[:rounds],
        rest[rounds : 2 * rounds],
        rest[2 * rounds :],
    )
    listed = (3 + picks) * BLOCK
    half_rows = acc.shape[1] // 2
    acc[...] = jnp.zeros_like(acc)
    for n in range(2):
        shared = None
        for turn in range(rounds):
            part = dot(keeps[turn][n, :, listed:], sides[turn][n], ((0,), (0,)))
            shared = part if shared is None else shared + part
        own_ref[n, half_rows:] = shared
        other_ref[n, half_rows:] = shared
    for turn in range(rounds):
        for block in range(run_blocks):
            _, rows = key_rows_of(pos_ref, table_ref, rounds, run_blocks, turn, block, picks)
            mine = slice(block * BLOCK, (block + 1) * BLOCK)
            for n in range(2):
                part = dot(keeps[turn][n, mine, :listed], sides[turn][n, mine], ((0,), (0,)))
                for m, r in enumerate(rows):
                    acc[n, pl.ds(r, BLOCK)] += part[m * BLOCK : (m + 1) * BLOCK]
    for n in range(2):
        own_ref[n, :half_rows] = acc[n, :half_rows]
        other_ref[n, :half_rows] = acc[n, half_rows:]


def key_grads(where, table, sides, keeps, picks):
    rounds = len(sides)
    _, tokens, width = sides[0].shape
    run_blocks = tokens // BLOCK
    entries = keeps[0].shape[2]
    count = entries - (3 + picks) * BLOCK
    out = jax.ShapeDtypeStruct((2, rounds * tokens + count, width), F32)
    return pl.pallas_call(
        functools.partial(key_grads_kernel, rounds, run_blocks, picks),
        out_shape=[out, out],
        in_specs=[SMEM, SMEM] + [VMEM] * (2 * rounds),
        out_specs=[VMEM, VMEM],
        scratch_shapes=[pltpu.VMEM((2, 2 * rounds * tokens, width), F32)],
        cost_estimate=pl.CostEstimate(
            flops=4 * rounds * tokens * entries * width,
            transcendentals=0,
            bytes_accessed=4 * rounds * tokens * (entries + 4 * width),
        ),
        name="key_grads",
    )(where, table, *sides, *keeps)


def total_kernel(rounds, pos_ref, global_ref, own_ref, came_ref, *rest):
    outs, acc = rest[:rounds], rest[rounds]
    k, h = pos_ref[0], pos_ref[1]
    width = own_ref.shape[2]
    tokens = outs[0].shape[1]
    half_rows = rounds * tokens
    scale = width**-0.5
    acc[:, : own_ref.shape[1]] = own_ref[...] + came_ref[...]

    def step(t, carry):
        place = global_ref[t]
        row = slot_of(place // tokens, k, h, rounds) * tokens + lax.rem(place, tokens)
        row = jnp.where(row < half_rows, row, own_ref.shape[1])
        for n in range(2):
            acc[n, pl.ds(row, 1)] += acc[n, pl.ds(half_rows + t, 1)]
        return carry

    lax.fori_loop(0, global_ref.shape[0], step, 0, unroll=4)
    for i in range(rounds):
        mine = slice(i * tokens, (i + 1) * tokens)
        outs[i][0] = (acc[0, mine] * scale).astype(BF16)
        outs[i][1] = acc[1, mine].astype(BF16)


def total(where, global_pos, own, came, rounds):
    rows, width = own.shape[1:]
    tokens = (rows - global_pos.shape[0]) // rounds
    return pl.pallas_call(
        functools.partial(total_kernel, rounds),
        out_shape=[jax.ShapeDtypeStruct((2, tokens, width), BF16)] * rounds,
        in_specs=[SMEM, SMEM, VMEM, VMEM],
        out_specs=[VMEM] * rounds,
        scratch_shapes=[pltpu.VMEM((2, rows + 8, width), F32)],
        cost_estimate=pl.CostEstimate(
            flops=4 * rows * width, transcendentals=0, bytes_accessed=20 * rows * width
        ),
        name="total",
    )(where, global_pos, own, came)


def by_heads(query_rows, key_rows, value_rows, grad_out, rand_blocks, global_pos):
    seq_count, head_count = lax.axis_size("seq"), lax.axis_size("head")
    _, rounds, total_blocks, picks = rand_blocks.shape
    seq_index, head_index = lax.axis_index("seq"), lax.axis_index("head")
    where = jnp.stack([seq_index, head_index % 2]).astype(jnp.int32)
    sibling = [(i, i ^ 1) for i in range(head_count)]
    there = [round_pairs(seq_count, head_count, i) for i in range(rounds)]
    back = [[(j, i) for i, j in pairs] for pairs in there]

    def send(parts, pairs):
        return [lax.ppermute(part, AXES, p) for part, p in zip(parts, pairs)]

    kv = send(pack(where, key_rows, value_rows, rounds), there)
    sides = send(pack(where, query_rows, grad_out, rounds), there)
    other_table = lax.ppermute(rand_blocks, "head", sibling)
    kv_other = [lax.ppermute(part, "head", sibling) for part in kv]
    mine = (seq_index // rounds) == (head_index % 2)
    tables = jnp.where(mine, rand_blocks, other_table)
    table = lax.dynamic_index_in_dim(tables[0], seq_index % rounds, 0, keepdims=False)
    table = table.reshape(total_blocks * picks)

    all_kv, picked = gather(where, global_pos, kv, kv_other)
    mixes, keeps = [], []
    for n in range(GROUPS):
        turns = tuple(range(n * rounds // GROUPS, (n + 1) * rounds // GROUPS))
        mix, keep = attend(
            where, table, all_kv, picked, [sides[t] for t in turns], turns, rounds, picks
        )
        mixes += mix
        keeps += keep
    mixes = send(mixes, back)
    own, other = key_grads(where, table, sides, keeps, picks)
    came = lax.ppermute(other, "head", sibling)
    grads = send(total(where, global_pos, own, came, rounds), back)
    attended, grad_query = unpack(where, mixes)
    grad_key, grad_value = unpack(where, grads)
    return attended, grad_query, grad_key, grad_value


def extended_2(value, sides, width):
    for axis, dim in sides:
        size, length = (lax.axis_size(axis), value.shape[dim])
        up = [(i, (i + 1) % size) for i in range(size - 1)]
        down = [(j, i) for i, j in up]
        last = lax.slice_in_dim(value, length - width, length, axis=dim)
        first = lax.slice_in_dim(value, 0, width, axis=dim)
        before = lax.ppermute(last, axis, up)
        after = lax.ppermute(first, axis, down)
        value = jnp.concatenate([before, value, after], axis=dim)
    return value


def by_blocks(query_rows, key_rows, value_rows, grad_out, rand_blocks, global_pos):
    batch_count, tok_local, columns = query_rows.shape
    seq_count = lax.axis_size("seq")
    seq_index = lax.axis_index("seq")
    heads_local = rand_blocks.shape[1]
    total_blocks = rand_blocks.shape[2]
    pick_count = rand_blocks.shape[3]
    head_dim = columns // heads_local
    blocks_local = tok_local // BLOCK
    score_scale = head_dim ** (-0.5)
    slot_count = batch_count * heads_local * blocks_local * pick_count
    capacity = (slot_count + seq_count - 1) // seq_count
    buffer_rows = seq_count * capacity
    f32 = jnp.float32
    bf16 = jnp.bfloat16

    def to_blocks(array):
        return array.reshape(batch_count, blocks_local, BLOCK, heads_local, head_dim).transpose(
            0, 3, 1, 2, 4
        )

    def from_blocks(array):
        return array.transpose(0, 2, 3, 1, 4).reshape(batch_count, tok_local, columns)

    def pair_blocks(array):
        return array.reshape(2, batch_count, blocks_local, BLOCK, heads_local, head_dim).transpose(
            0, 1, 4, 2, 3, 5
        )

    def global_sum(array):
        return lax.psum(array, "seq")

    key_value = jnp.stack([key_rows, value_rows])
    edge_rows = jnp.concatenate([key_value[:, :, :BLOCK], key_value[:, :, -BLOCK:]], axis=2)
    extended = extended_2(edge_rows, (("seq", 2),), BLOCK)
    padded = jnp.concatenate([extended[:, :, :BLOCK], key_value, extended[:, :, -BLOCK:]], axis=2)

    def shifted(start):
        return pair_blocks(padded[:, :, start : start + tok_local])

    window_lists = jnp.concatenate([shifted(0), shifted(BLOCK), shifted(2 * BLOCK)], axis=4)
    my_table = lax.dynamic_slice_in_dim(
        rand_blocks, seq_index * blocks_local, blocks_local, 2
    ).reshape(slot_count)
    holder = my_table // blocks_local
    holder_hot = (holder[:, None] == jnp.arange(seq_count)[None, :]).astype(jnp.int32)
    holder_rank = jnp.sum((jnp.cumsum(holder_hot, axis=0) - 1) * holder_hot, axis=1)
    position = holder * capacity + holder_rank
    requests = rand_blocks.reshape(batch_count, heads_local, seq_count, blocks_local, pick_count)
    requests = requests.transpose(2, 0, 1, 3, 4).reshape(seq_count, slot_count)
    wanted = (requests // blocks_local == seq_index).astype(jnp.int32)
    wanted_rank = jnp.cumsum(wanted, axis=1) - 1
    chosen = wanted[:, None, :] * (
        wanted_rank[:, None, :] == jnp.arange(capacity)[None, :, None]
    ).astype(jnp.int32)
    slot_live = (jnp.sum(chosen, axis=2) > 0).reshape(buffer_rows)
    slot_index = jnp.sum(chosen * jnp.arange(slot_count)[None, None, :], axis=2)
    which_batch = slot_index // (heads_local * blocks_local * pick_count)
    which_head = slot_index // (blocks_local * pick_count) % heads_local
    which_block = jnp.take_along_axis(requests, slot_index, axis=1) % blocks_local
    stacked = key_value.reshape(
        2, batch_count, blocks_local, BLOCK, heads_local, head_dim
    ).transpose(1, 2, 4, 0, 3, 5)
    outgoing = stacked[which_batch, which_block, which_head].reshape(
        buffer_rows, 2, BLOCK, head_dim
    )
    incoming = lax.all_to_all(outgoing, "seq", split_axis=0, concat_axis=0, tiled=True)
    fetched = incoming[position].reshape(
        batch_count, heads_local, blocks_local, pick_count, 2, BLOCK, head_dim
    )
    fetched = fetched.transpose(4, 0, 1, 2, 3, 5, 6).reshape(
        2, batch_count, heads_local, blocks_local, pick_count * BLOCK, head_dim
    )
    local_pos = global_pos - seq_index * tok_local
    pick_hot = (local_pos[:, None] == jnp.arange(tok_local)[None, :]).astype(bf16)
    owned_rows = jnp.einsum("gt,pbtc->pbgc", pick_hot, key_value, preferred_element_type=f32)
    shared = global_sum(owned_rows).astype(bf16)
    globals_count = shared.shape[2]
    global_kv = shared.reshape(2, batch_count, globals_count, heads_local, head_dim).transpose(
        0, 1, 3, 2, 4
    )
    global_kv = jnp.broadcast_to(
        global_kv[:, :, :, None],
        (2, batch_count, heads_local, blocks_local, globals_count, head_dim),
    )
    lists_all = jnp.concatenate([window_lists, fetched, global_kv], axis=4)
    key_lists = lists_all[0]
    value_lists = lists_all[1]
    key_count = key_lists.shape[3]
    block_ids = seq_index * blocks_local + jnp.arange(blocks_local)
    column_ids = jnp.arange(key_count)[None, :]
    middle_ok = jnp.where(
        (column_ids >= 2 * BLOCK) & (column_ids < 3 * BLOCK),
        (block_ids < total_blocks - 1)[:, None],
        True,
    )
    valid_mask = jnp.where(column_ids < BLOCK, (block_ids > 0)[:, None], middle_ok)
    query_blocks = to_blocks(query_rows)
    grad_blocks = to_blocks(grad_out)
    scores = (
        jnp.einsum("bhjqd,bhjkd->bhjqk", query_blocks, key_lists, preferred_element_type=f32)
        * score_scale
    )
    scores = jnp.where(valid_mask[None, None, :, None, :], scores, -1e30)
    row_max = jnp.max(scores, axis=-1, keepdims=True)
    log_total = row_max + jnp.log(jnp.sum(jnp.exp(scores - row_max), axis=-1, keepdims=True))
    weights = jnp.exp(scores - log_total)
    weights_b = weights.astype(bf16)
    mixed_rows = jnp.einsum(
        "bhjqk,bhjkd->bhjqd", weights_b, value_lists, preferred_element_type=f32
    )
    attended = from_blocks(mixed_rows.astype(bf16))
    row_delta = jnp.sum(grad_blocks.astype(f32) * mixed_rows, axis=-1, keepdims=True)
    grad_probs = jnp.einsum(
        "bhjqd,bhjkd->bhjqk", grad_blocks, value_lists, preferred_element_type=f32
    )
    dscore_b = (weights * (grad_probs - row_delta)).astype(bf16)
    grad_query = (
        jnp.einsum("bhjqk,bhjkd->bhjqd", dscore_b, key_lists, preferred_element_type=f32)
        * score_scale
    )

    def key_grads(lower, upper):
        key_part = (
            jnp.einsum(
                "bhjqk,bhjqd->bhjkd",
                dscore_b[..., lower:upper],
                query_blocks,
                preferred_element_type=f32,
            )
            * score_scale
        )
        value_part = jnp.einsum(
            "bhjqk,bhjqd->bhjkd",
            weights_b[..., lower:upper],
            grad_blocks,
            preferred_element_type=f32,
        )
        return jnp.stack([key_part, value_part])

    window_cols = 3 * BLOCK
    random_cols = pick_count * BLOCK
    window_grads = key_grads(0, window_cols).reshape(
        2, batch_count, heads_local, blocks_local, 3, BLOCK, head_dim
    )
    padded_grads = jnp.pad(
        window_grads[:, :, :, :, 0], ((0, 0), (0, 0), (0, 0), (0, 2), (0, 0), (0, 0))
    )
    padded_grads = padded_grads + jnp.pad(
        window_grads[:, :, :, :, 1], ((0, 0), (0, 0), (0, 0), (1, 1), (0, 0), (0, 0))
    )
    padded_grads = padded_grads + jnp.pad(
        window_grads[:, :, :, :, 2], ((0, 0), (0, 0), (0, 0), (2, 0), (0, 0), (0, 0))
    )
    own_grads = padded_grads[:, :, :, 1:-1]
    rim_grads = jnp.stack([padded_grads[:, :, :, 0], padded_grads[:, :, :, -1]], axis=3)
    returned = extended_2(rim_grads.astype(jnp.bfloat16), (("seq", 3),), 1).astype(rim_grads.dtype)
    own_grads = own_grads.at[:, :, :, 0].add(returned[:, :, :, 0])
    own_grads = own_grads.at[:, :, :, -1].add(returned[:, :, :, 3])
    global_grads = jnp.sum(key_grads(window_cols + random_cols, key_count), axis=3)
    global_grads = global_grads.transpose(0, 1, 3, 2, 4).reshape(
        2, batch_count, globals_count, columns
    )
    global_summed = global_sum(global_grads)
    inside = (local_pos >= 0) & (local_pos < tok_local)
    safe_pos = jnp.where(inside, local_pos, tok_local)
    global_local = (
        jnp.zeros((2, batch_count, tok_local, columns), f32)
        .at[:, :, safe_pos]
        .add(global_summed, mode="drop")
    )
    global_part = pair_blocks(global_local)
    target = ((which_batch * blocks_local + which_block) * heads_local + which_head).reshape(
        buffer_rows
    )
    random_grads = key_grads(window_cols, window_cols + random_cols)
    per_slot = random_grads.reshape(
        2, batch_count, heads_local, blocks_local, pick_count, BLOCK, head_dim
    )
    per_slot = per_slot.transpose(1, 2, 3, 4, 0, 5, 6).reshape(slot_count, 2, BLOCK, head_dim)
    sending = jnp.zeros((buffer_rows, 2, BLOCK, head_dim), f32).at[position].set(per_slot)
    arrived = lax.all_to_all(
        sending.astype(jnp.bfloat16), "seq", split_axis=0, concat_axis=0, tiled=True
    ).astype(sending.dtype)
    kept = jnp.where(slot_live[:, None, None, None], arrived, 0.0)
    summed = (
        jnp.zeros((batch_count * blocks_local * heads_local, 2, BLOCK, head_dim), f32)
        .at[target]
        .add(kept)
    )
    random_part = summed.reshape(
        batch_count, blocks_local, heads_local, 2, BLOCK, head_dim
    ).transpose(3, 0, 2, 1, 4, 5)
    total_grads = own_grads + random_part + global_part
    grad_key = from_blocks(total_grads[0].astype(bf16))
    grad_value = from_blocks(total_grads[1].astype(bf16))
    return (attended, from_blocks(grad_query.astype(bf16)), grad_key, grad_value)


def body(query_rows, key_rows, value_rows, grad_out, rand_blocks, global_pos):
    seq_count, head_count = lax.axis_size("seq"), lax.axis_size("head")
    batch_count, heads_local = rand_blocks.shape[:2]
    whole_heads = seq_count == 2 * heads_local and head_count % 2 == 0 and batch_count == 1
    form = by_heads if whole_heads else by_blocks
    return form(query_rows, key_rows, value_rows, grad_out, rand_blocks, global_pos)


def solution(mesh):
    return jax.shard_map(
        body,
        mesh=mesh,
        in_specs=(
            P(None, "seq", "head"),
            P(None, "seq", "head"),
            P(None, "seq", "head"),
            P(None, "seq", "head"),
            P(None, "head", None, None),
            P(),
        ),
        out_specs=(
            P(None, "seq", "head"),
            P(None, "seq", "head"),
            P(None, "seq", "head"),
            P(None, "seq", "head"),
        ),
        check_vma=False,
    )
```

```python
import functools

import jax
import jax.numpy as jnp
from jax import lax
from jax.experimental import pallas as pl
from jax.experimental.pallas import tpu as pltpu
from jax.sharding import PartitionSpec as P


BLOCK = 64
AXES = ("seq", "head")
GROUPS = 2
CHUNK = 2
VMEM = pl.BlockSpec(memory_space=pltpu.VMEM)
SMEM = pl.BlockSpec(memory_space=pltpu.SMEM)
HBM = pl.BlockSpec(memory_space=pltpu.HBM)
F32 = jnp.float32
BF16 = jnp.bfloat16


def dot(a, b, dims):
    return lax.dot_general(a, b, (dims, ((), ())), preferred_element_type=F32)


def round_pairs(seq_count, head_count, i):
    rounds = seq_count // 2
    pairs = []
    for s in range(seq_count):
        for head in range(head_count):
            y, c = head // 2, head % 2
            k = rounds * c + (s + i) % rounds
            pairs.append((s * head_count + head, k * head_count + 2 * y + s // rounds))
    return pairs


def pack_kernel(rounds, width, pos_ref, a_ref, b_ref, *rest):
    outs, (buf, in_sem, out_sem) = rest[:rounds], rest[rounds:]
    s = pos_ref[0]
    loads = []
    for i in range(rounds):
        col = pl.multiple_of(lax.rem(s + i, rounds) * width, width)
        for n, ref in enumerate((a_ref, b_ref)):
            copy = pltpu.make_async_copy(
                ref.at[0, :, pl.ds(col, width)], buf.at[i, n], in_sem.at[i, n]
            )
            copy.start()
            loads.append(copy)
    stores = []
    for i in range(rounds):
        loads[2 * i].wait()
        loads[2 * i + 1].wait()
        copy = pltpu.make_async_copy(buf.at[i], outs[i], out_sem.at[i])
        copy.start()
        stores.append(copy)
    for copy in stores:
        copy.wait()


def pack(where, a, b, rounds):
    _, tokens, columns = a.shape
    width = columns // rounds
    out = jax.ShapeDtypeStruct((2, tokens, width), a.dtype)
    return pl.pallas_call(
        functools.partial(pack_kernel, rounds, width),
        out_shape=[out] * rounds,
        in_specs=[SMEM, HBM, HBM],
        out_specs=[HBM] * rounds,
        scratch_shapes=[
            pltpu.VMEM((rounds, 2, tokens, width), a.dtype),
            pltpu.SemaphoreType.DMA((rounds, 2)),
            pltpu.SemaphoreType.DMA((rounds,)),
        ],
        cost_estimate=pl.CostEstimate(
            flops=0, transcendentals=0, bytes_accessed=8 * tokens * columns
        ),
        name="pack",
    )(where, a, b)


def unpack_kernel(rounds, width, pos_ref, *rest):
    ins, outs, (buf, in_sem, out_sem) = rest[:rounds], rest[rounds : rounds + 2], rest[rounds + 2 :]
    s = pos_ref[0]
    loads = []
    for i in range(rounds):
        copy = pltpu.make_async_copy(ins[i], buf.at[i], in_sem.at[i])
        copy.start()
        loads.append(copy)
    stores = []
    for i in range(rounds):
        loads[i].wait()
        col = pl.multiple_of(lax.rem(s + i, rounds) * width, width)
        for n in range(2):
            copy = pltpu.make_async_copy(
                buf.at[i, n], outs[n].at[0, :, pl.ds(col, width)], out_sem.at[i, n]
            )
            copy.start()
            stores.append(copy)
    for copy in stores:
        copy.wait()


def unpack(where, parts):
    rounds = len(parts)
    _, tokens, width = parts[0].shape
    out = jax.ShapeDtypeStruct((1, tokens, rounds * width), parts[0].dtype)
    return pl.pallas_call(
        functools.partial(unpack_kernel, rounds, width),
        out_shape=[out] * 2,
        in_specs=[SMEM] + [HBM] * rounds,
        out_specs=[HBM] * 2,
        scratch_shapes=[
            pltpu.VMEM((rounds, 2, tokens, width), parts[0].dtype),
            pltpu.SemaphoreType.DMA((rounds,)),
            pltpu.SemaphoreType.DMA((rounds, 2)),
        ],
        cost_estimate=pl.CostEstimate(
            flops=0, transcendentals=0, bytes_accessed=8 * rounds * tokens * width
        ),
        name="unpack",
    )(where, *parts)


def slot_of(run, k, h, rounds):
    turn = (k - run % rounds) % rounds
    return jnp.where(run // rounds == h, 0, rounds) + turn


def first_rows(table, k, h, rounds, run_blocks):
    total, _ = table.shape
    runs = h * rounds + (k - jnp.arange(rounds)) % rounds
    blocks = (runs[:, None] * run_blocks + jnp.arange(run_blocks)[None, :]).reshape(-1)
    window = jnp.clip(blocks[:, None] + jnp.arange(-1, 2)[None, :], 0, total - 1)
    named = jnp.concatenate([window, table[blocks]], axis=1)
    place = slot_of(named // run_blocks, k, h, rounds) * run_blocks + named % run_blocks
    edge = (blocks == 0) + 2 * (blocks == total - 1)
    return (place * BLOCK).astype(jnp.int32).reshape(-1), edge.astype(jnp.int32)


def gather_kernel(rounds, rows_ref, *rest):
    parts, (all_ref, picked_ref, sem) = rest[: 2 * rounds], rest[2 * rounds :]
    tokens = all_ref.shape[1] // (2 * rounds)
    copies = []
    for n in range(2 * rounds):
        copy = pltpu.make_async_copy(
            parts[n], all_ref.at[:, pl.ds(n * tokens, tokens), :], sem.at[n]
        )
        copy.start()
        copies.append(copy)
    rows = rows_ref[...]
    count = rows.shape[0]
    sums = [None, None]
    for n in range(2 * rounds):
        ids = lax.broadcasted_iota(jnp.int32, (count, tokens), 1) + n * tokens
        hot = jnp.where(ids == rows, 1.0, 0.0).astype(BF16)
        copies[n].wait()
        for m in range(2):
            part = dot(hot, all_ref[m, n * tokens : (n + 1) * tokens], ((1,), (0,)))
            sums[m] = part if n == 0 else sums[m] + part
    for m in range(2):
        picked_ref[m] = sums[m].astype(BF16)


def gather(global_rows, own, other):
    rounds = len(own)
    _, tokens, width = own[0].shape
    count = global_rows.shape[0]
    return pl.pallas_call(
        functools.partial(gather_kernel, rounds),
        out_shape=[
            jax.ShapeDtypeStruct((2, 2 * rounds * tokens, width), BF16),
            jax.ShapeDtypeStruct((2, count, width), BF16),
        ],
        in_specs=[VMEM] + [HBM] * (2 * rounds),
        out_specs=[VMEM, VMEM],
        scratch_shapes=[pltpu.SemaphoreType.DMA((2 * rounds,))],
        cost_estimate=pl.CostEstimate(
            flops=8 * count * rounds * tokens * width,
            transcendentals=0,
            bytes_accessed=16 * rounds * tokens * width,
        ),
        name="gather",
    )(global_rows.reshape(count, 1), *own, *other)


def attend_kernel(run_blocks, listed, turns, rows_ref, edge_ref, all_ref, picked_ref, *rest):
    count = len(turns)
    sides, mixes, keeps = rest[:count], rest[count : 2 * count], rest[2 * count : 3 * count]
    side_buf, mix_buf, in_sem, out_sem = rest[3 * count :]
    loads, stores = [], []
    for n in range(count):
        copy = pltpu.make_async_copy(sides[n], side_buf.at[n], in_sem.at[n])
        copy.start()
        loads.append(copy)
    scale = all_ref.shape[2] ** -0.5
    column = lax.broadcasted_iota(jnp.int32, (1, 4 * BLOCK), 1)

    def begin(n, block):
        mine = slice(block * BLOCK, (block + 1) * BLOCK)
        query, grad = side_buf[n, 0, mine], side_buf[n, 1, mine]
        index = turns[n] * run_blocks + block
        rows = [
            pl.multiple_of(rows_ref[index * listed + m], BLOCK) for m in range(listed)
        ]
        keys, values = [
            jnp.concatenate(
                [all_ref[m, pl.ds(r, BLOCK)] for r in rows] + [picked_ref[m]], axis=0
            )
            for m in range(2)
        ]
        scores = dot(query, keys, ((1,), (1,))) * scale
        probs = dot(grad, values, ((1,), (1,)))
        edge = edge_ref[index]
        out = ((column < BLOCK) & (edge % 2 == 1)) | (
            (column >= 2 * BLOCK) & (column < 3 * BLOCK) & (edge >= 2)
        )
        near = jnp.where(out, -1e30, scores[:, : 4 * BLOCK])
        scores = jnp.concatenate([near, scores[:, 4 * BLOCK :]], axis=1)
        return n, mine, keys, values, scores, probs

    def finish(state):
        weighed = []
        for n, mine, keys, values, scores, probs in state:
            peak = jnp.max(scores, axis=1, keepdims=True)
            powers = jnp.exp(scores - peak)
            weights = powers * (1.0 / jnp.sum(powers, axis=1, keepdims=True))
            weights_b = weights.astype(BF16)
            keeps[n][1, mine] = weights_b
            weighed.append((weights, weights_b))
        scored = []
        for (n, mine, keys, values, scores, probs), (weights, weights_b) in zip(state, weighed):
            delta = jnp.sum(weights_b.astype(F32) * probs, axis=1, keepdims=True)
            dscore_b = (weights * (probs - delta)).astype(BF16)
            keeps[n][0, mine] = dscore_b
            scored.append(dscore_b)
        for (n, mine, keys, values, _, _), (_, weights_b), dscore_b in zip(
            state, weighed, scored
        ):
            mixed = dot(weights_b, values, ((1,), (0,)))
            grad_query = dot(dscore_b, keys, ((1,), (0,))) * scale
            mix_buf[n, 0, mine] = mixed.astype(BF16)
            mix_buf[n, 1, mine] = grad_query.astype(BF16)

    held = None
    for n in range(count):
        loads[n].wait()
        for block in range(0, run_blocks, CHUNK):
            state = [begin(n, b) for b in range(block, block + CHUNK)]
            if held is not None:
                finish(held)
                if block == 0:
                    copy = pltpu.make_async_copy(mix_buf.at[n - 1], mixes[n - 1], out_sem.at[n - 1])
                    copy.start()
                    stores.append(copy)
            held = state
    finish(held)
    copy = pltpu.make_async_copy(mix_buf.at[count - 1], mixes[count - 1], out_sem.at[count - 1])
    copy.start()
    stores.append(copy)
    for copy in stores:
        copy.wait()


def attend(rows, edge, all_kv, picked, sides, turns):
    _, tokens, width = sides[0].shape
    run_blocks = tokens // BLOCK
    listed = rows.shape[0] // edge.shape[0]
    entries = listed * BLOCK + picked.shape[1]
    count = len(turns)
    outs = pl.pallas_call(
        functools.partial(attend_kernel, run_blocks, listed, turns),
        out_shape=[jax.ShapeDtypeStruct((2, tokens, width), BF16)] * count
        + [jax.ShapeDtypeStruct((2, tokens, entries), BF16)] * count,
        in_specs=[SMEM, SMEM, VMEM, VMEM] + [HBM] * count,
        out_specs=[HBM] * count + [VMEM] * count,
        scratch_shapes=[
            pltpu.VMEM((count, 2, tokens, width), BF16),
            pltpu.VMEM((count, 2, tokens, width), BF16),
            pltpu.SemaphoreType.DMA((count,)),
            pltpu.SemaphoreType.DMA((count,)),
        ],
        cost_estimate=pl.CostEstimate(
            flops=8 * count * tokens * entries * width,
            transcendentals=count * tokens * entries,
            bytes_accessed=4 * all_kv.size,
        ),
        name="attend",
    )(rows, edge, all_kv, picked, *sides)
    return outs[:count], outs[count:]


def key_grads_kernel(rounds, run_blocks, listed, rows_ref, *rest):
    sides, keeps = rest[:rounds], rest[rounds : 2 * rounds]
    acc, other_ref, side_buf, in_sem, out_sem = rest[2 * rounds :]
    loads = []
    for turn in range(rounds):
        copy = pltpu.make_async_copy(sides[turn], side_buf.at[turn], in_sem.at[turn])
        copy.start()
        loads.append(copy)
    entries = listed * BLOCK
    half = rounds * run_blocks * BLOCK
    acc[:, : 2 * half] = jnp.zeros((2, 2 * half, acc.shape[2]), F32)
    for copy in loads:
        copy.wait()
    for n in range(2):
        shared = None
        for turn in range(rounds):
            part = dot(keeps[turn][n, :, entries:], side_buf[turn, n], ((0,), (0,)))
            shared = part if shared is None else shared + part
        acc[n, 2 * half :] = shared
    for turn in range(rounds):
        for block in range(run_blocks):
            index = turn * run_blocks + block
            mine = slice(block * BLOCK, (block + 1) * BLOCK)
            parts = [
                dot(keeps[turn][n, mine, :entries], side_buf[turn, n, mine], ((0,), (0,)))
                for n in range(2)
            ]
            for m in range(listed):
                row = pl.multiple_of(rows_ref[index * listed + m], BLOCK)
                for n in range(2):
                    acc[n, pl.ds(row, BLOCK)] += parts[n][m * BLOCK : (m + 1) * BLOCK]
    stores = [
        pltpu.make_async_copy(
            acc.at[:, pl.ds(half, acc.shape[1] - half), :], other_ref, out_sem.at[0]
        )
    ]
    for copy in stores:
        copy.start()
    for copy in stores:
        copy.wait()


def key_grads(rows, sides, keeps):
    rounds = len(sides)
    _, tokens, width = sides[0].shape
    run_blocks = tokens // BLOCK
    listed = rows.shape[0] // (rounds * run_blocks)
    entries = keeps[0].shape[2]
    half, count = rounds * tokens, entries - listed * BLOCK
    return pl.pallas_call(
        functools.partial(key_grads_kernel, rounds, run_blocks, listed),
        out_shape=[
            jax.ShapeDtypeStruct((2, 2 * half + count, width), F32),
            jax.ShapeDtypeStruct((2, half + count, width), F32),
        ],
        in_specs=[SMEM] + [HBM] * rounds + [VMEM] * rounds,
        out_specs=[VMEM, HBM],
        scratch_shapes=[
            pltpu.VMEM((rounds, 2, tokens, width), BF16),
            pltpu.SemaphoreType.DMA((rounds,)),
            pltpu.SemaphoreType.DMA((1,)),
        ],
        cost_estimate=pl.CostEstimate(
            flops=4 * rounds * tokens * entries * width,
            transcendentals=0,
            bytes_accessed=4 * rounds * tokens * (entries + 4 * width),
        ),
        name="key_grads",
    )(rows, *sides, *keeps)


def total_kernel(rounds, rows_ref, acc_ref, came_ref, *rest):
    outs, (came_buf, out_buf, in_sem, out_sem) = rest[:rounds], rest[rounds:]
    load = pltpu.make_async_copy(came_ref, came_buf, in_sem.at[0])
    load.start()
    tokens, width = outs[0].shape[1:]
    half = rounds * tokens
    count = rows_ref.shape[1]
    scale = width**-0.5
    rows = rows_ref[...]
    load.wait()
    halves = []
    for n in range(2):
        shared = acc_ref[n, 2 * half :] + came_buf[n, half:]
        high = shared.astype(BF16)
        halves += [high, (shared - high.astype(F32)).astype(BF16)]
    halves = jnp.concatenate(halves, axis=1)
    stores = []
    for i in range(rounds):
        ids = lax.broadcasted_iota(jnp.int32, (tokens, count), 0) + i * tokens
        hot = jnp.where(ids == rows, 1.0, 0.0).astype(BF16)
        spread = dot(hot, halves, ((1,), (0,)))
        mine = slice(i * tokens, (i + 1) * tokens)
        for n in range(2):
            whole = acc_ref[n, mine] + came_buf[n, mine]
            whole = whole + spread[:, 2 * n * width : (2 * n + 1) * width]
            whole = whole + spread[:, (2 * n + 1) * width : (2 * n + 2) * width]
            if n == 0:
                whole = whole * scale
            out_buf[i, n] = whole.astype(BF16)
        copy = pltpu.make_async_copy(out_buf.at[i], outs[i], out_sem.at[i])
        copy.start()
        stores.append(copy)
    for copy in stores:
        copy.wait()


def total(global_rows, acc, came, rounds):
    rows, width = came.shape[1:]
    count = global_rows.shape[0]
    tokens = (rows - count) // rounds
    return pl.pallas_call(
        functools.partial(total_kernel, rounds),
        out_shape=[jax.ShapeDtypeStruct((2, tokens, width), BF16)] * rounds,
        in_specs=[VMEM, VMEM, HBM],
        out_specs=[HBM] * rounds,
        scratch_shapes=[
            pltpu.VMEM(came.shape, F32),
            pltpu.VMEM((rounds, 2, tokens, width), BF16),
            pltpu.SemaphoreType.DMA((1,)),
            pltpu.SemaphoreType.DMA((rounds,)),
        ],
        cost_estimate=pl.CostEstimate(
            flops=4 * rows * width, transcendentals=0, bytes_accessed=20 * rows * width
        ),
        name="total",
    )(global_rows.reshape(1, count), acc, came)


def by_heads(query_rows, key_rows, value_rows, grad_out, rand_blocks, global_pos):
    seq_count, head_count = lax.axis_size("seq"), lax.axis_size("head")
    _, rounds, _, _ = rand_blocks.shape
    tokens = query_rows.shape[1]
    run_blocks = tokens // BLOCK
    k, head_index = lax.axis_index("seq"), lax.axis_index("head")
    h = head_index % 2
    where = k.astype(jnp.int32).reshape(1)
    sibling = [(i, i ^ 1) for i in range(head_count)]
    there = [round_pairs(seq_count, head_count, i) for i in range(rounds)]
    back = [[(j, i) for i, j in pairs] for pairs in there]

    def send(parts, pairs):
        out = []
        for n, part in enumerate(parts):
            out.append(lax.ppermute(part, AXES, pairs[n]))
        return out

    def swap(parts):
        out = []
        for part in parts:
            out.append(lax.ppermute(part, "head", sibling))
        return out

    kv = send(pack(where, key_rows, value_rows, rounds), there)
    sides = send(pack(where, query_rows, grad_out, rounds), there)
    (other_table,) = swap([rand_blocks])
    kv_other = swap(kv)
    tables = jnp.where(k // rounds == h, rand_blocks, other_table)
    table = lax.dynamic_index_in_dim(tables[0], k % rounds, 0, keepdims=False)
    rows, edge = first_rows(table, k, h, rounds, run_blocks)
    global_rows = slot_of(global_pos // tokens, k, h, rounds) * tokens + global_pos % tokens
    global_rows = global_rows.astype(jnp.int32)

    all_kv, picked = gather(global_rows, kv, kv_other)
    mixes, keeps = [], []
    for n in range(GROUPS):
        turns = tuple(range(n * rounds // GROUPS, (n + 1) * rounds // GROUPS))
        mix, keep = attend(rows, edge, all_kv, picked, [sides[t] for t in turns], turns)
        mixes += mix
        keeps += keep
    mixes = send(mixes, back)
    acc, other = key_grads(rows, sides, keeps)
    (came,) = swap([other])
    grads = total(global_rows, acc, came, rounds)
    grads = send(grads, back)
    attended, grad_query = unpack(where, mixes)
    grad_key, grad_value = unpack(where, grads)
    return attended, grad_query, grad_key, grad_value


def extended_2(value, sides, width):
    for axis, dim in sides:
        size, length = (lax.axis_size(axis), value.shape[dim])
        up = [(i, (i + 1) % size) for i in range(size - 1)]
        down = [(j, i) for i, j in up]
        last = lax.slice_in_dim(value, length - width, length, axis=dim)
        first = lax.slice_in_dim(value, 0, width, axis=dim)
        before = lax.ppermute(last, axis, up)
        after = lax.ppermute(first, axis, down)
        value = jnp.concatenate([before, value, after], axis=dim)
    return value


def by_blocks(query_rows, key_rows, value_rows, grad_out, rand_blocks, global_pos):
    batch_count, tok_local, columns = query_rows.shape
    seq_count = lax.axis_size("seq")
    seq_index = lax.axis_index("seq")
    heads_local = rand_blocks.shape[1]
    total_blocks = rand_blocks.shape[2]
    pick_count = rand_blocks.shape[3]
    head_dim = columns // heads_local
    blocks_local = tok_local // BLOCK
    score_scale = head_dim ** (-0.5)
    slot_count = batch_count * heads_local * blocks_local * pick_count
    capacity = (slot_count + seq_count - 1) // seq_count
    buffer_rows = seq_count * capacity
    f32 = jnp.float32
    bf16 = jnp.bfloat16

    def to_blocks(array):
        return array.reshape(batch_count, blocks_local, BLOCK, heads_local, head_dim).transpose(
            0, 3, 1, 2, 4
        )

    def from_blocks(array):
        return array.transpose(0, 2, 3, 1, 4).reshape(batch_count, tok_local, columns)

    def pair_blocks(array):
        return array.reshape(2, batch_count, blocks_local, BLOCK, heads_local, head_dim).transpose(
            0, 1, 4, 2, 3, 5
        )

    def global_sum(array):
        return lax.psum(array, "seq")

    key_value = jnp.stack([key_rows, value_rows])
    edge_rows = jnp.concatenate([key_value[:, :, :BLOCK], key_value[:, :, -BLOCK:]], axis=2)
    extended = extended_2(edge_rows, (("seq", 2),), BLOCK)
    padded = jnp.concatenate([extended[:, :, :BLOCK], key_value, extended[:, :, -BLOCK:]], axis=2)

    def shifted(start):
        return pair_blocks(padded[:, :, start : start + tok_local])

    window_lists = jnp.concatenate([shifted(0), shifted(BLOCK), shifted(2 * BLOCK)], axis=4)
    my_table = lax.dynamic_slice_in_dim(
        rand_blocks, seq_index * blocks_local, blocks_local, 2
    ).reshape(slot_count)
    holder = my_table // blocks_local
    holder_hot = (holder[:, None] == jnp.arange(seq_count)[None, :]).astype(jnp.int32)
    holder_rank = jnp.sum((jnp.cumsum(holder_hot, axis=0) - 1) * holder_hot, axis=1)
    position = holder * capacity + holder_rank
    requests = rand_blocks.reshape(batch_count, heads_local, seq_count, blocks_local, pick_count)
    requests = requests.transpose(2, 0, 1, 3, 4).reshape(seq_count, slot_count)
    wanted = (requests // blocks_local == seq_index).astype(jnp.int32)
    wanted_rank = jnp.cumsum(wanted, axis=1) - 1
    chosen = wanted[:, None, :] * (
        wanted_rank[:, None, :] == jnp.arange(capacity)[None, :, None]
    ).astype(jnp.int32)
    slot_live = (jnp.sum(chosen, axis=2) > 0).reshape(buffer_rows)
    slot_index = jnp.sum(chosen * jnp.arange(slot_count)[None, None, :], axis=2)
    which_batch = slot_index // (heads_local * blocks_local * pick_count)
    which_head = slot_index // (blocks_local * pick_count) % heads_local
    which_block = jnp.take_along_axis(requests, slot_index, axis=1) % blocks_local
    stacked = key_value.reshape(
        2, batch_count, blocks_local, BLOCK, heads_local, head_dim
    ).transpose(1, 2, 4, 0, 3, 5)
    outgoing = stacked[which_batch, which_block, which_head].reshape(
        buffer_rows, 2, BLOCK, head_dim
    )
    incoming = lax.all_to_all(outgoing, "seq", split_axis=0, concat_axis=0, tiled=True)
    fetched = incoming[position].reshape(
        batch_count, heads_local, blocks_local, pick_count, 2, BLOCK, head_dim
    )
    fetched = fetched.transpose(4, 0, 1, 2, 3, 5, 6).reshape(
        2, batch_count, heads_local, blocks_local, pick_count * BLOCK, head_dim
    )
    local_pos = global_pos - seq_index * tok_local
    pick_hot = (local_pos[:, None] == jnp.arange(tok_local)[None, :]).astype(bf16)
    owned_rows = jnp.einsum("gt,pbtc->pbgc", pick_hot, key_value, preferred_element_type=f32)
    shared = global_sum(owned_rows).astype(bf16)
    globals_count = shared.shape[2]
    global_kv = shared.reshape(2, batch_count, globals_count, heads_local, head_dim).transpose(
        0, 1, 3, 2, 4
    )
    global_kv = jnp.broadcast_to(
        global_kv[:, :, :, None],
        (2, batch_count, heads_local, blocks_local, globals_count, head_dim),
    )
    lists_all = jnp.concatenate([window_lists, fetched, global_kv], axis=4)
    key_lists = lists_all[0]
    value_lists = lists_all[1]
    key_count = key_lists.shape[3]
    block_ids = seq_index * blocks_local + jnp.arange(blocks_local)
    column_ids = jnp.arange(key_count)[None, :]
    middle_ok = jnp.where(
        (column_ids >= 2 * BLOCK) & (column_ids < 3 * BLOCK),
        (block_ids < total_blocks - 1)[:, None],
        True,
    )
    valid_mask = jnp.where(column_ids < BLOCK, (block_ids > 0)[:, None], middle_ok)
    query_blocks = to_blocks(query_rows)
    grad_blocks = to_blocks(grad_out)
    scores = (
        jnp.einsum("bhjqd,bhjkd->bhjqk", query_blocks, key_lists, preferred_element_type=f32)
        * score_scale
    )
    scores = jnp.where(valid_mask[None, None, :, None, :], scores, -1e30)
    row_max = jnp.max(scores, axis=-1, keepdims=True)
    log_total = row_max + jnp.log(jnp.sum(jnp.exp(scores - row_max), axis=-1, keepdims=True))
    weights = jnp.exp(scores - log_total)
    weights_b = weights.astype(bf16)
    mixed_rows = jnp.einsum(
        "bhjqk,bhjkd->bhjqd", weights_b, value_lists, preferred_element_type=f32
    )
    attended = from_blocks(mixed_rows.astype(bf16))
    row_delta = jnp.sum(grad_blocks.astype(f32) * mixed_rows, axis=-1, keepdims=True)
    grad_probs = jnp.einsum(
        "bhjqd,bhjkd->bhjqk", grad_blocks, value_lists, preferred_element_type=f32
    )
    dscore_b = (weights * (grad_probs - row_delta)).astype(bf16)
    grad_query = (
        jnp.einsum("bhjqk,bhjkd->bhjqd", dscore_b, key_lists, preferred_element_type=f32)
        * score_scale
    )

    def key_grads(lower, upper):
        key_part = (
            jnp.einsum(
                "bhjqk,bhjqd->bhjkd",
                dscore_b[..., lower:upper],
                query_blocks,
                preferred_element_type=f32,
            )
            * score_scale
        )
        value_part = jnp.einsum(
            "bhjqk,bhjqd->bhjkd",
            weights_b[..., lower:upper],
            grad_blocks,
            preferred_element_type=f32,
        )
        return jnp.stack([key_part, value_part])

    window_cols = 3 * BLOCK
    random_cols = pick_count * BLOCK
    window_grads = key_grads(0, window_cols).reshape(
        2, batch_count, heads_local, blocks_local, 3, BLOCK, head_dim
    )
    padded_grads = jnp.pad(
        window_grads[:, :, :, :, 0], ((0, 0), (0, 0), (0, 0), (0, 2), (0, 0), (0, 0))
    )
    padded_grads = padded_grads + jnp.pad(
        window_grads[:, :, :, :, 1], ((0, 0), (0, 0), (0, 0), (1, 1), (0, 0), (0, 0))
    )
    padded_grads = padded_grads + jnp.pad(
        window_grads[:, :, :, :, 2], ((0, 0), (0, 0), (0, 0), (2, 0), (0, 0), (0, 0))
    )
    own_grads = padded_grads[:, :, :, 1:-1]
    rim_grads = jnp.stack([padded_grads[:, :, :, 0], padded_grads[:, :, :, -1]], axis=3)
    returned = extended_2(rim_grads.astype(jnp.bfloat16), (("seq", 3),), 1).astype(rim_grads.dtype)
    own_grads = own_grads.at[:, :, :, 0].add(returned[:, :, :, 0])
    own_grads = own_grads.at[:, :, :, -1].add(returned[:, :, :, 3])
    global_grads = jnp.sum(key_grads(window_cols + random_cols, key_count), axis=3)
    global_grads = global_grads.transpose(0, 1, 3, 2, 4).reshape(
        2, batch_count, globals_count, columns
    )
    global_summed = global_sum(global_grads)
    inside = (local_pos >= 0) & (local_pos < tok_local)
    safe_pos = jnp.where(inside, local_pos, tok_local)
    global_local = (
        jnp.zeros((2, batch_count, tok_local, columns), f32)
        .at[:, :, safe_pos]
        .add(global_summed, mode="drop")
    )
    global_part = pair_blocks(global_local)
    target = ((which_batch * blocks_local + which_block) * heads_local + which_head).reshape(
        buffer_rows
    )
    random_grads = key_grads(window_cols, window_cols + random_cols)
    per_slot = random_grads.reshape(
        2, batch_count, heads_local, blocks_local, pick_count, BLOCK, head_dim
    )
    per_slot = per_slot.transpose(1, 2, 3, 4, 0, 5, 6).reshape(slot_count, 2, BLOCK, head_dim)
    sending = jnp.zeros((buffer_rows, 2, BLOCK, head_dim), f32).at[position].set(per_slot)
    arrived = lax.all_to_all(
        sending.astype(jnp.bfloat16), "seq", split_axis=0, concat_axis=0, tiled=True
    ).astype(sending.dtype)
    kept = jnp.where(slot_live[:, None, None, None], arrived, 0.0)
    summed = (
        jnp.zeros((batch_count * blocks_local * heads_local, 2, BLOCK, head_dim), f32)
        .at[target]
        .add(kept)
    )
    random_part = summed.reshape(
        batch_count, blocks_local, heads_local, 2, BLOCK, head_dim
    ).transpose(3, 0, 2, 1, 4, 5)
    total_grads = own_grads + random_part + global_part
    grad_key = from_blocks(total_grads[0].astype(bf16))
    grad_value = from_blocks(total_grads[1].astype(bf16))
    return (attended, from_blocks(grad_query.astype(bf16)), grad_key, grad_value)


def body(query_rows, key_rows, value_rows, grad_out, rand_blocks, global_pos):
    seq_count, head_count = lax.axis_size("seq"), lax.axis_size("head")
    batch_count, heads_local = rand_blocks.shape[:2]
    whole_heads = seq_count == 2 * heads_local and head_count % 2 == 0 and batch_count == 1
    form = by_heads if whole_heads else by_blocks
    return form(query_rows, key_rows, value_rows, grad_out, rand_blocks, global_pos)


def solution(mesh):
    return jax.shard_map(
        body,
        mesh=mesh,
        in_specs=(
            P(None, "seq", "head"),
            P(None, "seq", "head"),
            P(None, "seq", "head"),
            P(None, "seq", "head"),
            P(None, "head", None, None),
            P(),
        ),
        out_specs=(
            P(None, "seq", "head"),
            P(None, "seq", "head"),
            P(None, "seq", "head"),
            P(None, "seq", "head"),
        ),
        check_vma=False,
    )
```

```python
import functools

import jax
import jax.numpy as jnp
from jax import lax
from jax.experimental import pallas as pl
from jax.experimental.pallas import tpu as pltpu
from jax.sharding import PartitionSpec as P


BLOCK = 64
AXES = ("seq", "head")
GROUPS = 2
CHUNK = 2
GRANT = 24 * 1024 * 1024
VMEM = pl.BlockSpec(memory_space=pltpu.VMEM)
SMEM = pl.BlockSpec(memory_space=pltpu.SMEM)
PARAMS = pltpu.CompilerParams(vmem_limit_bytes=GRANT)
HBM = pl.BlockSpec(memory_space=pltpu.HBM)
F32 = jnp.float32
BF16 = jnp.bfloat16


def dot(a, b, dims):
    return lax.dot_general(a, b, (dims, ((), ())), preferred_element_type=F32)


def round_pairs(seq_count, head_count, i):
    rounds = seq_count // 2
    pairs = []
    for s in range(seq_count):
        for head in range(head_count):
            y, c = head // 2, head % 2
            k = rounds * c + (s % rounds ^ i)
            pairs.append((s * head_count + head, k * head_count + 2 * y + s // rounds))
    return pairs


def pack_kernel(rounds, width, pos_ref, a_ref, b_ref, *rest):
    outs, (buf, in_sem, out_sem) = rest[:rounds], rest[rounds:]
    s = pos_ref[0]
    loads = []
    for i in range(rounds):
        col = pl.multiple_of((lax.rem(s, rounds) ^ i) * width, width)
        for n, ref in enumerate((a_ref, b_ref)):
            copy = pltpu.make_async_copy(
                ref.at[0, :, pl.ds(col, width)], buf.at[i, n], in_sem.at[i, n]
            )
            copy.start()
            loads.append(copy)
    stores = []
    for i in range(rounds):
        loads[2 * i].wait()
        loads[2 * i + 1].wait()
        copy = pltpu.make_async_copy(buf.at[i], outs[i], out_sem.at[i])
        copy.start()
        stores.append(copy)
    for copy in stores:
        copy.wait()


def pack(where, a, b, rounds):
    _, tokens, columns = a.shape
    width = columns // rounds
    out = jax.ShapeDtypeStruct((2, tokens, width), a.dtype)
    return pl.pallas_call(
        functools.partial(pack_kernel, rounds, width),
        out_shape=[out] * rounds,
        in_specs=[SMEM, HBM, HBM],
        out_specs=[HBM] * rounds,
        scratch_shapes=[
            pltpu.VMEM((rounds, 2, tokens, width), a.dtype),
            pltpu.SemaphoreType.DMA((rounds, 2)),
            pltpu.SemaphoreType.DMA((rounds,)),
        ],
        compiler_params=PARAMS,
        cost_estimate=pl.CostEstimate(
            flops=0, transcendentals=0, bytes_accessed=8 * tokens * columns
        ),
        name="pack",
    )(where, a, b)


def unpack_kernel(rounds, width, pos_ref, *rest):
    ins, outs, (buf, in_sem, out_sem) = rest[:rounds], rest[rounds : rounds + 2], rest[rounds + 2 :]
    s = pos_ref[0]
    loads = []
    for i in range(rounds):
        copy = pltpu.make_async_copy(ins[i], buf.at[i], in_sem.at[i])
        copy.start()
        loads.append(copy)
    stores = []
    for i in range(rounds):
        loads[i].wait()
        col = pl.multiple_of((lax.rem(s, rounds) ^ i) * width, width)
        for n in range(2):
            copy = pltpu.make_async_copy(
                buf.at[i, n], outs[n].at[0, :, pl.ds(col, width)], out_sem.at[i, n]
            )
            copy.start()
            stores.append(copy)
    for copy in stores:
        copy.wait()


def unpack(where, parts):
    rounds = len(parts)
    _, tokens, width = parts[0].shape
    out = jax.ShapeDtypeStruct((1, tokens, rounds * width), parts[0].dtype)
    return pl.pallas_call(
        functools.partial(unpack_kernel, rounds, width),
        out_shape=[out] * 2,
        in_specs=[SMEM] + [HBM] * rounds,
        out_specs=[HBM] * 2,
        scratch_shapes=[
            pltpu.VMEM((rounds, 2, tokens, width), parts[0].dtype),
            pltpu.SemaphoreType.DMA((rounds,)),
            pltpu.SemaphoreType.DMA((rounds, 2)),
        ],
        compiler_params=PARAMS,
        cost_estimate=pl.CostEstimate(
            flops=0, transcendentals=0, bytes_accessed=8 * rounds * tokens * width
        ),
        name="unpack",
    )(where, *parts)


def slot_of(run, k, h, rounds):
    turn = (k ^ run) % rounds
    return jnp.where(run // rounds == h, 0, rounds) + turn


def first_rows(table, k, h, rounds, run_blocks):
    total, _ = table.shape
    runs = h * rounds + (k % rounds ^ jnp.arange(rounds))
    blocks = (runs[:, None] * run_blocks + jnp.arange(run_blocks)[None, :]).reshape(-1)
    window = jnp.clip(blocks[:, None] + jnp.arange(-1, 2)[None, :], 0, total - 1)
    named = jnp.concatenate([window, table[blocks]], axis=1)
    place = slot_of(named // run_blocks, k, h, rounds) * run_blocks + named % run_blocks
    edge = (blocks == 0) + 2 * (blocks == total - 1)
    return (place * BLOCK).astype(jnp.int32).reshape(-1), edge.astype(jnp.int32)


def gather_kernel(rounds, rows_ref, *rest):
    parts, (all_ref, picked_ref, sem) = rest[: 2 * rounds], rest[2 * rounds :]
    tokens = all_ref.shape[1] // (2 * rounds)
    copies = []
    for n in range(2 * rounds):
        copy = pltpu.make_async_copy(
            parts[n], all_ref.at[:, pl.ds(n * tokens, tokens), :], sem.at[n]
        )
        copy.start()
        copies.append(copy)
    rows = rows_ref[...]
    count = rows.shape[0]
    sums = [None, None]
    for n in range(2 * rounds):
        ids = lax.broadcasted_iota(jnp.int32, (count, tokens), 1) + n * tokens
        hot = jnp.where(ids == rows, 1.0, 0.0).astype(BF16)
        copies[n].wait()
        for m in range(2):
            part = dot(hot, all_ref[m, n * tokens : (n + 1) * tokens], ((1,), (0,)))
            sums[m] = part if n == 0 else sums[m] + part
    for m in range(2):
        picked_ref[m] = sums[m].astype(BF16)


def gather(global_rows, own, other):
    rounds = len(own)
    _, tokens, width = own[0].shape
    count = global_rows.shape[0]
    return pl.pallas_call(
        functools.partial(gather_kernel, rounds),
        out_shape=[
            jax.ShapeDtypeStruct((2, 2 * rounds * tokens, width), BF16),
            jax.ShapeDtypeStruct((2, count, width), BF16),
        ],
        in_specs=[VMEM] + [HBM] * (2 * rounds),
        out_specs=[VMEM, VMEM],
        scratch_shapes=[pltpu.SemaphoreType.DMA((2 * rounds,))],
        compiler_params=PARAMS,
        cost_estimate=pl.CostEstimate(
            flops=8 * count * rounds * tokens * width,
            transcendentals=0,
            bytes_accessed=16 * rounds * tokens * width,
        ),
        name="gather",
    )(global_rows.reshape(count, 1), *own, *other)


def attend_kernel(run_blocks, listed, turns, rows_ref, edge_ref, all_ref, picked_ref, *rest):
    count = len(turns)
    sides, mixes, keeps = rest[:count], rest[count : 2 * count], rest[2 * count : 3 * count]
    side_buf, mix_buf, in_sem, out_sem = rest[3 * count :]
    loads, stores = [], []
    for n in range(count):
        copy = pltpu.make_async_copy(sides[n], side_buf.at[n], in_sem.at[n])
        copy.start()
        loads.append(copy)
    scale = all_ref.shape[2] ** -0.5
    column = lax.broadcasted_iota(jnp.int32, (1, 4 * BLOCK), 1)

    def begin(n, block):
        mine = slice(block * BLOCK, (block + 1) * BLOCK)
        query, grad = side_buf[n, 0, mine], side_buf[n, 1, mine]
        index = turns[n] * run_blocks + block
        rows = [
            pl.multiple_of(rows_ref[index * listed + m], BLOCK) for m in range(listed)
        ]
        keys, values = [
            jnp.concatenate(
                [all_ref[m, pl.ds(r, BLOCK)] for r in rows] + [picked_ref[m]], axis=0
            )
            for m in range(2)
        ]
        scores = dot(query, keys, ((1,), (1,))) * scale
        probs = dot(grad, values, ((1,), (1,)))
        edge = edge_ref[index]
        out = ((column < BLOCK) & (edge % 2 == 1)) | (
            (column >= 2 * BLOCK) & (column < 3 * BLOCK) & (edge >= 2)
        )
        near = jnp.where(out, -1e30, scores[:, : 4 * BLOCK])
        scores = jnp.concatenate([near, scores[:, 4 * BLOCK :]], axis=1)
        return n, mine, keys, values, scores, probs

    def finish(state):
        weighed = []
        for n, mine, keys, values, scores, probs in state:
            peak = jnp.max(scores, axis=1, keepdims=True)
            powers = jnp.exp(scores - peak)
            weights = powers * (1.0 / jnp.sum(powers, axis=1, keepdims=True))
            weights_b = weights.astype(BF16)
            keeps[n][1, mine] = weights_b
            weighed.append((weights, weights_b))
        scored = []
        for (n, mine, keys, values, scores, probs), (weights, weights_b) in zip(state, weighed):
            delta = jnp.sum(weights_b.astype(F32) * probs, axis=1, keepdims=True)
            dscore_b = (weights * (probs - delta)).astype(BF16)
            keeps[n][0, mine] = dscore_b
            scored.append(dscore_b)
        for (n, mine, keys, values, _, _), (_, weights_b), dscore_b in zip(
            state, weighed, scored
        ):
            mixed = dot(weights_b, values, ((1,), (0,)))
            grad_query = dot(dscore_b, keys, ((1,), (0,))) * scale
            mix_buf[n, 0, mine] = mixed.astype(BF16)
            mix_buf[n, 1, mine] = grad_query.astype(BF16)

    held = None
    for n in range(count):
        loads[n].wait()
        for block in range(0, run_blocks, CHUNK):
            state = [begin(n, b) for b in range(block, block + CHUNK)]
            if held is not None:
                finish(held)
                if block == 0:
                    copy = pltpu.make_async_copy(mix_buf.at[n - 1], mixes[n - 1], out_sem.at[n - 1])
                    copy.start()
                    stores.append(copy)
            held = state
    finish(held)
    copy = pltpu.make_async_copy(mix_buf.at[count - 1], mixes[count - 1], out_sem.at[count - 1])
    copy.start()
    stores.append(copy)
    for copy in stores:
        copy.wait()


def attend(rows, edge, all_kv, picked, sides, turns):
    _, tokens, width = sides[0].shape
    run_blocks = tokens // BLOCK
    listed = rows.shape[0] // edge.shape[0]
    entries = listed * BLOCK + picked.shape[1]
    count = len(turns)
    outs = pl.pallas_call(
        functools.partial(attend_kernel, run_blocks, listed, turns),
        out_shape=[jax.ShapeDtypeStruct((2, tokens, width), BF16)] * count
        + [jax.ShapeDtypeStruct((2, tokens, entries), BF16)] * count,
        in_specs=[SMEM, SMEM, VMEM, VMEM] + [HBM] * count,
        out_specs=[HBM] * count + [VMEM] * count,
        scratch_shapes=[
            pltpu.VMEM((count, 2, tokens, width), BF16),
            pltpu.VMEM((count, 2, tokens, width), BF16),
            pltpu.SemaphoreType.DMA((count,)),
            pltpu.SemaphoreType.DMA((count,)),
        ],
        compiler_params=PARAMS,
        cost_estimate=pl.CostEstimate(
            flops=8 * count * tokens * entries * width,
            transcendentals=count * tokens * entries,
            bytes_accessed=4 * all_kv.size,
        ),
        name="attend",
    )(rows, edge, all_kv, picked, *sides)
    return outs[:count], outs[count:]


def key_grads_kernel(rounds, run_blocks, listed, rows_ref, *rest):
    sides, keeps = rest[:rounds], rest[rounds : 2 * rounds]
    acc, other_ref, side_buf, in_sem, out_sem = rest[2 * rounds :]
    loads = []
    for turn in range(rounds):
        copy = pltpu.make_async_copy(sides[turn], side_buf.at[turn], in_sem.at[turn])
        copy.start()
        loads.append(copy)
    entries = listed * BLOCK
    half = rounds * run_blocks * BLOCK
    acc[:, : 2 * half] = jnp.zeros((2, 2 * half, acc.shape[2]), F32)
    for copy in loads:
        copy.wait()
    for n in range(2):
        shared = None
        for turn in range(rounds):
            part = dot(keeps[turn][n, :, entries:], side_buf[turn, n], ((0,), (0,)))
            shared = part if shared is None else shared + part
        acc[n, 2 * half :] = shared
    for turn in range(rounds):
        for block in range(run_blocks):
            index = turn * run_blocks + block
            mine = slice(block * BLOCK, (block + 1) * BLOCK)
            parts = [
                dot(keeps[turn][n, mine, :entries], side_buf[turn, n, mine], ((0,), (0,)))
                for n in range(2)
            ]
            for m in range(listed):
                row = pl.multiple_of(rows_ref[index * listed + m], BLOCK)
                for n in range(2):
                    acc[n, pl.ds(row, BLOCK)] += parts[n][m * BLOCK : (m + 1) * BLOCK]
    stores = [
        pltpu.make_async_copy(
            acc.at[:, pl.ds(half, acc.shape[1] - half), :], other_ref, out_sem.at[0]
        )
    ]
    for copy in stores:
        copy.start()
    for copy in stores:
        copy.wait()


def key_grads(rows, sides, keeps):
    rounds = len(sides)
    _, tokens, width = sides[0].shape
    run_blocks = tokens // BLOCK
    listed = rows.shape[0] // (rounds * run_blocks)
    entries = keeps[0].shape[2]
    half, count = rounds * tokens, entries - listed * BLOCK
    return pl.pallas_call(
        functools.partial(key_grads_kernel, rounds, run_blocks, listed),
        out_shape=[
            jax.ShapeDtypeStruct((2, 2 * half + count, width), F32),
            jax.ShapeDtypeStruct((2, half + count, width), F32),
        ],
        in_specs=[SMEM] + [HBM] * rounds + [VMEM] * rounds,
        out_specs=[VMEM, HBM],
        scratch_shapes=[
            pltpu.VMEM((rounds, 2, tokens, width), BF16),
            pltpu.SemaphoreType.DMA((rounds,)),
            pltpu.SemaphoreType.DMA((1,)),
        ],
        compiler_params=PARAMS,
        cost_estimate=pl.CostEstimate(
            flops=4 * rounds * tokens * entries * width,
            transcendentals=0,
            bytes_accessed=4 * rounds * tokens * (entries + 4 * width),
        ),
        name="key_grads",
    )(rows, *sides, *keeps)


def total_kernel(rounds, rows_ref, acc_ref, came_ref, *rest):
    outs, (came_buf, out_buf, in_sem, out_sem) = rest[:rounds], rest[rounds:]
    load = pltpu.make_async_copy(came_ref, came_buf, in_sem.at[0])
    load.start()
    tokens, width = outs[0].shape[1:]
    half = rounds * tokens
    count = rows_ref.shape[1]
    scale = width**-0.5
    rows = rows_ref[...]
    load.wait()
    halves = []
    for n in range(2):
        shared = acc_ref[n, 2 * half :] + came_buf[n, half:]
        high = shared.astype(BF16)
        halves += [high, (shared - high.astype(F32)).astype(BF16)]
    halves = jnp.concatenate(halves, axis=1)
    stores = []
    for i in range(rounds):
        ids = lax.broadcasted_iota(jnp.int32, (tokens, count), 0) + i * tokens
        hot = jnp.where(ids == rows, 1.0, 0.0).astype(BF16)
        spread = dot(hot, halves, ((1,), (0,)))
        mine = slice(i * tokens, (i + 1) * tokens)
        for n in range(2):
            whole = acc_ref[n, mine] + came_buf[n, mine]
            whole = whole + spread[:, 2 * n * width : (2 * n + 1) * width]
            whole = whole + spread[:, (2 * n + 1) * width : (2 * n + 2) * width]
            if n == 0:
                whole = whole * scale
            out_buf[i, n] = whole.astype(BF16)
        copy = pltpu.make_async_copy(out_buf.at[i], outs[i], out_sem.at[i])
        copy.start()
        stores.append(copy)
    for copy in stores:
        copy.wait()


def total(global_rows, acc, came, rounds):
    rows, width = came.shape[1:]
    count = global_rows.shape[0]
    tokens = (rows - count) // rounds
    return pl.pallas_call(
        functools.partial(total_kernel, rounds),
        out_shape=[jax.ShapeDtypeStruct((2, tokens, width), BF16)] * rounds,
        in_specs=[VMEM, VMEM, HBM],
        out_specs=[HBM] * rounds,
        scratch_shapes=[
            pltpu.VMEM(came.shape, F32),
            pltpu.VMEM((rounds, 2, tokens, width), BF16),
            pltpu.SemaphoreType.DMA((1,)),
            pltpu.SemaphoreType.DMA((rounds,)),
        ],
        compiler_params=PARAMS,
        cost_estimate=pl.CostEstimate(
            flops=4 * rows * width, transcendentals=0, bytes_accessed=20 * rows * width
        ),
        name="total",
    )(global_rows.reshape(1, count), acc, came)


def by_heads(query_rows, key_rows, value_rows, grad_out, rand_blocks, global_pos):
    seq_count, head_count = lax.axis_size("seq"), lax.axis_size("head")
    _, rounds, _, _ = rand_blocks.shape
    tokens = query_rows.shape[1]
    run_blocks = tokens // BLOCK
    k, head_index = lax.axis_index("seq"), lax.axis_index("head")
    h = head_index % 2
    where = k.astype(jnp.int32).reshape(1)
    sibling = [(i, i ^ 1) for i in range(head_count)]
    there = [round_pairs(seq_count, head_count, i) for i in range(rounds)]

    def send(parts, pairs):
        out = []
        for n, part in enumerate(parts):
            out.append(lax.ppermute(part, AXES, pairs[n]))
        return out

    def swap(parts):
        out = []
        for part in parts:
            out.append(lax.ppermute(part, "head", sibling))
        return out

    kv = send(pack(where, key_rows, value_rows, rounds), there)
    sides = send(pack(where, query_rows, grad_out, rounds), there)
    (other_table,) = swap([rand_blocks])
    kv_other = swap(kv)
    tables = jnp.where(k // rounds == h, rand_blocks, other_table)
    table = lax.dynamic_index_in_dim(tables[0], k % rounds, 0, keepdims=False)
    rows, edge = first_rows(table, k, h, rounds, run_blocks)
    global_rows = slot_of(global_pos // tokens, k, h, rounds) * tokens + global_pos % tokens
    global_rows = global_rows.astype(jnp.int32)

    all_kv, picked = gather(global_rows, kv, kv_other)
    mixes, keeps = [], []
    for n in range(GROUPS):
        turns = tuple(range(n * rounds // GROUPS, (n + 1) * rounds // GROUPS))
        mix, keep = attend(rows, edge, all_kv, picked, [sides[t] for t in turns], turns)
        mixes += mix
        keeps += keep
    mixes = send(mixes, there)
    acc, other = key_grads(rows, sides, keeps)
    (came,) = swap([other])
    grads = total(global_rows, acc, came, rounds)
    grads = send(grads, there)
    attended, grad_query = unpack(where, mixes)
    grad_key, grad_value = unpack(where, grads)
    return attended, grad_query, grad_key, grad_value


def extended_2(value, sides, width):
    for axis, dim in sides:
        size, length = (lax.axis_size(axis), value.shape[dim])
        up = [(i, (i + 1) % size) for i in range(size - 1)]
        down = [(j, i) for i, j in up]
        last = lax.slice_in_dim(value, length - width, length, axis=dim)
        first = lax.slice_in_dim(value, 0, width, axis=dim)
        before = lax.ppermute(last, axis, up)
        after = lax.ppermute(first, axis, down)
        value = jnp.concatenate([before, value, after], axis=dim)
    return value


def by_blocks(query_rows, key_rows, value_rows, grad_out, rand_blocks, global_pos):
    batch_count, tok_local, columns = query_rows.shape
    seq_count = lax.axis_size("seq")
    seq_index = lax.axis_index("seq")
    heads_local = rand_blocks.shape[1]
    total_blocks = rand_blocks.shape[2]
    pick_count = rand_blocks.shape[3]
    head_dim = columns // heads_local
    blocks_local = tok_local // BLOCK
    score_scale = head_dim ** (-0.5)
    slot_count = batch_count * heads_local * blocks_local * pick_count
    capacity = (slot_count + seq_count - 1) // seq_count
    buffer_rows = seq_count * capacity
    f32 = jnp.float32
    bf16 = jnp.bfloat16

    def to_blocks(array):
        return array.reshape(batch_count, blocks_local, BLOCK, heads_local, head_dim).transpose(
            0, 3, 1, 2, 4
        )

    def from_blocks(array):
        return array.transpose(0, 2, 3, 1, 4).reshape(batch_count, tok_local, columns)

    def pair_blocks(array):
        return array.reshape(2, batch_count, blocks_local, BLOCK, heads_local, head_dim).transpose(
            0, 1, 4, 2, 3, 5
        )

    def global_sum(array):
        return lax.psum(array, "seq")

    key_value = jnp.stack([key_rows, value_rows])
    edge_rows = jnp.concatenate([key_value[:, :, :BLOCK], key_value[:, :, -BLOCK:]], axis=2)
    extended = extended_2(edge_rows, (("seq", 2),), BLOCK)
    padded = jnp.concatenate([extended[:, :, :BLOCK], key_value, extended[:, :, -BLOCK:]], axis=2)

    def shifted(start):
        return pair_blocks(padded[:, :, start : start + tok_local])

    window_lists = jnp.concatenate([shifted(0), shifted(BLOCK), shifted(2 * BLOCK)], axis=4)
    my_table = lax.dynamic_slice_in_dim(
        rand_blocks, seq_index * blocks_local, blocks_local, 2
    ).reshape(slot_count)
    holder = my_table // blocks_local
    holder_hot = (holder[:, None] == jnp.arange(seq_count)[None, :]).astype(jnp.int32)
    holder_rank = jnp.sum((jnp.cumsum(holder_hot, axis=0) - 1) * holder_hot, axis=1)
    position = holder * capacity + holder_rank
    requests = rand_blocks.reshape(batch_count, heads_local, seq_count, blocks_local, pick_count)
    requests = requests.transpose(2, 0, 1, 3, 4).reshape(seq_count, slot_count)
    wanted = (requests // blocks_local == seq_index).astype(jnp.int32)
    wanted_rank = jnp.cumsum(wanted, axis=1) - 1
    chosen = wanted[:, None, :] * (
        wanted_rank[:, None, :] == jnp.arange(capacity)[None, :, None]
    ).astype(jnp.int32)
    slot_live = (jnp.sum(chosen, axis=2) > 0).reshape(buffer_rows)
    slot_index = jnp.sum(chosen * jnp.arange(slot_count)[None, None, :], axis=2)
    which_batch = slot_index // (heads_local * blocks_local * pick_count)
    which_head = slot_index // (blocks_local * pick_count) % heads_local
    which_block = jnp.take_along_axis(requests, slot_index, axis=1) % blocks_local
    stacked = key_value.reshape(
        2, batch_count, blocks_local, BLOCK, heads_local, head_dim
    ).transpose(1, 2, 4, 0, 3, 5)
    outgoing = stacked[which_batch, which_block, which_head].reshape(
        buffer_rows, 2, BLOCK, head_dim
    )
    incoming = lax.all_to_all(outgoing, "seq", split_axis=0, concat_axis=0, tiled=True)
    fetched = incoming[position].reshape(
        batch_count, heads_local, blocks_local, pick_count, 2, BLOCK, head_dim
    )
    fetched = fetched.transpose(4, 0, 1, 2, 3, 5, 6).reshape(
        2, batch_count, heads_local, blocks_local, pick_count * BLOCK, head_dim
    )
    local_pos = global_pos - seq_index * tok_local
    pick_hot = (local_pos[:, None] == jnp.arange(tok_local)[None, :]).astype(bf16)
    owned_rows = jnp.einsum("gt,pbtc->pbgc", pick_hot, key_value, preferred_element_type=f32)
    shared = global_sum(owned_rows).astype(bf16)
    globals_count = shared.shape[2]
    global_kv = shared.reshape(2, batch_count, globals_count, heads_local, head_dim).transpose(
        0, 1, 3, 2, 4
    )
    global_kv = jnp.broadcast_to(
        global_kv[:, :, :, None],
        (2, batch_count, heads_local, blocks_local, globals_count, head_dim),
    )
    lists_all = jnp.concatenate([window_lists, fetched, global_kv], axis=4)
    key_lists = lists_all[0]
    value_lists = lists_all[1]
    key_count = key_lists.shape[3]
    block_ids = seq_index * blocks_local + jnp.arange(blocks_local)
    column_ids = jnp.arange(key_count)[None, :]
    middle_ok = jnp.where(
        (column_ids >= 2 * BLOCK) & (column_ids < 3 * BLOCK),
        (block_ids < total_blocks - 1)[:, None],
        True,
    )
    valid_mask = jnp.where(column_ids < BLOCK, (block_ids > 0)[:, None], middle_ok)
    query_blocks = to_blocks(query_rows)
    grad_blocks = to_blocks(grad_out)
    scores = (
        jnp.einsum("bhjqd,bhjkd->bhjqk", query_blocks, key_lists, preferred_element_type=f32)
        * score_scale
    )
    scores = jnp.where(valid_mask[None, None, :, None, :], scores, -1e30)
    row_max = jnp.max(scores, axis=-1, keepdims=True)
    log_total = row_max + jnp.log(jnp.sum(jnp.exp(scores - row_max), axis=-1, keepdims=True))
    weights = jnp.exp(scores - log_total)
    weights_b = weights.astype(bf16)
    mixed_rows = jnp.einsum(
        "bhjqk,bhjkd->bhjqd", weights_b, value_lists, preferred_element_type=f32
    )
    attended = from_blocks(mixed_rows.astype(bf16))
    row_delta = jnp.sum(grad_blocks.astype(f32) * mixed_rows, axis=-1, keepdims=True)
    grad_probs = jnp.einsum(
        "bhjqd,bhjkd->bhjqk", grad_blocks, value_lists, preferred_element_type=f32
    )
    dscore_b = (weights * (grad_probs - row_delta)).astype(bf16)
    grad_query = (
        jnp.einsum("bhjqk,bhjkd->bhjqd", dscore_b, key_lists, preferred_element_type=f32)
        * score_scale
    )

    def key_grads(lower, upper):
        key_part = (
            jnp.einsum(
                "bhjqk,bhjqd->bhjkd",
                dscore_b[..., lower:upper],
                query_blocks,
                preferred_element_type=f32,
            )
            * score_scale
        )
        value_part = jnp.einsum(
            "bhjqk,bhjqd->bhjkd",
            weights_b[..., lower:upper],
            grad_blocks,
            preferred_element_type=f32,
        )
        return jnp.stack([key_part, value_part])

    window_cols = 3 * BLOCK
    random_cols = pick_count * BLOCK
    window_grads = key_grads(0, window_cols).reshape(
        2, batch_count, heads_local, blocks_local, 3, BLOCK, head_dim
    )
    padded_grads = jnp.pad(
        window_grads[:, :, :, :, 0], ((0, 0), (0, 0), (0, 0), (0, 2), (0, 0), (0, 0))
    )
    padded_grads = padded_grads + jnp.pad(
        window_grads[:, :, :, :, 1], ((0, 0), (0, 0), (0, 0), (1, 1), (0, 0), (0, 0))
    )
    padded_grads = padded_grads + jnp.pad(
        window_grads[:, :, :, :, 2], ((0, 0), (0, 0), (0, 0), (2, 0), (0, 0), (0, 0))
    )
    own_grads = padded_grads[:, :, :, 1:-1]
    rim_grads = jnp.stack([padded_grads[:, :, :, 0], padded_grads[:, :, :, -1]], axis=3)
    returned = extended_2(rim_grads.astype(jnp.bfloat16), (("seq", 3),), 1).astype(rim_grads.dtype)
    own_grads = own_grads.at[:, :, :, 0].add(returned[:, :, :, 0])
    own_grads = own_grads.at[:, :, :, -1].add(returned[:, :, :, 3])
    global_grads = jnp.sum(key_grads(window_cols + random_cols, key_count), axis=3)
    global_grads = global_grads.transpose(0, 1, 3, 2, 4).reshape(
        2, batch_count, globals_count, columns
    )
    global_summed = global_sum(global_grads)
    inside = (local_pos >= 0) & (local_pos < tok_local)
    safe_pos = jnp.where(inside, local_pos, tok_local)
    global_local = (
        jnp.zeros((2, batch_count, tok_local, columns), f32)
        .at[:, :, safe_pos]
        .add(global_summed, mode="drop")
    )
    global_part = pair_blocks(global_local)
    target = ((which_batch * blocks_local + which_block) * heads_local + which_head).reshape(
        buffer_rows
    )
    random_grads = key_grads(window_cols, window_cols + random_cols)
    per_slot = random_grads.reshape(
        2, batch_count, heads_local, blocks_local, pick_count, BLOCK, head_dim
    )
    per_slot = per_slot.transpose(1, 2, 3, 4, 0, 5, 6).reshape(slot_count, 2, BLOCK, head_dim)
    sending = jnp.zeros((buffer_rows, 2, BLOCK, head_dim), f32).at[position].set(per_slot)
    arrived = lax.all_to_all(
        sending.astype(jnp.bfloat16), "seq", split_axis=0, concat_axis=0, tiled=True
    ).astype(sending.dtype)
    kept = jnp.where(slot_live[:, None, None, None], arrived, 0.0)
    summed = (
        jnp.zeros((batch_count * blocks_local * heads_local, 2, BLOCK, head_dim), f32)
        .at[target]
        .add(kept)
    )
    random_part = summed.reshape(
        batch_count, blocks_local, heads_local, 2, BLOCK, head_dim
    ).transpose(3, 0, 2, 1, 4, 5)
    total_grads = own_grads + random_part + global_part
    grad_key = from_blocks(total_grads[0].astype(bf16))
    grad_value = from_blocks(total_grads[1].astype(bf16))
    return (attended, from_blocks(grad_query.astype(bf16)), grad_key, grad_value)


def body(query_rows, key_rows, value_rows, grad_out, rand_blocks, global_pos):
    seq_count, head_count = lax.axis_size("seq"), lax.axis_size("head")
    batch_count, heads_local = rand_blocks.shape[:2]
    whole_heads = seq_count == 2 * heads_local and heads_local & (heads_local - 1) == 0
    whole_heads = whole_heads and head_count % 2 == 0 and batch_count == 1
    form = by_heads if whole_heads else by_blocks
    return form(query_rows, key_rows, value_rows, grad_out, rand_blocks, global_pos)


def solution(mesh):
    return jax.shard_map(
        body,
        mesh=mesh,
        in_specs=(
            P(None, "seq", "head"),
            P(None, "seq", "head"),
            P(None, "seq", "head"),
            P(None, "seq", "head"),
            P(None, "head", None, None),
            P(),
        ),
        out_specs=(
            P(None, "seq", "head"),
            P(None, "seq", "head"),
            P(None, "seq", "head"),
            P(None, "seq", "head"),
        ),
        check_vma=False,
    )
```

```python
import functools

import jax
import jax.numpy as jnp
from jax import lax
from jax.experimental import pallas as pl
from jax.experimental.pallas import tpu as pltpu
from jax.sharding import PartitionSpec as P


BLOCK = 64
AXES = ("seq", "head")
GROUPS = 2
CHUNK = 2
GRANT = 24 * 1024 * 1024
VMEM = pl.BlockSpec(memory_space=pltpu.VMEM)
SMEM = pl.BlockSpec(memory_space=pltpu.SMEM)
PARAMS = pltpu.CompilerParams(vmem_limit_bytes=GRANT)
PACK_PARAMS = pltpu.CompilerParams(vmem_limit_bytes=GRANT)
HBM = pl.BlockSpec(memory_space=pltpu.HBM)
F32 = jnp.float32
BF16 = jnp.bfloat16


def dot(a, b, dims):
    return lax.dot_general(a, b, (dims, ((), ())), preferred_element_type=F32)


def round_pairs(seq_count, head_count, i):
    rounds = seq_count // 2
    pairs = []
    for s in range(seq_count):
        for head in range(head_count):
            y, c = head // 2, head % 2
            k = rounds * c + (s % rounds ^ i)
            pairs.append((s * head_count + head, k * head_count + 2 * y + s // rounds))
    return pairs


def keep_in_hbm(array):
    return pltpu.with_memory_space_constraint(array, pltpu.HBM)


def pack_kernel(rounds, width, where_ref, *rest):
    ins, outs, sem = rest[:4], rest[4:-1], rest[-1]
    turn = lax.rem(where_ref[0], rounds)
    copies = []
    for m in range(2):
        for i in range(rounds):
            col = pl.multiple_of((turn ^ i) * width, width)
            for n in range(2):
                copy = pltpu.make_async_copy(
                    ins[2 * m + n].at[0, :, pl.ds(col, width)],
                    outs[m * rounds + i].at[n],
                    sem.at[m * rounds + i, n],
                )
                copy.start()
                copies.append(copy)
    for copy in copies:
        copy.wait()


def pack(where, arrays, rounds):
    _, tokens, columns = arrays[0].shape
    width = columns // rounds
    out = jax.ShapeDtypeStruct((2, tokens, width), BF16)
    outs = pl.pallas_call(
        functools.partial(pack_kernel, rounds, width),
        out_shape=[out] * (2 * rounds),
        in_specs=[SMEM] + [HBM] * 4,
        out_specs=[VMEM] * (2 * rounds),
        scratch_shapes=[pltpu.SemaphoreType.DMA((2 * rounds, 2))],
        compiler_params=PACK_PARAMS,
        cost_estimate=pl.CostEstimate(
            flops=0, transcendentals=0, bytes_accessed=16 * tokens * columns
        ),
        name="pack",
    )(where, *[keep_in_hbm(a) for a in arrays])
    return outs[:rounds], outs[rounds:]


def unpack_kernel(rounds, width, where_ref, *rest):
    ins, outs, sem = rest[:rounds], rest[rounds:-1], rest[-1]
    turn = lax.rem(where_ref[0], rounds)
    copies = []
    for i in range(rounds):
        col = pl.multiple_of((turn ^ i) * width, width)
        for n in range(2):
            copy = pltpu.make_async_copy(
                ins[i].at[n], outs[n].at[0, :, pl.ds(col, width)], sem.at[i, n]
            )
            copy.start()
            copies.append(copy)
    for copy in copies:
        copy.wait()


def unpack(where, parts):
    rounds = len(parts)
    _, tokens, width = parts[0].shape
    out = jax.ShapeDtypeStruct((1, tokens, rounds * width), BF16)
    return pl.pallas_call(
        functools.partial(unpack_kernel, rounds, width),
        out_shape=[out] * 2,
        in_specs=[SMEM] + [VMEM] * rounds,
        out_specs=[HBM] * 2,
        scratch_shapes=[pltpu.SemaphoreType.DMA((rounds, 2))],
        compiler_params=PARAMS,
        cost_estimate=pl.CostEstimate(
            flops=0, transcendentals=0, bytes_accessed=8 * rounds * tokens * width
        ),
        name="unpack",
    )(where, *parts)


def attend_kernel(
    rounds, run_blocks, picks, turns, opens, closes, where_ref, mine_ref, other_table_ref, *rest
):
    rest = list(rest)
    take = lambda n: [rest.pop(0) for _ in range(n)]
    count = len(turns)
    if opens:
        (global_ref,), parts = take(1), take(2 * rounds)
    else:
        all_ref, picked_ref, _ = take(3)
    sides = take(count)
    mixes = take(count)
    if opens:
        all_ref, picked_ref = take(2)
    (acc,) = take(1)
    if closes:
        (send_ref,) = take(1)
    (keep,) = take(1)

    k, h = where_ref[0], where_ref[1]
    tokens = run_blocks * BLOCK
    half = rounds * tokens
    total_blocks = 2 * rounds * run_blocks
    listed = (3 + picks) * BLOCK
    flip = (h * rounds + lax.rem(k, rounds)) * run_blocks
    head = lax.rem(k, rounds) * (total_blocks * picks)
    mine = k // rounds == h
    scale = all_ref.shape[2] ** -0.5
    column = lax.broadcasted_iota(jnp.int32, (1, 4 * BLOCK), 1)

    if opens:
        spots = global_ref[...] ^ (flip * BLOCK)
        sums = [None, None]
        for n in range(2 * rounds):
            ids = lax.broadcasted_iota(jnp.int32, (spots.shape[0], tokens), 1) + n * tokens
            hot = jnp.where(ids == spots, 1.0, 0.0).astype(BF16)
            for m in range(2):
                part = parts[n][m]
                all_ref[m, n * tokens : (n + 1) * tokens] = part
                product = dot(hot, part, ((1,), (0,)))
                sums[m] = product if n == 0 else sums[m] + product
        for m in range(2):
            picked_ref[m] = sums[m].astype(BF16)
        acc[...] = jnp.zeros_like(acc)

    def begin(n, block):
        rows_of = slice(block * BLOCK, (block + 1) * BLOCK)
        query, grad = sides[n][0, rows_of], sides[n][1, rows_of]
        index = (turns[n] * run_blocks + block) ^ flip
        named = [
            jnp.maximum(index - 1, 0),
            index,
            jnp.minimum(index + 1, total_blocks - 1),
        ]
        for m in range(picks):
            at = head + index * picks + m
            named.append(jnp.where(mine, mine_ref[at], other_table_ref[at]))
        rows = [pl.multiple_of((b ^ flip) * BLOCK, BLOCK) for b in named]
        keys, values = [
            jnp.concatenate(
                [all_ref[m, pl.ds(r, BLOCK)] for r in rows] + [picked_ref[m]], axis=0
            )
            for m in range(2)
        ]
        scores = dot(query, keys, ((1,), (1,))) * scale
        probs = dot(grad, values, ((1,), (1,)))
        out = ((column < BLOCK) & (index == 0)) | (
            (column >= 2 * BLOCK) & (column < 3 * BLOCK) & (index == total_blocks - 1)
        )
        near = jnp.where(out, -1e30, scores[:, : 4 * BLOCK])
        scores = jnp.concatenate([near, scores[:, 4 * BLOCK :]], axis=1)
        return n, rows_of, rows, query, grad, keys, values, scores, probs

    def finish(state):
        weighed, scored = [], []
        for n, rows_of, rows, query, grad, keys, values, scores, probs in state:
            peak = jnp.max(scores, axis=1, keepdims=True)
            powers = jnp.exp(scores - peak)
            weights = powers * (1.0 / jnp.sum(powers, axis=1, keepdims=True))
            weighed.append((weights, weights.astype(BF16)))
        for (*_, probs), (weights, weights_b) in zip(state, weighed):
            delta = jnp.sum(weights_b.astype(F32) * probs, axis=1, keepdims=True)
            scored.append((weights * (probs - delta)).astype(BF16))
        for (n, rows_of, rows, query, grad, keys, values, _, _), (_, weights_b), dscore_b in zip(
            state, weighed, scored
        ):
            mixed = dot(weights_b, values, ((1,), (0,)))
            grad_query = dot(dscore_b, keys, ((1,), (0,))) * scale
            mixes[n][0, rows_of] = mixed.astype(BF16)
            mixes[n][1, rows_of] = grad_query.astype(BF16)
            keep[n, 0, rows_of] = dscore_b[:, listed:]
            keep[n, 1, rows_of] = weights_b[:, listed:]
            key_part = dot(dscore_b[:, :listed], query, ((0,), (0,)))
            value_part = dot(weights_b[:, :listed], grad, ((0,), (0,)))
            for m, r in enumerate(rows):
                span = slice(m * BLOCK, (m + 1) * BLOCK)
                acc[0, pl.ds(r, BLOCK)] += key_part[span]
                acc[1, pl.ds(r, BLOCK)] += value_part[span]

    held = None
    for n in range(count):
        for block in range(0, run_blocks, CHUNK):
            state = [begin(n, b) for b in range(block, block + CHUNK)]
            if held is not None:
                finish(held)
            held = state
    finish(held)
    for m in range(2):
        shared = acc[m, 2 * half :]
        for n in range(count):
            shared = shared + dot(keep[n, m], sides[n][m], ((0,), (0,)))
        acc[m, 2 * half :] = shared
        if closes:
            send_ref[m, :half] = acc[m, half : 2 * half]
            send_ref[m, half:] = shared


def attend(where, tables, global_pos, parts, state, sides, turns, rounds, picks):
    opens, closes = state is None, turns[-1] == rounds - 1
    _, tokens, width = sides[0].shape
    run_blocks = tokens // BLOCK
    shared = global_pos.shape[0]
    entries = (3 + picks) * BLOCK + shared
    count = len(turns)
    half = rounds * tokens
    one = jax.ShapeDtypeStruct((2, tokens, width), BF16)
    acc = jax.ShapeDtypeStruct((2, 2 * half + shared, width), F32)
    out_shape = [one] * count
    if opens:
        given = [global_pos.reshape(shared, 1), *parts]
        out_shape += [
            jax.ShapeDtypeStruct((2, 2 * half, width), BF16),
            jax.ShapeDtypeStruct((2, shared, width), BF16),
        ]
        aliases = {}
    else:
        given = list(state)
        aliases = {3 + len(given) - 1: count}
    out_shape += [acc]
    if closes:
        out_shape += [jax.ShapeDtypeStruct((2, half + shared, width), F32)]
    outs = pl.pallas_call(
        functools.partial(
            attend_kernel, rounds, run_blocks, picks, turns, opens, closes
        ),
        out_shape=out_shape,
        in_specs=[SMEM] * 3 + [VMEM] * (len(given) + count),
        out_specs=[VMEM] * len(out_shape),
        input_output_aliases=aliases,
        scratch_shapes=[pltpu.VMEM((count, 2, tokens, shared), BF16)],
        compiler_params=PARAMS,
        cost_estimate=pl.CostEstimate(
            flops=12 * count * tokens * entries * width,
            transcendentals=count * tokens * entries,
            bytes_accessed=12 * half * width,
        ),
        name="attend",
    )(where, *tables, *given, *sides)
    return outs[:count], outs[count:]


def total_kernel(rounds, where_ref, global_ref, acc_ref, came_ref, *outs):
    tokens, width = outs[0].shape[1:]
    half = rounds * tokens
    count = global_ref.shape[1]
    scale = width**-0.5
    flip = (where_ref[1] * rounds + lax.rem(where_ref[0], rounds)) * tokens
    spots = global_ref[...] ^ flip
    halves = []
    for n in range(2):
        shared = acc_ref[n, 2 * half :] + came_ref[n, half:]
        high = shared.astype(BF16)
        halves += [high, (shared - high.astype(F32)).astype(BF16)]
    halves = jnp.concatenate(halves, axis=1)
    for i in range(rounds):
        ids = lax.broadcasted_iota(jnp.int32, (tokens, count), 0) + i * tokens
        hot = jnp.where(ids == spots, 1.0, 0.0).astype(BF16)
        spread = dot(hot, halves, ((1,), (0,)))
        mine = slice(i * tokens, (i + 1) * tokens)
        for n in range(2):
            whole = acc_ref[n, mine] + came_ref[n, mine]
            whole = whole + spread[:, 2 * n * width : (2 * n + 1) * width]
            whole = whole + spread[:, (2 * n + 1) * width : (2 * n + 2) * width]
            if n == 0:
                whole = whole * scale
            outs[i][n] = whole.astype(BF16)


def total(where, global_pos, acc, came, rounds):
    rows, width = came.shape[1:]
    count = global_pos.shape[0]
    tokens = (rows - count) // rounds
    return pl.pallas_call(
        functools.partial(total_kernel, rounds),
        out_shape=[jax.ShapeDtypeStruct((2, tokens, width), BF16)] * rounds,
        in_specs=[SMEM] + [VMEM] * 3,
        out_specs=[VMEM] * rounds,
        compiler_params=PARAMS,
        cost_estimate=pl.CostEstimate(
            flops=4 * rows * width, transcendentals=0, bytes_accessed=20 * rows * width
        ),
        name="total",
    )(where, global_pos.reshape(1, count), acc, came)


def by_heads(query_rows, key_rows, value_rows, grad_out, rand_blocks, global_pos):
    seq_count, head_count = lax.axis_size("seq"), lax.axis_size("head")
    _, rounds, _, picks = rand_blocks.shape
    k, head_index = lax.axis_index("seq"), lax.axis_index("head")
    where = jnp.stack([k, head_index & 1]).astype(jnp.int32)
    sibling = [(i, i ^ 1) for i in range(head_count)]
    trades = [round_pairs(seq_count, head_count, i) for i in range(rounds)]

    def send(parts, first=0):
        out = []
        for n, part in enumerate(parts):
            out.append(lax.ppermute(part, AXES, trades[first + n]))
        return out

    def swap(parts):
        out = []
        for part in parts:
            out.append(lax.ppermute(part, "head", sibling))
        return out

    kv, sides = pack(where, [key_rows, value_rows, query_rows, grad_out], rounds)
    kv = send(kv)
    sides = send(sides)
    table = rand_blocks.reshape(rand_blocks.size)
    tables = [table, *swap([table])]
    parts = kv + swap(kv)
    mixes, state = [], None
    for n in range(GROUPS):
        turns = tuple(range(n * rounds // GROUPS, (n + 1) * rounds // GROUPS))
        mix, new = attend(
            where,
            tables,
            global_pos,
            parts,
            state,
            [sides[t] for t in turns],
            turns,
            rounds,
            picks,
        )
        mixes += send(mix, turns[0])
        state = new if state is None else (*state[:2], *new)
    _, _, acc, leaving = state
    (came,) = swap([leaving])
    grads = total(where, global_pos, acc, came, rounds)
    grads = send(grads)
    attended, grad_query = unpack(where, mixes)
    grad_key, grad_value = unpack(where, grads)
    return attended, grad_query, grad_key, grad_value


def extended_2(value, sides, width):
    for axis, dim in sides:
        size, length = (lax.axis_size(axis), value.shape[dim])
        up = [(i, (i + 1) % size) for i in range(size - 1)]
        down = [(j, i) for i, j in up]
        last = lax.slice_in_dim(value, length - width, length, axis=dim)
        first = lax.slice_in_dim(value, 0, width, axis=dim)
        before = lax.ppermute(last, axis, up)
        after = lax.ppermute(first, axis, down)
        value = jnp.concatenate([before, value, after], axis=dim)
    return value


def by_blocks(query_rows, key_rows, value_rows, grad_out, rand_blocks, global_pos):
    batch_count, tok_local, columns = query_rows.shape
    seq_count = lax.axis_size("seq")
    seq_index = lax.axis_index("seq")
    heads_local = rand_blocks.shape[1]
    total_blocks = rand_blocks.shape[2]
    pick_count = rand_blocks.shape[3]
    head_dim = columns // heads_local
    blocks_local = tok_local // BLOCK
    score_scale = head_dim ** (-0.5)
    slot_count = batch_count * heads_local * blocks_local * pick_count
    capacity = (slot_count + seq_count - 1) // seq_count
    buffer_rows = seq_count * capacity
    f32 = jnp.float32
    bf16 = jnp.bfloat16

    def to_blocks(array):
        return array.reshape(batch_count, blocks_local, BLOCK, heads_local, head_dim).transpose(
            0, 3, 1, 2, 4
        )

    def from_blocks(array):
        return array.transpose(0, 2, 3, 1, 4).reshape(batch_count, tok_local, columns)

    def pair_blocks(array):
        return array.reshape(2, batch_count, blocks_local, BLOCK, heads_local, head_dim).transpose(
            0, 1, 4, 2, 3, 5
        )

    def global_sum(array):
        return lax.psum(array, "seq")

    key_value = jnp.stack([key_rows, value_rows])
    edge_rows = jnp.concatenate([key_value[:, :, :BLOCK], key_value[:, :, -BLOCK:]], axis=2)
    extended = extended_2(edge_rows, (("seq", 2),), BLOCK)
    padded = jnp.concatenate([extended[:, :, :BLOCK], key_value, extended[:, :, -BLOCK:]], axis=2)

    def shifted(start):
        return pair_blocks(padded[:, :, start : start + tok_local])

    window_lists = jnp.concatenate([shifted(0), shifted(BLOCK), shifted(2 * BLOCK)], axis=4)
    my_table = lax.dynamic_slice_in_dim(
        rand_blocks, seq_index * blocks_local, blocks_local, 2
    ).reshape(slot_count)
    holder = my_table // blocks_local
    holder_hot = (holder[:, None] == jnp.arange(seq_count)[None, :]).astype(jnp.int32)
    holder_rank = jnp.sum((jnp.cumsum(holder_hot, axis=0) - 1) * holder_hot, axis=1)
    position = holder * capacity + holder_rank
    requests = rand_blocks.reshape(batch_count, heads_local, seq_count, blocks_local, pick_count)
    requests = requests.transpose(2, 0, 1, 3, 4).reshape(seq_count, slot_count)
    wanted = (requests // blocks_local == seq_index).astype(jnp.int32)
    wanted_rank = jnp.cumsum(wanted, axis=1) - 1
    chosen = wanted[:, None, :] * (
        wanted_rank[:, None, :] == jnp.arange(capacity)[None, :, None]
    ).astype(jnp.int32)
    slot_live = (jnp.sum(chosen, axis=2) > 0).reshape(buffer_rows)
    slot_index = jnp.sum(chosen * jnp.arange(slot_count)[None, None, :], axis=2)
    which_batch = slot_index // (heads_local * blocks_local * pick_count)
    which_head = slot_index // (blocks_local * pick_count) % heads_local
    which_block = jnp.take_along_axis(requests, slot_index, axis=1) % blocks_local
    stacked = key_value.reshape(
        2, batch_count, blocks_local, BLOCK, heads_local, head_dim
    ).transpose(1, 2, 4, 0, 3, 5)
    outgoing = stacked[which_batch, which_block, which_head].reshape(
        buffer_rows, 2, BLOCK, head_dim
    )
    incoming = lax.all_to_all(outgoing, "seq", split_axis=0, concat_axis=0, tiled=True)
    fetched = incoming[position].reshape(
        batch_count, heads_local, blocks_local, pick_count, 2, BLOCK, head_dim
    )
    fetched = fetched.transpose(4, 0, 1, 2, 3, 5, 6).reshape(
        2, batch_count, heads_local, blocks_local, pick_count * BLOCK, head_dim
    )
    local_pos = global_pos - seq_index * tok_local
    pick_hot = (local_pos[:, None] == jnp.arange(tok_local)[None, :]).astype(bf16)
    owned_rows = jnp.einsum("gt,pbtc->pbgc", pick_hot, key_value, preferred_element_type=f32)
    shared = global_sum(owned_rows).astype(bf16)
    globals_count = shared.shape[2]
    global_kv = shared.reshape(2, batch_count, globals_count, heads_local, head_dim).transpose(
        0, 1, 3, 2, 4
    )
    global_kv = jnp.broadcast_to(
        global_kv[:, :, :, None],
        (2, batch_count, heads_local, blocks_local, globals_count, head_dim),
    )
    lists_all = jnp.concatenate([window_lists, fetched, global_kv], axis=4)
    key_lists = lists_all[0]
    value_lists = lists_all[1]
    key_count = key_lists.shape[3]
    block_ids = seq_index * blocks_local + jnp.arange(blocks_local)
    column_ids = jnp.arange(key_count)[None, :]
    middle_ok = jnp.where(
        (column_ids >= 2 * BLOCK) & (column_ids < 3 * BLOCK),
        (block_ids < total_blocks - 1)[:, None],
        True,
    )
    valid_mask = jnp.where(column_ids < BLOCK, (block_ids > 0)[:, None], middle_ok)
    query_blocks = to_blocks(query_rows)
    grad_blocks = to_blocks(grad_out)
    scores = (
        jnp.einsum("bhjqd,bhjkd->bhjqk", query_blocks, key_lists, preferred_element_type=f32)
        * score_scale
    )
    scores = jnp.where(valid_mask[None, None, :, None, :], scores, -1e30)
    row_max = jnp.max(scores, axis=-1, keepdims=True)
    log_total = row_max + jnp.log(jnp.sum(jnp.exp(scores - row_max), axis=-1, keepdims=True))
    weights = jnp.exp(scores - log_total)
    weights_b = weights.astype(bf16)
    mixed_rows = jnp.einsum(
        "bhjqk,bhjkd->bhjqd", weights_b, value_lists, preferred_element_type=f32
    )
    attended = from_blocks(mixed_rows.astype(bf16))
    row_delta = jnp.sum(grad_blocks.astype(f32) * mixed_rows, axis=-1, keepdims=True)
    grad_probs = jnp.einsum(
        "bhjqd,bhjkd->bhjqk", grad_blocks, value_lists, preferred_element_type=f32
    )
    dscore_b = (weights * (grad_probs - row_delta)).astype(bf16)
    grad_query = (
        jnp.einsum("bhjqk,bhjkd->bhjqd", dscore_b, key_lists, preferred_element_type=f32)
        * score_scale
    )

    def key_grads(lower, upper):
        key_part = (
            jnp.einsum(
                "bhjqk,bhjqd->bhjkd",
                dscore_b[..., lower:upper],
                query_blocks,
                preferred_element_type=f32,
            )
            * score_scale
        )
        value_part = jnp.einsum(
            "bhjqk,bhjqd->bhjkd",
            weights_b[..., lower:upper],
            grad_blocks,
            preferred_element_type=f32,
        )
        return jnp.stack([key_part, value_part])

    window_cols = 3 * BLOCK
    random_cols = pick_count * BLOCK
    window_grads = key_grads(0, window_cols).reshape(
        2, batch_count, heads_local, blocks_local, 3, BLOCK, head_dim
    )
    padded_grads = jnp.pad(
        window_grads[:, :, :, :, 0], ((0, 0), (0, 0), (0, 0), (0, 2), (0, 0), (0, 0))
    )
    padded_grads = padded_grads + jnp.pad(
        window_grads[:, :, :, :, 1], ((0, 0), (0, 0), (0, 0), (1, 1), (0, 0), (0, 0))
    )
    padded_grads = padded_grads + jnp.pad(
        window_grads[:, :, :, :, 2], ((0, 0), (0, 0), (0, 0), (2, 0), (0, 0), (0, 0))
    )
    own_grads = padded_grads[:, :, :, 1:-1]
    rim_grads = jnp.stack([padded_grads[:, :, :, 0], padded_grads[:, :, :, -1]], axis=3)
    returned = extended_2(rim_grads.astype(jnp.bfloat16), (("seq", 3),), 1).astype(rim_grads.dtype)
    own_grads = own_grads.at[:, :, :, 0].add(returned[:, :, :, 0])
    own_grads = own_grads.at[:, :, :, -1].add(returned[:, :, :, 3])
    global_grads = jnp.sum(key_grads(window_cols + random_cols, key_count), axis=3)
    global_grads = global_grads.transpose(0, 1, 3, 2, 4).reshape(
        2, batch_count, globals_count, columns
    )
    global_summed = global_sum(global_grads)
    inside = (local_pos >= 0) & (local_pos < tok_local)
    safe_pos = jnp.where(inside, local_pos, tok_local)
    global_local = (
        jnp.zeros((2, batch_count, tok_local, columns), f32)
        .at[:, :, safe_pos]
        .add(global_summed, mode="drop")
    )
    global_part = pair_blocks(global_local)
    target = ((which_batch * blocks_local + which_block) * heads_local + which_head).reshape(
        buffer_rows
    )
    random_grads = key_grads(window_cols, window_cols + random_cols)
    per_slot = random_grads.reshape(
        2, batch_count, heads_local, blocks_local, pick_count, BLOCK, head_dim
    )
    per_slot = per_slot.transpose(1, 2, 3, 4, 0, 5, 6).reshape(slot_count, 2, BLOCK, head_dim)
    sending = jnp.zeros((buffer_rows, 2, BLOCK, head_dim), f32).at[position].set(per_slot)
    arrived = lax.all_to_all(
        sending.astype(jnp.bfloat16), "seq", split_axis=0, concat_axis=0, tiled=True
    ).astype(sending.dtype)
    kept = jnp.where(slot_live[:, None, None, None], arrived, 0.0)
    summed = (
        jnp.zeros((batch_count * blocks_local * heads_local, 2, BLOCK, head_dim), f32)
        .at[target]
        .add(kept)
    )
    random_part = summed.reshape(
        batch_count, blocks_local, heads_local, 2, BLOCK, head_dim
    ).transpose(3, 0, 2, 1, 4, 5)
    total_grads = own_grads + random_part + global_part
    grad_key = from_blocks(total_grads[0].astype(bf16))
    grad_value = from_blocks(total_grads[1].astype(bf16))
    return (attended, from_blocks(grad_query.astype(bf16)), grad_key, grad_value)


def body(query_rows, key_rows, value_rows, grad_out, rand_blocks, global_pos):
    seq_count, head_count = lax.axis_size("seq"), lax.axis_size("head")
    batch_count, heads_local = rand_blocks.shape[:2]
    tokens = query_rows.shape[1]
    whole_heads = seq_count == 2 * heads_local and heads_local & (heads_local - 1) == 0
    whole_heads = whole_heads and heads_local > 1 and tokens & (tokens - 1) == 0
    whole_heads = whole_heads and head_count % 2 == 0 and batch_count == 1
    form = by_heads if whole_heads else by_blocks
    return form(query_rows, key_rows, value_rows, grad_out, rand_blocks, global_pos)


def solution(mesh):
    return jax.shard_map(
        body,
        mesh=mesh,
        in_specs=(
            P(None, "seq", "head"),
            P(None, "seq", "head"),
            P(None, "seq", "head"),
            P(None, "seq", "head"),
            P(None, "head", None, None),
            P(),
        ),
        out_specs=(
            P(None, "seq", "head"),
            P(None, "seq", "head"),
            P(None, "seq", "head"),
            P(None, "seq", "head"),
        ),
        check_vma=False,
    )
```

```python
import functools

import jax
import jax.numpy as jnp
from jax import lax
from jax.experimental import pallas as pl
from jax.experimental.pallas import tpu as pltpu
from jax.sharding import PartitionSpec as P


BLOCK = 64
AXES = ("seq", "head")
GROUPS = 2
CHUNK = 2
GRANT = 24 * 1024 * 1024
VMEM = pl.BlockSpec(memory_space=pltpu.VMEM)
SMEM = pl.BlockSpec(memory_space=pltpu.SMEM)
PARAMS = pltpu.CompilerParams(vmem_limit_bytes=GRANT)
PACK_PARAMS = pltpu.CompilerParams(vmem_limit_bytes=GRANT)
HBM = pl.BlockSpec(memory_space=pltpu.HBM)
F32 = jnp.float32
BF16 = jnp.bfloat16


def dot(a, b, dims):
    return lax.dot_general(a, b, (dims, ((), ())), preferred_element_type=F32)


def round_pairs(seq_count, head_count, i):
    rounds = seq_count // 2
    pairs = []
    for s in range(seq_count):
        for head in range(head_count):
            y, c = head // 2, head % 2
            k = rounds * c + (s % rounds ^ i)
            pairs.append((s * head_count + head, k * head_count + 2 * y + s // rounds))
    return pairs


def keep_in_hbm(array):
    return pltpu.with_memory_space_constraint(array, pltpu.HBM)


def pack_kernel(rounds, width, where_ref, *rest):
    ins, outs, sem = rest[:4], rest[4:-1], rest[-1]
    turn = lax.rem(where_ref[0], rounds)
    copies = []
    for m in range(2):
        for i in range(rounds):
            col = pl.multiple_of((turn ^ i) * width, width)
            for n in range(2):
                copy = pltpu.make_async_copy(
                    ins[2 * m + n].at[0, :, pl.ds(col, width)],
                    outs[m * rounds + i].at[n],
                    sem.at[m * rounds + i, n],
                )
                copy.start()
                copies.append(copy)
    for copy in copies:
        copy.wait()


def pack(where, arrays, rounds):
    _, tokens, columns = arrays[0].shape
    width = columns // rounds
    out = jax.ShapeDtypeStruct((2, tokens, width), BF16)
    outs = pl.pallas_call(
        functools.partial(pack_kernel, rounds, width),
        out_shape=[out] * (2 * rounds),
        in_specs=[SMEM] + [HBM] * 4,
        out_specs=[VMEM] * (2 * rounds),
        scratch_shapes=[pltpu.SemaphoreType.DMA((2 * rounds, 2))],
        compiler_params=PACK_PARAMS,
        cost_estimate=pl.CostEstimate(
            flops=0, transcendentals=0, bytes_accessed=16 * tokens * columns
        ),
        name="pack",
    )(where, *[keep_in_hbm(a) for a in arrays])
    return outs[:rounds], outs[rounds:]


def unpack_kernel(rounds, width, where_ref, *rest):
    ins, outs, sem = rest[:rounds], rest[rounds:-1], rest[-1]
    turn = lax.rem(where_ref[0], rounds)
    copies = []
    for i in range(rounds):
        col = pl.multiple_of((turn ^ i) * width, width)
        for n in range(2):
            copy = pltpu.make_async_copy(
                ins[i].at[n], outs[n].at[0, :, pl.ds(col, width)], sem.at[i, n]
            )
            copy.start()
            copies.append(copy)
    for copy in copies:
        copy.wait()


def unpack(where, parts):
    rounds = len(parts)
    _, tokens, width = parts[0].shape
    out = jax.ShapeDtypeStruct((1, tokens, rounds * width), BF16)
    return pl.pallas_call(
        functools.partial(unpack_kernel, rounds, width),
        out_shape=[out] * 2,
        in_specs=[SMEM] + [VMEM] * rounds,
        out_specs=[HBM] * 2,
        scratch_shapes=[pltpu.SemaphoreType.DMA((rounds, 2))],
        compiler_params=PARAMS,
        cost_estimate=pl.CostEstimate(
            flops=0, transcendentals=0, bytes_accessed=8 * rounds * tokens * width
        ),
        name="unpack",
    )(where, *parts)


def attend_kernel(
    rounds, run_blocks, picks, turns, opens, closes, where_ref, mine_ref, other_table_ref, *rest
):
    rest = list(rest)
    take = lambda n: [rest.pop(0) for _ in range(n)]
    count = len(turns)
    if opens:
        (global_ref,), parts = take(1), take(2 * rounds)
    else:
        all_ref, picked_ref, _ = take(3)
    sides = take(count)
    mixes = take(count)
    if opens:
        all_ref, picked_ref = take(2)
    (acc,) = take(1)
    if closes:
        (send_ref,) = take(1)
    (keep,) = take(1)

    k, h = where_ref[0], where_ref[1]
    tokens = run_blocks * BLOCK
    half = rounds * tokens
    total_blocks = 2 * rounds * run_blocks
    listed = (3 + picks) * BLOCK
    flip = (h * rounds + lax.rem(k, rounds)) * run_blocks
    head = lax.rem(k, rounds) * (total_blocks * picks)
    mine = k // rounds == h
    scale = all_ref.shape[2] ** -0.5
    column = lax.broadcasted_iota(jnp.int32, (1, 4 * BLOCK), 1)

    if opens:
        shared = global_ref.shape[1]
        spots = jnp.broadcast_to(global_ref[...] ^ (flip * BLOCK), (shared, shared)).T[:, :1]
        sums = [None, None]
        for n in range(2 * rounds):
            ids = lax.broadcasted_iota(jnp.int32, (shared, tokens), 1) + n * tokens
            hot = jnp.where(ids == spots, 1.0, 0.0).astype(BF16)
            for m in range(2):
                part = parts[n][m]
                all_ref[m, n * tokens : (n + 1) * tokens] = part
                product = dot(hot, part, ((1,), (0,)))
                sums[m] = product if n == 0 else sums[m] + product
        for m in range(2):
            picked_ref[m] = sums[m].astype(BF16)
        acc[...] = jnp.zeros_like(acc)

    def begin(n, block):
        rows_of = slice(block * BLOCK, (block + 1) * BLOCK)
        query, grad = sides[n][0, rows_of], sides[n][1, rows_of]
        index = (turns[n] * run_blocks + block) ^ flip
        named = [
            jnp.maximum(index - 1, 0),
            index,
            jnp.minimum(index + 1, total_blocks - 1),
        ]
        for m in range(picks):
            at = head + index * picks + m
            named.append(jnp.where(mine, mine_ref[at], other_table_ref[at]))
        rows = [pl.multiple_of((b ^ flip) * BLOCK, BLOCK) for b in named]
        keys, values = [
            jnp.concatenate(
                [all_ref[m, pl.ds(r, BLOCK)] for r in rows] + [picked_ref[m]], axis=0
            )
            for m in range(2)
        ]
        scores = dot(query, keys, ((1,), (1,))) * scale
        probs = dot(grad, values, ((1,), (1,)))
        out = ((column < BLOCK) & (index == 0)) | (
            (column >= 2 * BLOCK) & (column < 3 * BLOCK) & (index == total_blocks - 1)
        )
        near = jnp.where(out, -1e30, scores[:, : 4 * BLOCK])
        scores = jnp.concatenate([near, scores[:, 4 * BLOCK :]], axis=1)
        return n, rows_of, rows, query, grad, keys, values, scores, probs

    def finish(state):
        weighed, scored = [], []
        for n, rows_of, rows, query, grad, keys, values, scores, probs in state:
            peak = jnp.max(scores, axis=1, keepdims=True)
            powers = jnp.exp(scores - peak)
            weights = powers * (1.0 / jnp.sum(powers, axis=1, keepdims=True))
            weighed.append((weights, weights.astype(BF16)))
        for (*_, probs), (weights, weights_b) in zip(state, weighed):
            delta = jnp.sum(weights_b.astype(F32) * probs, axis=1, keepdims=True)
            scored.append((weights * (probs - delta)).astype(BF16))
        for (n, rows_of, rows, query, grad, keys, values, _, _), (_, weights_b), dscore_b in zip(
            state, weighed, scored
        ):
            mixed = dot(weights_b, values, ((1,), (0,)))
            grad_query = dot(dscore_b, keys, ((1,), (0,))) * scale
            mixes[n][0, rows_of] = mixed.astype(BF16)
            mixes[n][1, rows_of] = grad_query.astype(BF16)
            keep[n, 0, rows_of] = dscore_b[:, listed:]
            keep[n, 1, rows_of] = weights_b[:, listed:]
            key_part = dot(dscore_b[:, :listed], query, ((0,), (0,)))
            value_part = dot(weights_b[:, :listed], grad, ((0,), (0,)))
            for m, r in enumerate(rows):
                span = slice(m * BLOCK, (m + 1) * BLOCK)
                acc[0, pl.ds(r, BLOCK)] += key_part[span]
                acc[1, pl.ds(r, BLOCK)] += value_part[span]

    held = None
    for n in range(count):
        for block in range(0, run_blocks, CHUNK):
            state = [begin(n, b) for b in range(block, block + CHUNK)]
            if held is not None:
                finish(held)
            held = state
    finish(held)
    for m in range(2):
        shared = acc[m, 2 * half :]
        for n in range(count):
            shared = shared + dot(keep[n, m], sides[n][m], ((0,), (0,)))
        acc[m, 2 * half :] = shared
        if closes:
            send_ref[m, :half] = acc[m, half : 2 * half]
            send_ref[m, half:] = shared


def attend(where, tables, global_pos, parts, state, sides, turns, rounds, picks):
    opens, closes = state is None, turns[-1] == rounds - 1
    _, tokens, width = sides[0].shape
    run_blocks = tokens // BLOCK
    shared = global_pos.shape[0]
    entries = (3 + picks) * BLOCK + shared
    count = len(turns)
    half = rounds * tokens
    one = jax.ShapeDtypeStruct((2, tokens, width), BF16)
    acc = jax.ShapeDtypeStruct((2, 2 * half + shared, width), F32)
    out_shape = [one] * count
    if opens:
        given = [global_pos.reshape(1, shared), *parts]
        out_shape += [
            jax.ShapeDtypeStruct((2, 2 * half, width), BF16),
            jax.ShapeDtypeStruct((2, shared, width), BF16),
        ]
        aliases = {}
    else:
        given = list(state)
        aliases = {3 + len(given) - 1: count}
    out_shape += [acc]
    if closes:
        out_shape += [jax.ShapeDtypeStruct((2, half + shared, width), F32)]
    outs = pl.pallas_call(
        functools.partial(
            attend_kernel, rounds, run_blocks, picks, turns, opens, closes
        ),
        out_shape=out_shape,
        in_specs=[SMEM] * 3 + [VMEM] * (len(given) + count),
        out_specs=[VMEM] * len(out_shape),
        input_output_aliases=aliases,
        scratch_shapes=[pltpu.VMEM((count, 2, tokens, shared), BF16)],
        compiler_params=PARAMS,
        cost_estimate=pl.CostEstimate(
            flops=12 * count * tokens * entries * width,
            transcendentals=count * tokens * entries,
            bytes_accessed=12 * half * width,
        ),
        name="attend",
    )(where, *tables, *given, *sides)
    return outs[:count], outs[count:]


def total_kernel(rounds, where_ref, global_ref, acc_ref, came_ref, *outs):
    tokens, width = outs[0].shape[1:]
    half = rounds * tokens
    count = global_ref.shape[1]
    scale = width**-0.5
    flip = (where_ref[1] * rounds + lax.rem(where_ref[0], rounds)) * tokens
    spots = global_ref[...] ^ flip
    halves = []
    for n in range(2):
        shared = acc_ref[n, 2 * half :] + came_ref[n, half:]
        high = shared.astype(BF16)
        halves += [high, (shared - high.astype(F32)).astype(BF16)]
    halves = jnp.concatenate(halves, axis=1)
    for i in range(rounds):
        ids = lax.broadcasted_iota(jnp.int32, (tokens, count), 0) + i * tokens
        hot = jnp.where(ids == spots, 1.0, 0.0).astype(BF16)
        spread = dot(hot, halves, ((1,), (0,)))
        mine = slice(i * tokens, (i + 1) * tokens)
        for n in range(2):
            whole = acc_ref[n, mine] + came_ref[n, mine]
            whole = whole + spread[:, 2 * n * width : (2 * n + 1) * width]
            whole = whole + spread[:, (2 * n + 1) * width : (2 * n + 2) * width]
            if n == 0:
                whole = whole * scale
            outs[i][n] = whole.astype(BF16)


def total(where, global_pos, acc, came, rounds):
    rows, width = came.shape[1:]
    count = global_pos.shape[0]
    tokens = (rows - count) // rounds
    return pl.pallas_call(
        functools.partial(total_kernel, rounds),
        out_shape=[jax.ShapeDtypeStruct((2, tokens, width), BF16)] * rounds,
        in_specs=[SMEM] + [VMEM] * 3,
        out_specs=[VMEM] * rounds,
        compiler_params=PARAMS,
        cost_estimate=pl.CostEstimate(
            flops=4 * rows * width, transcendentals=0, bytes_accessed=20 * rows * width
        ),
        name="total",
    )(where, global_pos.reshape(1, count), acc, came)


def by_heads(query_rows, key_rows, value_rows, grad_out, rand_blocks, global_pos):
    seq_count, head_count = lax.axis_size("seq"), lax.axis_size("head")
    _, rounds, _, picks = rand_blocks.shape
    k, head_index = lax.axis_index("seq"), lax.axis_index("head")
    where = jnp.stack([k, head_index & 1]).astype(jnp.int32)
    sibling = [(i, i ^ 1) for i in range(head_count)]
    trades = [round_pairs(seq_count, head_count, i) for i in range(rounds)]

    def send(parts, first=0):
        out = []
        for n, part in enumerate(parts):
            out.append(lax.ppermute(part, AXES, trades[first + n]))
        return out

    def swap(parts):
        out = []
        for part in parts:
            out.append(lax.ppermute(part, "head", sibling))
        return out

    kv, sides = pack(where, [key_rows, value_rows, query_rows, grad_out], rounds)
    kv = send(kv)
    sides = send(sides)
    table = rand_blocks.reshape(rand_blocks.size)
    tables = [table, *swap([table])]
    parts = kv + swap(kv)
    mixes, state = [], None
    for n in range(GROUPS):
        turns = tuple(range(n * rounds // GROUPS, (n + 1) * rounds // GROUPS))
        mix, new = attend(
            where,
            tables,
            global_pos,
            parts,
            state,
            [sides[t] for t in turns],
            turns,
            rounds,
            picks,
        )
        mixes += send(mix, turns[0])
        state = new if state is None else (*state[:2], *new)
    _, _, acc, leaving = state
    (came,) = swap([leaving])
    grads = total(where, global_pos, acc, came, rounds)
    grads = send(grads)
    attended, grad_query = unpack(where, mixes)
    grad_key, grad_value = unpack(where, grads)
    return attended, grad_query, grad_key, grad_value


def extended_2(value, sides, width):
    for axis, dim in sides:
        size, length = (lax.axis_size(axis), value.shape[dim])
        up = [(i, (i + 1) % size) for i in range(size - 1)]
        down = [(j, i) for i, j in up]
        last = lax.slice_in_dim(value, length - width, length, axis=dim)
        first = lax.slice_in_dim(value, 0, width, axis=dim)
        before = lax.ppermute(last, axis, up)
        after = lax.ppermute(first, axis, down)
        value = jnp.concatenate([before, value, after], axis=dim)
    return value


def by_blocks(query_rows, key_rows, value_rows, grad_out, rand_blocks, global_pos):
    batch_count, tok_local, columns = query_rows.shape
    seq_count = lax.axis_size("seq")
    seq_index = lax.axis_index("seq")
    heads_local = rand_blocks.shape[1]
    total_blocks = rand_blocks.shape[2]
    pick_count = rand_blocks.shape[3]
    head_dim = columns // heads_local
    blocks_local = tok_local // BLOCK
    score_scale = head_dim ** (-0.5)
    slot_count = batch_count * heads_local * blocks_local * pick_count
    capacity = (slot_count + seq_count - 1) // seq_count
    buffer_rows = seq_count * capacity
    f32 = jnp.float32
    bf16 = jnp.bfloat16

    def to_blocks(array):
        return array.reshape(batch_count, blocks_local, BLOCK, heads_local, head_dim).transpose(
            0, 3, 1, 2, 4
        )

    def from_blocks(array):
        return array.transpose(0, 2, 3, 1, 4).reshape(batch_count, tok_local, columns)

    def pair_blocks(array):
        return array.reshape(2, batch_count, blocks_local, BLOCK, heads_local, head_dim).transpose(
            0, 1, 4, 2, 3, 5
        )

    def global_sum(array):
        return lax.psum(array, "seq")

    key_value = jnp.stack([key_rows, value_rows])
    edge_rows = jnp.concatenate([key_value[:, :, :BLOCK], key_value[:, :, -BLOCK:]], axis=2)
    extended = extended_2(edge_rows, (("seq", 2),), BLOCK)
    padded = jnp.concatenate([extended[:, :, :BLOCK], key_value, extended[:, :, -BLOCK:]], axis=2)

    def shifted(start):
        return pair_blocks(padded[:, :, start : start + tok_local])

    window_lists = jnp.concatenate([shifted(0), shifted(BLOCK), shifted(2 * BLOCK)], axis=4)
    my_table = lax.dynamic_slice_in_dim(
        rand_blocks, seq_index * blocks_local, blocks_local, 2
    ).reshape(slot_count)
    holder = my_table // blocks_local
    holder_hot = (holder[:, None] == jnp.arange(seq_count)[None, :]).astype(jnp.int32)
    holder_rank = jnp.sum((jnp.cumsum(holder_hot, axis=0) - 1) * holder_hot, axis=1)
    position = holder * capacity + holder_rank
    requests = rand_blocks.reshape(batch_count, heads_local, seq_count, blocks_local, pick_count)
    requests = requests.transpose(2, 0, 1, 3, 4).reshape(seq_count, slot_count)
    wanted = (requests // blocks_local == seq_index).astype(jnp.int32)
    wanted_rank = jnp.cumsum(wanted, axis=1) - 1
    chosen = wanted[:, None, :] * (
        wanted_rank[:, None, :] == jnp.arange(capacity)[None, :, None]
    ).astype(jnp.int32)
    slot_live = (jnp.sum(chosen, axis=2) > 0).reshape(buffer_rows)
    slot_index = jnp.sum(chosen * jnp.arange(slot_count)[None, None, :], axis=2)
    which_batch = slot_index // (heads_local * blocks_local * pick_count)
    which_head = slot_index // (blocks_local * pick_count) % heads_local
    which_block = jnp.take_along_axis(requests, slot_index, axis=1) % blocks_local
    stacked = key_value.reshape(
        2, batch_count, blocks_local, BLOCK, heads_local, head_dim
    ).transpose(1, 2, 4, 0, 3, 5)
    outgoing = stacked[which_batch, which_block, which_head].reshape(
        buffer_rows, 2, BLOCK, head_dim
    )
    incoming = lax.all_to_all(outgoing, "seq", split_axis=0, concat_axis=0, tiled=True)
    fetched = incoming[position].reshape(
        batch_count, heads_local, blocks_local, pick_count, 2, BLOCK, head_dim
    )
    fetched = fetched.transpose(4, 0, 1, 2, 3, 5, 6).reshape(
        2, batch_count, heads_local, blocks_local, pick_count * BLOCK, head_dim
    )
    local_pos = global_pos - seq_index * tok_local
    pick_hot = (local_pos[:, None] == jnp.arange(tok_local)[None, :]).astype(bf16)
    owned_rows = jnp.einsum("gt,pbtc->pbgc", pick_hot, key_value, preferred_element_type=f32)
    shared = global_sum(owned_rows).astype(bf16)
    globals_count = shared.shape[2]
    global_kv = shared.reshape(2, batch_count, globals_count, heads_local, head_dim).transpose(
        0, 1, 3, 2, 4
    )
    global_kv = jnp.broadcast_to(
        global_kv[:, :, :, None],
        (2, batch_count, heads_local, blocks_local, globals_count, head_dim),
    )
    lists_all = jnp.concatenate([window_lists, fetched, global_kv], axis=4)
    key_lists = lists_all[0]
    value_lists = lists_all[1]
    key_count = key_lists.shape[3]
    block_ids = seq_index * blocks_local + jnp.arange(blocks_local)
    column_ids = jnp.arange(key_count)[None, :]
    middle_ok = jnp.where(
        (column_ids >= 2 * BLOCK) & (column_ids < 3 * BLOCK),
        (block_ids < total_blocks - 1)[:, None],
        True,
    )
    valid_mask = jnp.where(column_ids < BLOCK, (block_ids > 0)[:, None], middle_ok)
    query_blocks = to_blocks(query_rows)
    grad_blocks = to_blocks(grad_out)
    scores = (
        jnp.einsum("bhjqd,bhjkd->bhjqk", query_blocks, key_lists, preferred_element_type=f32)
        * score_scale
    )
    scores = jnp.where(valid_mask[None, None, :, None, :], scores, -1e30)
    row_max = jnp.max(scores, axis=-1, keepdims=True)
    log_total = row_max + jnp.log(jnp.sum(jnp.exp(scores - row_max), axis=-1, keepdims=True))
    weights = jnp.exp(scores - log_total)
    weights_b = weights.astype(bf16)
    mixed_rows = jnp.einsum(
        "bhjqk,bhjkd->bhjqd", weights_b, value_lists, preferred_element_type=f32
    )
    attended = from_blocks(mixed_rows.astype(bf16))
    row_delta = jnp.sum(grad_blocks.astype(f32) * mixed_rows, axis=-1, keepdims=True)
    grad_probs = jnp.einsum(
        "bhjqd,bhjkd->bhjqk", grad_blocks, value_lists, preferred_element_type=f32
    )
    dscore_b = (weights * (grad_probs - row_delta)).astype(bf16)
    grad_query = (
        jnp.einsum("bhjqk,bhjkd->bhjqd", dscore_b, key_lists, preferred_element_type=f32)
        * score_scale
    )

    def key_grads(lower, upper):
        key_part = (
            jnp.einsum(
                "bhjqk,bhjqd->bhjkd",
                dscore_b[..., lower:upper],
                query_blocks,
                preferred_element_type=f32,
            )
            * score_scale
        )
        value_part = jnp.einsum(
            "bhjqk,bhjqd->bhjkd",
            weights_b[..., lower:upper],
            grad_blocks,
            preferred_element_type=f32,
        )
        return jnp.stack([key_part, value_part])

    window_cols = 3 * BLOCK
    random_cols = pick_count * BLOCK
    window_grads = key_grads(0, window_cols).reshape(
        2, batch_count, heads_local, blocks_local, 3, BLOCK, head_dim
    )
    padded_grads = jnp.pad(
        window_grads[:, :, :, :, 0], ((0, 0), (0, 0), (0, 0), (0, 2), (0, 0), (0, 0))
    )
    padded_grads = padded_grads + jnp.pad(
        window_grads[:, :, :, :, 1], ((0, 0), (0, 0), (0, 0), (1, 1), (0, 0), (0, 0))
    )
    padded_grads = padded_grads + jnp.pad(
        window_grads[:, :, :, :, 2], ((0, 0), (0, 0), (0, 0), (2, 0), (0, 0), (0, 0))
    )
    own_grads = padded_grads[:, :, :, 1:-1]
    rim_grads = jnp.stack([padded_grads[:, :, :, 0], padded_grads[:, :, :, -1]], axis=3)
    returned = extended_2(rim_grads.astype(jnp.bfloat16), (("seq", 3),), 1).astype(rim_grads.dtype)
    own_grads = own_grads.at[:, :, :, 0].add(returned[:, :, :, 0])
    own_grads = own_grads.at[:, :, :, -1].add(returned[:, :, :, 3])
    global_grads = jnp.sum(key_grads(window_cols + random_cols, key_count), axis=3)
    global_grads = global_grads.transpose(0, 1, 3, 2, 4).reshape(
        2, batch_count, globals_count, columns
    )
    global_summed = global_sum(global_grads)
    inside = (local_pos >= 0) & (local_pos < tok_local)
    safe_pos = jnp.where(inside, local_pos, tok_local)
    global_local = (
        jnp.zeros((2, batch_count, tok_local, columns), f32)
        .at[:, :, safe_pos]
        .add(global_summed, mode="drop")
    )
    global_part = pair_blocks(global_local)
    target = ((which_batch * blocks_local + which_block) * heads_local + which_head).reshape(
        buffer_rows
    )
    random_grads = key_grads(window_cols, window_cols + random_cols)
    per_slot = random_grads.reshape(
        2, batch_count, heads_local, blocks_local, pick_count, BLOCK, head_dim
    )
    per_slot = per_slot.transpose(1, 2, 3, 4, 0, 5, 6).reshape(slot_count, 2, BLOCK, head_dim)
    sending = jnp.zeros((buffer_rows, 2, BLOCK, head_dim), f32).at[position].set(per_slot)
    arrived = lax.all_to_all(
        sending.astype(jnp.bfloat16), "seq", split_axis=0, concat_axis=0, tiled=True
    ).astype(sending.dtype)
    kept = jnp.where(slot_live[:, None, None, None], arrived, 0.0)
    summed = (
        jnp.zeros((batch_count * blocks_local * heads_local, 2, BLOCK, head_dim), f32)
        .at[target]
        .add(kept)
    )
    random_part = summed.reshape(
        batch_count, blocks_local, heads_local, 2, BLOCK, head_dim
    ).transpose(3, 0, 2, 1, 4, 5)
    total_grads = own_grads + random_part + global_part
    grad_key = from_blocks(total_grads[0].astype(bf16))
    grad_value = from_blocks(total_grads[1].astype(bf16))
    return (attended, from_blocks(grad_query.astype(bf16)), grad_key, grad_value)


def body(query_rows, key_rows, value_rows, grad_out, rand_blocks, global_pos):
    seq_count, head_count = lax.axis_size("seq"), lax.axis_size("head")
    batch_count, heads_local = rand_blocks.shape[:2]
    tokens = query_rows.shape[1]
    whole_heads = seq_count == 2 * heads_local and heads_local & (heads_local - 1) == 0
    whole_heads = whole_heads and heads_local > 1 and tokens & (tokens - 1) == 0
    whole_heads = whole_heads and head_count % 2 == 0 and batch_count == 1
    form = by_heads if whole_heads else by_blocks
    return form(query_rows, key_rows, value_rows, grad_out, rand_blocks, global_pos)


def solution(mesh):
    return jax.shard_map(
        body,
        mesh=mesh,
        in_specs=(
            P(None, "seq", "head"),
            P(None, "seq", "head"),
            P(None, "seq", "head"),
            P(None, "seq", "head"),
            P(None, "head", None, None),
            P(),
        ),
        out_specs=(
            P(None, "seq", "head"),
            P(None, "seq", "head"),
            P(None, "seq", "head"),
            P(None, "seq", "head"),
        ),
        check_vma=False,
    )
```

```python
import functools

import jax
import jax.numpy as jnp
from jax import lax
from jax.experimental import pallas as pl
from jax.experimental.pallas import tpu as pltpu
from jax.sharding import PartitionSpec as P


BLOCK = 64
AXES = ("seq", "head")
CHUNK = 4
GRANT = 24 * 1024 * 1024
VMEM = pl.BlockSpec(memory_space=pltpu.VMEM)
SMEM = pl.BlockSpec(memory_space=pltpu.SMEM)
PARAMS = pltpu.CompilerParams(vmem_limit_bytes=GRANT)
PACK_PARAMS = pltpu.CompilerParams(vmem_limit_bytes=GRANT)
HBM = pl.BlockSpec(memory_space=pltpu.HBM)
F32 = jnp.float32
BF16 = jnp.bfloat16


def dot(a, b, dims):
    return lax.dot_general(a, b, (dims, ((), ())), preferred_element_type=F32)


def round_order(rounds):
    return tuple(reversed(range(rounds)))


def attend_calls(rounds):
    order = round_order(rounds)
    return [order[:1], order[1:2], order[2:]] if rounds > 2 else [order]


def round_pairs(seq_count, head_count, i):
    rounds = seq_count // 2
    pairs = []
    for s in range(seq_count):
        for head in range(head_count):
            y, c = head // 2, head % 2
            k = rounds * c + (s % rounds ^ i)
            pairs.append((s * head_count + head, k * head_count + 2 * y + s // rounds))
    return pairs


def keep_in_hbm(array):
    return pltpu.with_memory_space_constraint(array, pltpu.HBM)


def pack_kernel(rounds, width, where_ref, *rest):
    ins, place_ref = rest[:4], rest[4]
    outs, place_out, sem, place_sem = rest[5:-3], rest[-3], rest[-2], rest[-1]
    turn = lax.rem(where_ref[0], rounds)
    copies = []
    for m in range(2):
        for i in range(rounds):
            col = pl.multiple_of((turn ^ i) * width, width)
            for n in range(2):
                copy = pltpu.make_async_copy(
                    ins[2 * m + n].at[0, :, pl.ds(col, width)],
                    outs[m * rounds + i].at[n],
                    sem.at[m * rounds + i, n],
                )
                copy.start()
                copies.append(copy)
    copy = pltpu.make_async_copy(place_ref, place_out, place_sem.at[0])
    copy.start()
    copies.append(copy)
    for copy in copies:
        copy.wait()


def pack(where, arrays, global_pos, rounds):
    _, tokens, columns = arrays[0].shape
    width = columns // rounds
    out = jax.ShapeDtypeStruct((2, tokens, width), BF16)
    outs = pl.pallas_call(
        functools.partial(pack_kernel, rounds, width),
        out_shape=[out] * (2 * rounds)
        + [jax.ShapeDtypeStruct((1, global_pos.shape[0]), jnp.int32)],
        in_specs=[SMEM] + [HBM] * 5,
        out_specs=[VMEM] * (2 * rounds + 1),
        scratch_shapes=[
            pltpu.SemaphoreType.DMA((2 * rounds, 2)),
            pltpu.SemaphoreType.DMA((1,)),
        ],
        compiler_params=PACK_PARAMS,
        cost_estimate=pl.CostEstimate(
            flops=0, transcendentals=0, bytes_accessed=16 * tokens * columns
        ),
        name="pack",
    )(where, *[keep_in_hbm(a) for a in arrays], keep_in_hbm(global_pos.reshape(1, -1)))
    return outs[:rounds], outs[rounds:-1], outs[-1]


def unpack_kernel(rounds, width, where_ref, *rest):
    ins, outs, sem = rest[:rounds], rest[rounds:-1], rest[-1]
    turn = lax.rem(where_ref[0], rounds)
    copies = []
    for i in range(rounds):
        col = pl.multiple_of((turn ^ i) * width, width)
        for n in range(2):
            copy = pltpu.make_async_copy(
                ins[i].at[n], outs[n].at[0, :, pl.ds(col, width)], sem.at[i, n]
            )
            copy.start()
            copies.append(copy)
    for copy in copies:
        copy.wait()


def unpack(where, parts):
    rounds = len(parts)
    _, tokens, width = parts[0].shape
    out = jax.ShapeDtypeStruct((1, tokens, rounds * width), BF16)
    return pl.pallas_call(
        functools.partial(unpack_kernel, rounds, width),
        out_shape=[out] * 2,
        in_specs=[SMEM] + [VMEM] * rounds,
        out_specs=[HBM] * 2,
        scratch_shapes=[pltpu.SemaphoreType.DMA((rounds, 2))],
        compiler_params=PARAMS,
        cost_estimate=pl.CostEstimate(
            flops=0, transcendentals=0, bytes_accessed=8 * rounds * tokens * width
        ),
        name="unpack",
    )(where, *parts)


def attend_kernel(
    rounds, run_blocks, picks, turns, opens, closes, where_ref, mine_ref, other_table_ref, *rest
):
    rest = list(rest)
    take = lambda n: [rest.pop(0) for _ in range(n)]
    count = len(turns)
    if opens:
        (global_ref,), parts = take(1), take(2 * rounds)
    else:
        all_ref, picked_ref, _ = take(3)
    sides = take(count)
    mixes = take(count)
    if opens:
        all_ref, picked_ref = take(2)
    (acc,) = take(1)
    if closes:
        (send_ref,) = take(1)
    (keep,) = take(1)

    k, h = where_ref[0], where_ref[1]
    tokens = run_blocks * BLOCK
    half = rounds * tokens
    total_blocks = 2 * rounds * run_blocks
    listed = (3 + picks) * BLOCK
    flip = (h * rounds + lax.rem(k, rounds)) * run_blocks
    head = lax.rem(k, rounds)
    mine = k // rounds == h
    scale = all_ref.shape[2] ** -0.5
    column = lax.broadcasted_iota(jnp.int32, (1, 4 * BLOCK), 1)

    if opens:
        shared = global_ref.shape[1]
        spots = jnp.broadcast_to(global_ref[...] ^ (flip * BLOCK), (shared, shared)).T[:, :1]
        sums = [None, None]
        for n in range(2 * rounds):
            ids = lax.broadcasted_iota(jnp.int32, (shared, tokens), 1) + n * tokens
            hot = jnp.where(ids == spots, 1.0, 0.0).astype(BF16)
            for m in range(2):
                part = parts[n][m]
                all_ref[m, n * tokens : (n + 1) * tokens] = part
                product = dot(hot, part, ((1,), (0,)))
                sums[m] = product if n == 0 else sums[m] + product
        for m in range(2):
            picked_ref[m] = sums[m].astype(BF16)
        acc[...] = jnp.zeros_like(acc)

    def begin(n, block):
        rows_of = slice(block * BLOCK, (block + 1) * BLOCK)
        query, grad = sides[n][0, rows_of], sides[n][1, rows_of]
        index = (turns[n] * run_blocks + block) ^ flip
        named = [
            jnp.maximum(index - 1, 0),
            index,
            jnp.minimum(index + 1, total_blocks - 1),
        ]
        for m in range(picks):
            named.append(
                jnp.where(mine, mine_ref[0, head, index, m], other_table_ref[0, head, index, m])
            )
        rows = [pl.multiple_of((b ^ flip) * BLOCK, BLOCK) for b in named]
        keys, values = [
            jnp.concatenate(
                [all_ref[m, pl.ds(r, BLOCK)] for r in rows] + [picked_ref[m]], axis=0
            )
            for m in range(2)
        ]
        scores = dot(query, keys, ((1,), (1,))) * scale
        probs = dot(grad, values, ((1,), (1,)))
        out = ((column < BLOCK) & (index == 0)) | (
            (column >= 2 * BLOCK) & (column < 3 * BLOCK) & (index == total_blocks - 1)
        )
        near = jnp.where(out, -1e30, scores[:, : 4 * BLOCK])
        scores = jnp.concatenate([near, scores[:, 4 * BLOCK :]], axis=1)
        return n, rows_of, rows, query, grad, keys, values, scores, probs

    def finish(state):
        weighed, scored = [], []
        for n, rows_of, rows, query, grad, keys, values, scores, probs in state:
            peak = jnp.max(scores, axis=1, keepdims=True)
            powers = jnp.exp(scores - peak)
            weights = powers * (1.0 / jnp.sum(powers, axis=1, keepdims=True))
            weighed.append((weights, weights.astype(BF16)))
        for (*_, probs), (weights, weights_b) in zip(state, weighed):
            delta = jnp.sum(weights_b.astype(F32) * probs, axis=1, keepdims=True)
            scored.append((weights * (probs - delta)).astype(BF16))
        for (n, rows_of, rows, query, grad, keys, values, _, _), (_, weights_b), dscore_b in zip(
            state, weighed, scored
        ):
            mixed = dot(weights_b, values, ((1,), (0,)))
            grad_query = dot(dscore_b, keys, ((1,), (0,))) * scale
            mixes[n][0, rows_of] = mixed.astype(BF16)
            mixes[n][1, rows_of] = grad_query.astype(BF16)
            keep[n, 0, rows_of] = dscore_b[:, listed:]
            keep[n, 1, rows_of] = weights_b[:, listed:]
            key_part = dot(dscore_b[:, :listed], query, ((0,), (0,)))
            value_part = dot(weights_b[:, :listed], grad, ((0,), (0,)))
            for m, r in enumerate(rows):
                span = slice(m * BLOCK, (m + 1) * BLOCK)
                acc[0, pl.ds(r, BLOCK)] += key_part[span]
                acc[1, pl.ds(r, BLOCK)] += value_part[span]

    held = None
    for n in range(count):
        for block in range(0, run_blocks, CHUNK):
            state = [begin(n, b) for b in range(block, block + CHUNK)]
            if held is not None:
                finish(held)
            held = state
    finish(held)
    for m in range(2):
        shared = acc[m, 2 * half :]
        for n in range(count):
            shared = shared + dot(keep[n, m], sides[n][m], ((0,), (0,)))
        acc[m, 2 * half :] = shared
        if closes:
            send_ref[m, :half] = acc[m, half : 2 * half]
            send_ref[m, half:] = shared


def attend(where, tables, places, parts, state, sides, turns, rounds, picks, closes):
    opens = state is None
    _, tokens, width = sides[0].shape
    run_blocks = tokens // BLOCK
    shared = places.shape[1]
    entries = (3 + picks) * BLOCK + shared
    count = len(turns)
    half = rounds * tokens
    one = jax.ShapeDtypeStruct((2, tokens, width), BF16)
    acc = jax.ShapeDtypeStruct((2, 2 * half + shared, width), F32)
    out_shape = [one] * count
    if opens:
        given = [places, *parts]
        out_shape += [
            jax.ShapeDtypeStruct((2, 2 * half, width), BF16),
            jax.ShapeDtypeStruct((2, shared, width), BF16),
        ]
        aliases = {}
    else:
        given = list(state)
        aliases = {3 + len(given) - 1: count}
    out_shape += [acc]
    if closes:
        out_shape += [jax.ShapeDtypeStruct((2, half + shared, width), F32)]
    outs = pl.pallas_call(
        functools.partial(
            attend_kernel, rounds, run_blocks, picks, turns, opens, closes
        ),
        out_shape=out_shape,
        in_specs=[SMEM] * 3 + [VMEM] * (len(given) + count),
        out_specs=[VMEM] * len(out_shape),
        input_output_aliases=aliases,
        scratch_shapes=[pltpu.VMEM((count, 2, tokens, shared), BF16)],
        compiler_params=PARAMS,
        cost_estimate=pl.CostEstimate(
            flops=12 * count * tokens * entries * width,
            transcendentals=count * tokens * entries,
            bytes_accessed=12 * half * width,
        ),
        name="attend",
    )(where, *tables, *given, *sides)
    return outs[:count], outs[count:]


def total_kernel(rounds, where_ref, global_ref, acc_ref, came_ref, *outs):
    tokens, width = outs[0].shape[1:]
    half = rounds * tokens
    count = global_ref.shape[1]
    scale = width**-0.5
    flip = (where_ref[1] * rounds + lax.rem(where_ref[0], rounds)) * tokens
    spots = global_ref[...] ^ flip
    halves = []
    for n in range(2):
        shared = acc_ref[n, 2 * half :] + came_ref[n, half:]
        high = shared.astype(BF16)
        halves += [high, (shared - high.astype(F32)).astype(BF16)]
    halves = jnp.concatenate(halves, axis=1)
    for i in range(rounds):
        ids = lax.broadcasted_iota(jnp.int32, (tokens, count), 0) + i * tokens
        hot = jnp.where(ids == spots, 1.0, 0.0).astype(BF16)
        spread = dot(hot, halves, ((1,), (0,)))
        mine = slice(i * tokens, (i + 1) * tokens)
        for n in range(2):
            whole = acc_ref[n, mine] + came_ref[n, mine]
            whole = whole + spread[:, 2 * n * width : (2 * n + 1) * width]
            whole = whole + spread[:, (2 * n + 1) * width : (2 * n + 2) * width]
            if n == 0:
                whole = whole * scale
            outs[i][n] = whole.astype(BF16)


def total(where, places, acc, came, rounds):
    rows, width = came.shape[1:]
    count = places.shape[1]
    tokens = (rows - count) // rounds
    return pl.pallas_call(
        functools.partial(total_kernel, rounds),
        out_shape=[jax.ShapeDtypeStruct((2, tokens, width), BF16)] * rounds,
        in_specs=[SMEM] + [VMEM] * 3,
        out_specs=[VMEM] * rounds,
        compiler_params=PARAMS,
        cost_estimate=pl.CostEstimate(
            flops=4 * rows * width, transcendentals=0, bytes_accessed=20 * rows * width
        ),
        name="total",
    )(where, places, acc, came)


def by_heads(query_rows, key_rows, value_rows, grad_out, rand_blocks, global_pos):
    seq_count, head_count = lax.axis_size("seq"), lax.axis_size("head")
    _, rounds, _, picks = rand_blocks.shape
    k, head_index = lax.axis_index("seq"), lax.axis_index("head")
    where = jnp.stack([k, head_index & 1]).astype(jnp.int32)
    sibling = [(i, i ^ 1) for i in range(head_count)]
    trades = [round_pairs(seq_count, head_count, i) for i in range(rounds)]

    order = round_order(rounds)

    def send(parts, turns=order):
        out = {}
        for n in turns:
            out[n] = lax.ppermute(parts[n], AXES, trades[n])
        return out

    def swap(parts):
        out = []
        for part in parts:
            out.append(lax.ppermute(part, "head", sibling))
        return out

    arrays = [key_rows, value_rows, query_rows, grad_out]
    kv, sides, places = pack(where, arrays, global_pos, rounds)
    kv = send(kv)
    sides = send(sides)
    tables = [rand_blocks, *swap([rand_blocks])]
    parts = [kv[n] for n in range(rounds)]
    parts += swap(parts)
    mixes, state = {}, None
    calls = attend_calls(rounds)
    for n, turns in enumerate(calls):
        mix, new = attend(
            where,
            tables,
            places,
            parts,
            state,
            [sides[t] for t in turns],
            turns,
            rounds,
            picks,
            n == len(calls) - 1,
        )
        mixes.update(send(dict(zip(turns, mix)), turns))
        state = new if state is None else (*state[:2], *new)
    _, _, acc, leaving = state
    (came,) = swap([leaving])
    grads = total(where, places, acc, came, rounds)
    grads = send(grads)
    attended, grad_query = unpack(where, [mixes[n] for n in range(rounds)])
    grad_key, grad_value = unpack(where, [grads[n] for n in range(rounds)])
    return attended, grad_query, grad_key, grad_value


def extended_2(value, sides, width):
    for axis, dim in sides:
        size, length = (lax.axis_size(axis), value.shape[dim])
        up = [(i, (i + 1) % size) for i in range(size - 1)]
        down = [(j, i) for i, j in up]
        last = lax.slice_in_dim(value, length - width, length, axis=dim)
        first = lax.slice_in_dim(value, 0, width, axis=dim)
        before = lax.ppermute(last, axis, up)
        after = lax.ppermute(first, axis, down)
        value = jnp.concatenate([before, value, after], axis=dim)
    return value


def by_blocks(query_rows, key_rows, value_rows, grad_out, rand_blocks, global_pos):
    batch_count, tok_local, columns = query_rows.shape
    seq_count = lax.axis_size("seq")
    seq_index = lax.axis_index("seq")
    heads_local = rand_blocks.shape[1]
    total_blocks = rand_blocks.shape[2]
    pick_count = rand_blocks.shape[3]
    head_dim = columns // heads_local
    blocks_local = tok_local // BLOCK
    score_scale = head_dim ** (-0.5)
    slot_count = batch_count * heads_local * blocks_local * pick_count
    capacity = (slot_count + seq_count - 1) // seq_count
    buffer_rows = seq_count * capacity
    f32 = jnp.float32
    bf16 = jnp.bfloat16

    def to_blocks(array):
        return array.reshape(batch_count, blocks_local, BLOCK, heads_local, head_dim).transpose(
            0, 3, 1, 2, 4
        )

    def from_blocks(array):
        return array.transpose(0, 2, 3, 1, 4).reshape(batch_count, tok_local, columns)

    def pair_blocks(array):
        return array.reshape(2, batch_count, blocks_local, BLOCK, heads_local, head_dim).transpose(
            0, 1, 4, 2, 3, 5
        )

    def global_sum(array):
        return lax.psum(array, "seq")

    key_value = jnp.stack([key_rows, value_rows])
    edge_rows = jnp.concatenate([key_value[:, :, :BLOCK], key_value[:, :, -BLOCK:]], axis=2)
    extended = extended_2(edge_rows, (("seq", 2),), BLOCK)
    padded = jnp.concatenate([extended[:, :, :BLOCK], key_value, extended[:, :, -BLOCK:]], axis=2)

    def shifted(start):
        return pair_blocks(padded[:, :, start : start + tok_local])

    window_lists = jnp.concatenate([shifted(0), shifted(BLOCK), shifted(2 * BLOCK)], axis=4)
    my_table = lax.dynamic_slice_in_dim(
        rand_blocks, seq_index * blocks_local, blocks_local, 2
    ).reshape(slot_count)
    holder = my_table // blocks_local
    holder_hot = (holder[:, None] == jnp.arange(seq_count)[None, :]).astype(jnp.int32)
    holder_rank = jnp.sum((jnp.cumsum(holder_hot, axis=0) - 1) * holder_hot, axis=1)
    position = holder * capacity + holder_rank
    requests = rand_blocks.reshape(batch_count, heads_local, seq_count, blocks_local, pick_count)
    requests = requests.transpose(2, 0, 1, 3, 4).reshape(seq_count, slot_count)
    wanted = (requests // blocks_local == seq_index).astype(jnp.int32)
    wanted_rank = jnp.cumsum(wanted, axis=1) - 1
    chosen = wanted[:, None, :] * (
        wanted_rank[:, None, :] == jnp.arange(capacity)[None, :, None]
    ).astype(jnp.int32)
    slot_live = (jnp.sum(chosen, axis=2) > 0).reshape(buffer_rows)
    slot_index = jnp.sum(chosen * jnp.arange(slot_count)[None, None, :], axis=2)
    which_batch = slot_index // (heads_local * blocks_local * pick_count)
    which_head = slot_index // (blocks_local * pick_count) % heads_local
    which_block = jnp.take_along_axis(requests, slot_index, axis=1) % blocks_local
    stacked = key_value.reshape(
        2, batch_count, blocks_local, BLOCK, heads_local, head_dim
    ).transpose(1, 2, 4, 0, 3, 5)
    outgoing = stacked[which_batch, which_block, which_head].reshape(
        buffer_rows, 2, BLOCK, head_dim
    )
    incoming = lax.all_to_all(outgoing, "seq", split_axis=0, concat_axis=0, tiled=True)
    fetched = incoming[position].reshape(
        batch_count, heads_local, blocks_local, pick_count, 2, BLOCK, head_dim
    )
    fetched = fetched.transpose(4, 0, 1, 2, 3, 5, 6).reshape(
        2, batch_count, heads_local, blocks_local, pick_count * BLOCK, head_dim
    )
    local_pos = global_pos - seq_index * tok_local
    pick_hot = (local_pos[:, None] == jnp.arange(tok_local)[None, :]).astype(bf16)
    owned_rows = jnp.einsum("gt,pbtc->pbgc", pick_hot, key_value, preferred_element_type=f32)
    shared = global_sum(owned_rows).astype(bf16)
    globals_count = shared.shape[2]
    global_kv = shared.reshape(2, batch_count, globals_count, heads_local, head_dim).transpose(
        0, 1, 3, 2, 4
    )
    global_kv = jnp.broadcast_to(
        global_kv[:, :, :, None],
        (2, batch_count, heads_local, blocks_local, globals_count, head_dim),
    )
    lists_all = jnp.concatenate([window_lists, fetched, global_kv], axis=4)
    key_lists = lists_all[0]
    value_lists = lists_all[1]
    key_count = key_lists.shape[3]
    block_ids = seq_index * blocks_local + jnp.arange(blocks_local)
    column_ids = jnp.arange(key_count)[None, :]
    middle_ok = jnp.where(
        (column_ids >= 2 * BLOCK) & (column_ids < 3 * BLOCK),
        (block_ids < total_blocks - 1)[:, None],
        True,
    )
    valid_mask = jnp.where(column_ids < BLOCK, (block_ids > 0)[:, None], middle_ok)
    query_blocks = to_blocks(query_rows)
    grad_blocks = to_blocks(grad_out)
    scores = (
        jnp.einsum("bhjqd,bhjkd->bhjqk", query_blocks, key_lists, preferred_element_type=f32)
        * score_scale
    )
    scores = jnp.where(valid_mask[None, None, :, None, :], scores, -1e30)
    row_max = jnp.max(scores, axis=-1, keepdims=True)
    log_total = row_max + jnp.log(jnp.sum(jnp.exp(scores - row_max), axis=-1, keepdims=True))
    weights = jnp.exp(scores - log_total)
    weights_b = weights.astype(bf16)
    mixed_rows = jnp.einsum(
        "bhjqk,bhjkd->bhjqd", weights_b, value_lists, preferred_element_type=f32
    )
    attended = from_blocks(mixed_rows.astype(bf16))
    row_delta = jnp.sum(grad_blocks.astype(f32) * mixed_rows, axis=-1, keepdims=True)
    grad_probs = jnp.einsum(
        "bhjqd,bhjkd->bhjqk", grad_blocks, value_lists, preferred_element_type=f32
    )
    dscore_b = (weights * (grad_probs - row_delta)).astype(bf16)
    grad_query = (
        jnp.einsum("bhjqk,bhjkd->bhjqd", dscore_b, key_lists, preferred_element_type=f32)
        * score_scale
    )

    def key_grads(lower, upper):
        key_part = (
            jnp.einsum(
                "bhjqk,bhjqd->bhjkd",
                dscore_b[..., lower:upper],
                query_blocks,
                preferred_element_type=f32,
            )
            * score_scale
        )
        value_part = jnp.einsum(
            "bhjqk,bhjqd->bhjkd",
            weights_b[..., lower:upper],
            grad_blocks,
            preferred_element_type=f32,
        )
        return jnp.stack([key_part, value_part])

    window_cols = 3 * BLOCK
    random_cols = pick_count * BLOCK
    window_grads = key_grads(0, window_cols).reshape(
        2, batch_count, heads_local, blocks_local, 3, BLOCK, head_dim
    )
    padded_grads = jnp.pad(
        window_grads[:, :, :, :, 0], ((0, 0), (0, 0), (0, 0), (0, 2), (0, 0), (0, 0))
    )
    padded_grads = padded_grads + jnp.pad(
        window_grads[:, :, :, :, 1], ((0, 0), (0, 0), (0, 0), (1, 1), (0, 0), (0, 0))
    )
    padded_grads = padded_grads + jnp.pad(
        window_grads[:, :, :, :, 2], ((0, 0), (0, 0), (0, 0), (2, 0), (0, 0), (0, 0))
    )
    own_grads = padded_grads[:, :, :, 1:-1]
    rim_grads = jnp.stack([padded_grads[:, :, :, 0], padded_grads[:, :, :, -1]], axis=3)
    returned = extended_2(rim_grads.astype(jnp.bfloat16), (("seq", 3),), 1).astype(rim_grads.dtype)
    own_grads = own_grads.at[:, :, :, 0].add(returned[:, :, :, 0])
    own_grads = own_grads.at[:, :, :, -1].add(returned[:, :, :, 3])
    global_grads = jnp.sum(key_grads(window_cols + random_cols, key_count), axis=3)
    global_grads = global_grads.transpose(0, 1, 3, 2, 4).reshape(
        2, batch_count, globals_count, columns
    )
    global_summed = global_sum(global_grads)
    inside = (local_pos >= 0) & (local_pos < tok_local)
    safe_pos = jnp.where(inside, local_pos, tok_local)
    global_local = (
        jnp.zeros((2, batch_count, tok_local, columns), f32)
        .at[:, :, safe_pos]
        .add(global_summed, mode="drop")
    )
    global_part = pair_blocks(global_local)
    target = ((which_batch * blocks_local + which_block) * heads_local + which_head).reshape(
        buffer_rows
    )
    random_grads = key_grads(window_cols, window_cols + random_cols)
    per_slot = random_grads.reshape(
        2, batch_count, heads_local, blocks_local, pick_count, BLOCK, head_dim
    )
    per_slot = per_slot.transpose(1, 2, 3, 4, 0, 5, 6).reshape(slot_count, 2, BLOCK, head_dim)
    sending = jnp.zeros((buffer_rows, 2, BLOCK, head_dim), f32).at[position].set(per_slot)
    arrived = lax.all_to_all(
        sending.astype(jnp.bfloat16), "seq", split_axis=0, concat_axis=0, tiled=True
    ).astype(sending.dtype)
    kept = jnp.where(slot_live[:, None, None, None], arrived, 0.0)
    summed = (
        jnp.zeros((batch_count * blocks_local * heads_local, 2, BLOCK, head_dim), f32)
        .at[target]
        .add(kept)
    )
    random_part = summed.reshape(
        batch_count, blocks_local, heads_local, 2, BLOCK, head_dim
    ).transpose(3, 0, 2, 1, 4, 5)
    total_grads = own_grads + random_part + global_part
    grad_key = from_blocks(total_grads[0].astype(bf16))
    grad_value = from_blocks(total_grads[1].astype(bf16))
    return (attended, from_blocks(grad_query.astype(bf16)), grad_key, grad_value)


def body(query_rows, key_rows, value_rows, grad_out, rand_blocks, global_pos):
    seq_count, head_count = lax.axis_size("seq"), lax.axis_size("head")
    batch_count, heads_local = rand_blocks.shape[:2]
    tokens = query_rows.shape[1]
    whole_heads = seq_count == 2 * heads_local and heads_local & (heads_local - 1) == 0
    whole_heads = whole_heads and heads_local > 1 and tokens & (tokens - 1) == 0
    whole_heads = whole_heads and head_count % 2 == 0 and batch_count == 1
    form = by_heads if whole_heads else by_blocks
    return form(query_rows, key_rows, value_rows, grad_out, rand_blocks, global_pos)


def solution(mesh):
    return jax.shard_map(
        body,
        mesh=mesh,
        in_specs=(
            P(None, "seq", "head"),
            P(None, "seq", "head"),
            P(None, "seq", "head"),
            P(None, "seq", "head"),
            P(None, "head", None, None),
            P(),
        ),
        out_specs=(
            P(None, "seq", "head"),
            P(None, "seq", "head"),
            P(None, "seq", "head"),
            P(None, "seq", "head"),
        ),
        check_vma=False,
    )
```

```python
import functools

import jax
import jax.numpy as jnp
from jax import lax
from jax.experimental import pallas as pl
from jax.experimental.pallas import tpu as pltpu
from jax.sharding import PartitionSpec as P


BLOCK = 64
AXES = ("seq", "head")
CHUNK = 4
GRANT = 24 * 1024 * 1024
VMEM = pl.BlockSpec(memory_space=pltpu.VMEM)
SMEM = pl.BlockSpec(memory_space=pltpu.SMEM)
PARAMS = pltpu.CompilerParams(vmem_limit_bytes=GRANT)
PACK_PARAMS = pltpu.CompilerParams(vmem_limit_bytes=GRANT)
HBM = pl.BlockSpec(memory_space=pltpu.HBM)
F32 = jnp.float32
BF16 = jnp.bfloat16


def dot(a, b, dims):
    return lax.dot_general(a, b, (dims, ((), ())), preferred_element_type=F32)


def round_order(rounds):
    return tuple(reversed(range(rounds)))


def attend_calls(rounds):
    order = round_order(rounds)
    return [order[: rounds // 2], order[rounds // 2 :]]


def round_pairs(seq_count, head_count, i):
    rounds = seq_count // 2
    pairs = []
    for s in range(seq_count):
        for head in range(head_count):
            y, c = head // 2, head % 2
            k = rounds * c + (s % rounds ^ i)
            pairs.append((s * head_count + head, k * head_count + 2 * y + s // rounds))
    return pairs


def keep_in_hbm(array):
    return pltpu.with_memory_space_constraint(array, pltpu.HBM)


def pack_kernel(rounds, width, where_ref, *rest):
    ins, place_ref = rest[:4], rest[4]
    outs, place_out, sem, place_sem = rest[5:-3], rest[-3], rest[-2], rest[-1]
    turn = lax.rem(where_ref[0], rounds)
    copies = []
    for m in range(2):
        for i in range(rounds):
            col = pl.multiple_of((turn ^ i) * width, width)
            for n in range(2):
                copy = pltpu.make_async_copy(
                    ins[2 * m + n].at[0, :, pl.ds(col, width)],
                    outs[m * rounds + i].at[n],
                    sem.at[m * rounds + i, n],
                )
                copy.start()
                copies.append(copy)
    copy = pltpu.make_async_copy(place_ref, place_out, place_sem.at[0])
    copy.start()
    copies.append(copy)
    for copy in copies:
        copy.wait()


def pack(where, arrays, global_pos, rounds):
    _, tokens, columns = arrays[0].shape
    width = columns // rounds
    out = jax.ShapeDtypeStruct((2, tokens, width), BF16)
    outs = pl.pallas_call(
        functools.partial(pack_kernel, rounds, width),
        out_shape=[out] * (2 * rounds)
        + [jax.ShapeDtypeStruct((1, global_pos.shape[0]), jnp.int32)],
        in_specs=[SMEM] + [HBM] * 5,
        out_specs=[VMEM] * (2 * rounds + 1),
        scratch_shapes=[
            pltpu.SemaphoreType.DMA((2 * rounds, 2)),
            pltpu.SemaphoreType.DMA((1,)),
        ],
        compiler_params=PACK_PARAMS,
        cost_estimate=pl.CostEstimate(
            flops=0, transcendentals=0, bytes_accessed=16 * tokens * columns
        ),
        name="pack",
    )(where, *[keep_in_hbm(a) for a in arrays], keep_in_hbm(global_pos.reshape(1, -1)))
    return outs[:rounds], outs[rounds:-1], outs[-1]


def unpack_kernel(rounds, width, where_ref, *rest):
    ins, outs, sem = rest[:rounds], rest[rounds:-1], rest[-1]
    turn = lax.rem(where_ref[0], rounds)
    copies = []
    for i in range(rounds):
        col = pl.multiple_of((turn ^ i) * width, width)
        for n in range(2):
            copy = pltpu.make_async_copy(
                ins[i].at[n], outs[n].at[0, :, pl.ds(col, width)], sem.at[i, n]
            )
            copy.start()
            copies.append(copy)
    for copy in copies:
        copy.wait()


def unpack(where, parts):
    rounds = len(parts)
    _, tokens, width = parts[0].shape
    out = jax.ShapeDtypeStruct((1, tokens, rounds * width), BF16)
    return pl.pallas_call(
        functools.partial(unpack_kernel, rounds, width),
        out_shape=[out] * 2,
        in_specs=[SMEM] + [VMEM] * rounds,
        out_specs=[HBM] * 2,
        scratch_shapes=[pltpu.SemaphoreType.DMA((rounds, 2))],
        compiler_params=PARAMS,
        cost_estimate=pl.CostEstimate(
            flops=0, transcendentals=0, bytes_accessed=8 * rounds * tokens * width
        ),
        name="unpack",
    )(where, *parts)


def attend_kernel(
    rounds, run_blocks, picks, turns, opens, closes, where_ref, mine_ref, other_table_ref, *rest
):
    rest = list(rest)
    take = lambda n: [rest.pop(0) for _ in range(n)]
    count = len(turns)
    if opens:
        (global_ref,), parts = take(1), take(2 * rounds)
    else:
        all_ref, picked_ref, _ = take(3)
    sides = take(count)
    mixes = take(count)
    if opens:
        all_ref, picked_ref = take(2)
    (acc,) = take(1)
    if closes:
        (send_ref,) = take(1)
    (keep,) = take(1)

    k, h = where_ref[0], where_ref[1]
    tokens = run_blocks * BLOCK
    half = rounds * tokens
    total_blocks = 2 * rounds * run_blocks
    listed = (3 + picks) * BLOCK
    flip = (h * rounds + lax.rem(k, rounds)) * run_blocks
    head = lax.rem(k, rounds) * (total_blocks * picks)
    mine = k // rounds == h
    scale = all_ref.shape[2] ** -0.5
    column = lax.broadcasted_iota(jnp.int32, (1, 4 * BLOCK), 1)

    if opens:
        shared = global_ref.shape[1]
        spots = jnp.broadcast_to(global_ref[...] ^ (flip * BLOCK), (shared, shared)).T[:, :1]
        sums = [None, None]
        for n in range(2 * rounds):
            ids = lax.broadcasted_iota(jnp.int32, (shared, tokens), 1) + n * tokens
            hot = jnp.where(ids == spots, 1.0, 0.0).astype(BF16)
            for m in range(2):
                part = parts[n][m]
                all_ref[m, n * tokens : (n + 1) * tokens] = part
                product = dot(hot, part, ((1,), (0,)))
                sums[m] = product if n == 0 else sums[m] + product
        for m in range(2):
            picked_ref[m] = sums[m].astype(BF16)
        acc[...] = jnp.zeros_like(acc)

    def begin(n, block):
        rows_of = slice(block * BLOCK, (block + 1) * BLOCK)
        query, grad = sides[n][0, rows_of], sides[n][1, rows_of]
        index = (turns[n] * run_blocks + block) ^ flip
        named = [
            jnp.maximum(index - 1, 0),
            index,
            jnp.minimum(index + 1, total_blocks - 1),
        ]
        for m in range(picks):
            at = head + index * picks + m
            named.append(jnp.where(mine, mine_ref[at], other_table_ref[at]))
        rows = [pl.multiple_of((b ^ flip) * BLOCK, BLOCK) for b in named]
        keys, values = [
            jnp.concatenate(
                [all_ref[m, pl.ds(r, BLOCK)] for r in rows] + [picked_ref[m]], axis=0
            )
            for m in range(2)
        ]
        scores = dot(query, keys, ((1,), (1,))) * scale
        probs = dot(grad, values, ((1,), (1,)))
        out = ((column < BLOCK) & (index == 0)) | (
            (column >= 2 * BLOCK) & (column < 3 * BLOCK) & (index == total_blocks - 1)
        )
        near = jnp.where(out, -1e30, scores[:, : 4 * BLOCK])
        scores = jnp.concatenate([near, scores[:, 4 * BLOCK :]], axis=1)
        return n, rows_of, rows, query, grad, keys, values, scores, probs

    def finish(state):
        weighed, scored = [], []
        for n, rows_of, rows, query, grad, keys, values, scores, probs in state:
            peak = jnp.max(scores, axis=1, keepdims=True)
            powers = jnp.exp(scores - peak)
            weights = powers * (1.0 / jnp.sum(powers, axis=1, keepdims=True))
            weighed.append((weights, weights.astype(BF16)))
        for (*_, probs), (weights, weights_b) in zip(state, weighed):
            delta = jnp.sum(weights_b.astype(F32) * probs, axis=1, keepdims=True)
            scored.append((weights * (probs - delta)).astype(BF16))
        for (n, rows_of, rows, query, grad, keys, values, _, _), (_, weights_b), dscore_b in zip(
            state, weighed, scored
        ):
            mixed = dot(weights_b, values, ((1,), (0,)))
            grad_query = dot(dscore_b, keys, ((1,), (0,))) * scale
            mixes[n][0, rows_of] = mixed.astype(BF16)
            mixes[n][1, rows_of] = grad_query.astype(BF16)
            keep[n, 0, rows_of] = dscore_b[:, listed:]
            keep[n, 1, rows_of] = weights_b[:, listed:]
            key_part = dot(dscore_b[:, :listed], query, ((0,), (0,)))
            value_part = dot(weights_b[:, :listed], grad, ((0,), (0,)))
            for m, r in enumerate(rows):
                span = slice(m * BLOCK, (m + 1) * BLOCK)
                acc[0, pl.ds(r, BLOCK)] += key_part[span]
                acc[1, pl.ds(r, BLOCK)] += value_part[span]

    held = None
    for n in range(count):
        for block in range(0, run_blocks, CHUNK):
            state = [begin(n, b) for b in range(block, block + CHUNK)]
            if held is not None:
                finish(held)
            held = state
    finish(held)
    for m in range(2):
        shared = acc[m, 2 * half :]
        for n in range(count):
            shared = shared + dot(keep[n, m], sides[n][m], ((0,), (0,)))
        acc[m, 2 * half :] = shared
        if closes:
            send_ref[m, :half] = acc[m, half : 2 * half]
            send_ref[m, half:] = shared


def attend(where, tables, places, parts, state, sides, turns, rounds, picks, closes):
    opens = state is None
    _, tokens, width = sides[0].shape
    run_blocks = tokens // BLOCK
    shared = places.shape[1]
    entries = (3 + picks) * BLOCK + shared
    count = len(turns)
    half = rounds * tokens
    one = jax.ShapeDtypeStruct((2, tokens, width), BF16)
    acc = jax.ShapeDtypeStruct((2, 2 * half + shared, width), F32)
    out_shape = [one] * count
    if opens:
        given = [places, *parts]
        out_shape += [
            jax.ShapeDtypeStruct((2, 2 * half, width), BF16),
            jax.ShapeDtypeStruct((2, shared, width), BF16),
        ]
        aliases = {}
    else:
        given = list(state)
        aliases = {3 + len(given) - 1: count}
    out_shape += [acc]
    if closes:
        out_shape += [jax.ShapeDtypeStruct((2, half + shared, width), F32)]
    outs = pl.pallas_call(
        functools.partial(
            attend_kernel, rounds, run_blocks, picks, turns, opens, closes
        ),
        out_shape=out_shape,
        in_specs=[SMEM] * 3 + [VMEM] * (len(given) + count),
        out_specs=[VMEM] * len(out_shape),
        input_output_aliases=aliases,
        scratch_shapes=[pltpu.VMEM((count, 2, tokens, shared), BF16)],
        compiler_params=PARAMS,
        cost_estimate=pl.CostEstimate(
            flops=12 * count * tokens * entries * width,
            transcendentals=count * tokens * entries,
            bytes_accessed=12 * half * width,
        ),
        name="attend",
    )(where, *tables, *given, *sides)
    return outs[:count], outs[count:]


def total_kernel(rounds, where_ref, global_ref, acc_ref, came_ref, *outs):
    tokens, width = outs[0].shape[1:]
    half = rounds * tokens
    count = global_ref.shape[1]
    scale = width**-0.5
    flip = (where_ref[1] * rounds + lax.rem(where_ref[0], rounds)) * tokens
    spots = global_ref[...] ^ flip
    halves = []
    for n in range(2):
        shared = acc_ref[n, 2 * half :] + came_ref[n, half:]
        high = shared.astype(BF16)
        halves += [high, (shared - high.astype(F32)).astype(BF16)]
    halves = jnp.concatenate(halves, axis=1)
    for i in range(rounds):
        ids = lax.broadcasted_iota(jnp.int32, (tokens, count), 0) + i * tokens
        hot = jnp.where(ids == spots, 1.0, 0.0).astype(BF16)
        spread = dot(hot, halves, ((1,), (0,)))
        mine = slice(i * tokens, (i + 1) * tokens)
        for n in range(2):
            whole = acc_ref[n, mine] + came_ref[n, mine]
            whole = whole + spread[:, 2 * n * width : (2 * n + 1) * width]
            whole = whole + spread[:, (2 * n + 1) * width : (2 * n + 2) * width]
            if n == 0:
                whole = whole * scale
            outs[i][n] = whole.astype(BF16)


def total(where, places, acc, came, rounds):
    rows, width = came.shape[1:]
    count = places.shape[1]
    tokens = (rows - count) // rounds
    return pl.pallas_call(
        functools.partial(total_kernel, rounds),
        out_shape=[jax.ShapeDtypeStruct((2, tokens, width), BF16)] * rounds,
        in_specs=[SMEM] + [VMEM] * 3,
        out_specs=[VMEM] * rounds,
        compiler_params=PARAMS,
        cost_estimate=pl.CostEstimate(
            flops=4 * rows * width, transcendentals=0, bytes_accessed=20 * rows * width
        ),
        name="total",
    )(where, places, acc, came)


def by_heads(query_rows, key_rows, value_rows, grad_out, rand_blocks, global_pos):
    seq_count, head_count = lax.axis_size("seq"), lax.axis_size("head")
    _, rounds, _, picks = rand_blocks.shape
    k, head_index = lax.axis_index("seq"), lax.axis_index("head")
    where = jnp.stack([k, head_index & 1]).astype(jnp.int32)
    sibling = [(i, i ^ 1) for i in range(head_count)]
    trades = [round_pairs(seq_count, head_count, i) for i in range(rounds)]

    order = round_order(rounds)

    def send(parts, turns=order):
        out = {}
        for n in turns:
            out[n] = lax.ppermute(parts[n], AXES, trades[n])
        return out

    def swap(parts):
        out = []
        for part in parts:
            out.append(lax.ppermute(part, "head", sibling))
        return out

    arrays = [key_rows, value_rows, query_rows, grad_out]
    kv, sides, places = pack(where, arrays, global_pos, rounds)
    kv = send(kv)
    sides = send(sides)
    table = rand_blocks.reshape(rand_blocks.size)
    tables = [table, *swap([table])]
    parts = [kv[n] for n in range(rounds)]
    parts += swap(parts)
    mixes, state = {}, None
    calls = attend_calls(rounds)
    for n, turns in enumerate(calls):
        mix, new = attend(
            where,
            tables,
            places,
            parts,
            state,
            [sides[t] for t in turns],
            turns,
            rounds,
            picks,
            n == len(calls) - 1,
        )
        mixes.update(send(dict(zip(turns, mix)), turns))
        state = new if state is None else (*state[:2], *new)
    _, _, acc, leaving = state
    (came,) = swap([leaving])
    grads = total(where, places, acc, came, rounds)
    grads = send(grads)
    attended, grad_query = unpack(where, [mixes[n] for n in range(rounds)])
    grad_key, grad_value = unpack(where, [grads[n] for n in range(rounds)])
    return attended, grad_query, grad_key, grad_value


def extended_2(value, sides, width):
    for axis, dim in sides:
        size, length = (lax.axis_size(axis), value.shape[dim])
        up = [(i, (i + 1) % size) for i in range(size - 1)]
        down = [(j, i) for i, j in up]
        last = lax.slice_in_dim(value, length - width, length, axis=dim)
        first = lax.slice_in_dim(value, 0, width, axis=dim)
        before = lax.ppermute(last, axis, up)
        after = lax.ppermute(first, axis, down)
        value = jnp.concatenate([before, value, after], axis=dim)
    return value


def by_blocks(query_rows, key_rows, value_rows, grad_out, rand_blocks, global_pos):
    batch_count, tok_local, columns = query_rows.shape
    seq_count = lax.axis_size("seq")
    seq_index = lax.axis_index("seq")
    heads_local = rand_blocks.shape[1]
    total_blocks = rand_blocks.shape[2]
    pick_count = rand_blocks.shape[3]
    head_dim = columns // heads_local
    blocks_local = tok_local // BLOCK
    score_scale = head_dim ** (-0.5)
    slot_count = batch_count * heads_local * blocks_local * pick_count
    capacity = (slot_count + seq_count - 1) // seq_count
    buffer_rows = seq_count * capacity
    f32 = jnp.float32
    bf16 = jnp.bfloat16

    def to_blocks(array):
        return array.reshape(batch_count, blocks_local, BLOCK, heads_local, head_dim).transpose(
            0, 3, 1, 2, 4
        )

    def from_blocks(array):
        return array.transpose(0, 2, 3, 1, 4).reshape(batch_count, tok_local, columns)

    def pair_blocks(array):
        return array.reshape(2, batch_count, blocks_local, BLOCK, heads_local, head_dim).transpose(
            0, 1, 4, 2, 3, 5
        )

    def global_sum(array):
        return lax.psum(array, "seq")

    key_value = jnp.stack([key_rows, value_rows])
    edge_rows = jnp.concatenate([key_value[:, :, :BLOCK], key_value[:, :, -BLOCK:]], axis=2)
    extended = extended_2(edge_rows, (("seq", 2),), BLOCK)
    padded = jnp.concatenate([extended[:, :, :BLOCK], key_value, extended[:, :, -BLOCK:]], axis=2)

    def shifted(start):
        return pair_blocks(padded[:, :, start : start + tok_local])

    window_lists = jnp.concatenate([shifted(0), shifted(BLOCK), shifted(2 * BLOCK)], axis=4)
    my_table = lax.dynamic_slice_in_dim(
        rand_blocks, seq_index * blocks_local, blocks_local, 2
    ).reshape(slot_count)
    holder = my_table // blocks_local
    holder_hot = (holder[:, None] == jnp.arange(seq_count)[None, :]).astype(jnp.int32)
    holder_rank = jnp.sum((jnp.cumsum(holder_hot, axis=0) - 1) * holder_hot, axis=1)
    position = holder * capacity + holder_rank
    requests = rand_blocks.reshape(batch_count, heads_local, seq_count, blocks_local, pick_count)
    requests = requests.transpose(2, 0, 1, 3, 4).reshape(seq_count, slot_count)
    wanted = (requests // blocks_local == seq_index).astype(jnp.int32)
    wanted_rank = jnp.cumsum(wanted, axis=1) - 1
    chosen = wanted[:, None, :] * (
        wanted_rank[:, None, :] == jnp.arange(capacity)[None, :, None]
    ).astype(jnp.int32)
    slot_live = (jnp.sum(chosen, axis=2) > 0).reshape(buffer_rows)
    slot_index = jnp.sum(chosen * jnp.arange(slot_count)[None, None, :], axis=2)
    which_batch = slot_index // (heads_local * blocks_local * pick_count)
    which_head = slot_index // (blocks_local * pick_count) % heads_local
    which_block = jnp.take_along_axis(requests, slot_index, axis=1) % blocks_local
    stacked = key_value.reshape(
        2, batch_count, blocks_local, BLOCK, heads_local, head_dim
    ).transpose(1, 2, 4, 0, 3, 5)
    outgoing = stacked[which_batch, which_block, which_head].reshape(
        buffer_rows, 2, BLOCK, head_dim
    )
    incoming = lax.all_to_all(outgoing, "seq", split_axis=0, concat_axis=0, tiled=True)
    fetched = incoming[position].reshape(
        batch_count, heads_local, blocks_local, pick_count, 2, BLOCK, head_dim
    )
    fetched = fetched.transpose(4, 0, 1, 2, 3, 5, 6).reshape(
        2, batch_count, heads_local, blocks_local, pick_count * BLOCK, head_dim
    )
    local_pos = global_pos - seq_index * tok_local
    pick_hot = (local_pos[:, None] == jnp.arange(tok_local)[None, :]).astype(bf16)
    owned_rows = jnp.einsum("gt,pbtc->pbgc", pick_hot, key_value, preferred_element_type=f32)
    shared = global_sum(owned_rows).astype(bf16)
    globals_count = shared.shape[2]
    global_kv = shared.reshape(2, batch_count, globals_count, heads_local, head_dim).transpose(
        0, 1, 3, 2, 4
    )
    global_kv = jnp.broadcast_to(
        global_kv[:, :, :, None],
        (2, batch_count, heads_local, blocks_local, globals_count, head_dim),
    )
    lists_all = jnp.concatenate([window_lists, fetched, global_kv], axis=4)
    key_lists = lists_all[0]
    value_lists = lists_all[1]
    key_count = key_lists.shape[3]
    block_ids = seq_index * blocks_local + jnp.arange(blocks_local)
    column_ids = jnp.arange(key_count)[None, :]
    middle_ok = jnp.where(
        (column_ids >= 2 * BLOCK) & (column_ids < 3 * BLOCK),
        (block_ids < total_blocks - 1)[:, None],
        True,
    )
    valid_mask = jnp.where(column_ids < BLOCK, (block_ids > 0)[:, None], middle_ok)
    query_blocks = to_blocks(query_rows)
    grad_blocks = to_blocks(grad_out)
    scores = (
        jnp.einsum("bhjqd,bhjkd->bhjqk", query_blocks, key_lists, preferred_element_type=f32)
        * score_scale
    )
    scores = jnp.where(valid_mask[None, None, :, None, :], scores, -1e30)
    row_max = jnp.max(scores, axis=-1, keepdims=True)
    log_total = row_max + jnp.log(jnp.sum(jnp.exp(scores - row_max), axis=-1, keepdims=True))
    weights = jnp.exp(scores - log_total)
    weights_b = weights.astype(bf16)
    mixed_rows = jnp.einsum(
        "bhjqk,bhjkd->bhjqd", weights_b, value_lists, preferred_element_type=f32
    )
    attended = from_blocks(mixed_rows.astype(bf16))
    row_delta = jnp.sum(grad_blocks.astype(f32) * mixed_rows, axis=-1, keepdims=True)
    grad_probs = jnp.einsum(
        "bhjqd,bhjkd->bhjqk", grad_blocks, value_lists, preferred_element_type=f32
    )
    dscore_b = (weights * (grad_probs - row_delta)).astype(bf16)
    grad_query = (
        jnp.einsum("bhjqk,bhjkd->bhjqd", dscore_b, key_lists, preferred_element_type=f32)
        * score_scale
    )

    def key_grads(lower, upper):
        key_part = (
            jnp.einsum(
                "bhjqk,bhjqd->bhjkd",
                dscore_b[..., lower:upper],
                query_blocks,
                preferred_element_type=f32,
            )
            * score_scale
        )
        value_part = jnp.einsum(
            "bhjqk,bhjqd->bhjkd",
            weights_b[..., lower:upper],
            grad_blocks,
            preferred_element_type=f32,
        )
        return jnp.stack([key_part, value_part])

    window_cols = 3 * BLOCK
    random_cols = pick_count * BLOCK
    window_grads = key_grads(0, window_cols).reshape(
        2, batch_count, heads_local, blocks_local, 3, BLOCK, head_dim
    )
    padded_grads = jnp.pad(
        window_grads[:, :, :, :, 0], ((0, 0), (0, 0), (0, 0), (0, 2), (0, 0), (0, 0))
    )
    padded_grads = padded_grads + jnp.pad(
        window_grads[:, :, :, :, 1], ((0, 0), (0, 0), (0, 0), (1, 1), (0, 0), (0, 0))
    )
    padded_grads = padded_grads + jnp.pad(
        window_grads[:, :, :, :, 2], ((0, 0), (0, 0), (0, 0), (2, 0), (0, 0), (0, 0))
    )
    own_grads = padded_grads[:, :, :, 1:-1]
    rim_grads = jnp.stack([padded_grads[:, :, :, 0], padded_grads[:, :, :, -1]], axis=3)
    returned = extended_2(rim_grads.astype(jnp.bfloat16), (("seq", 3),), 1).astype(rim_grads.dtype)
    own_grads = own_grads.at[:, :, :, 0].add(returned[:, :, :, 0])
    own_grads = own_grads.at[:, :, :, -1].add(returned[:, :, :, 3])
    global_grads = jnp.sum(key_grads(window_cols + random_cols, key_count), axis=3)
    global_grads = global_grads.transpose(0, 1, 3, 2, 4).reshape(
        2, batch_count, globals_count, columns
    )
    global_summed = global_sum(global_grads)
    inside = (local_pos >= 0) & (local_pos < tok_local)
    safe_pos = jnp.where(inside, local_pos, tok_local)
    global_local = (
        jnp.zeros((2, batch_count, tok_local, columns), f32)
        .at[:, :, safe_pos]
        .add(global_summed, mode="drop")
    )
    global_part = pair_blocks(global_local)
    target = ((which_batch * blocks_local + which_block) * heads_local + which_head).reshape(
        buffer_rows
    )
    random_grads = key_grads(window_cols, window_cols + random_cols)
    per_slot = random_grads.reshape(
        2, batch_count, heads_local, blocks_local, pick_count, BLOCK, head_dim
    )
    per_slot = per_slot.transpose(1, 2, 3, 4, 0, 5, 6).reshape(slot_count, 2, BLOCK, head_dim)
    sending = jnp.zeros((buffer_rows, 2, BLOCK, head_dim), f32).at[position].set(per_slot)
    arrived = lax.all_to_all(
        sending.astype(jnp.bfloat16), "seq", split_axis=0, concat_axis=0, tiled=True
    ).astype(sending.dtype)
    kept = jnp.where(slot_live[:, None, None, None], arrived, 0.0)
    summed = (
        jnp.zeros((batch_count * blocks_local * heads_local, 2, BLOCK, head_dim), f32)
        .at[target]
        .add(kept)
    )
    random_part = summed.reshape(
        batch_count, blocks_local, heads_local, 2, BLOCK, head_dim
    ).transpose(3, 0, 2, 1, 4, 5)
    total_grads = own_grads + random_part + global_part
    grad_key = from_blocks(total_grads[0].astype(bf16))
    grad_value = from_blocks(total_grads[1].astype(bf16))
    return (attended, from_blocks(grad_query.astype(bf16)), grad_key, grad_value)


def body(query_rows, key_rows, value_rows, grad_out, rand_blocks, global_pos):
    seq_count, head_count = lax.axis_size("seq"), lax.axis_size("head")
    batch_count, heads_local = rand_blocks.shape[:2]
    tokens = query_rows.shape[1]
    whole_heads = seq_count == 2 * heads_local and heads_local & (heads_local - 1) == 0
    whole_heads = whole_heads and heads_local > 1 and tokens & (tokens - 1) == 0
    whole_heads = whole_heads and head_count % 2 == 0 and batch_count == 1
    form = by_heads if whole_heads else by_blocks
    return form(query_rows, key_rows, value_rows, grad_out, rand_blocks, global_pos)


def solution(mesh):
    return jax.shard_map(
        body,
        mesh=mesh,
        in_specs=(
            P(None, "seq", "head"),
            P(None, "seq", "head"),
            P(None, "seq", "head"),
            P(None, "seq", "head"),
            P(None, "head", None, None),
            P(),
        ),
        out_specs=(
            P(None, "seq", "head"),
            P(None, "seq", "head"),
            P(None, "seq", "head"),
            P(None, "seq", "head"),
        ),
        check_vma=False,
    )
```

```python
import functools

import jax
import jax.numpy as jnp
from jax import lax
from jax.experimental import pallas as pl
from jax.experimental.pallas import tpu as pltpu
from jax.sharding import PartitionSpec as P


BLOCK = 64
AXES = ("seq", "head")
CHUNK = 4
GRANT = 24 * 1024 * 1024
VMEM = pl.BlockSpec(memory_space=pltpu.VMEM)
PARAMS = pltpu.CompilerParams(vmem_limit_bytes=GRANT)
PACK_PARAMS = pltpu.CompilerParams(vmem_limit_bytes=GRANT)
HBM = pl.BlockSpec(memory_space=pltpu.HBM)
F32 = jnp.float32
BF16 = jnp.bfloat16


def dot(a, b, dims):
    return lax.dot_general(a, b, (dims, ((), ())), preferred_element_type=F32)


def round_order(rounds):
    return (*range(1, rounds, 2), *range(0, rounds, 2))


def attend_calls(rounds):
    order = round_order(rounds)
    return [order[: rounds // 2], order[rounds // 2 :]]


def round_pairs(seq_count, head_count, i):
    rounds = seq_count // 2
    pairs = []
    for s in range(seq_count):
        for head in range(head_count):
            y, c = head // 2, head % 2
            k = rounds * c + (s % rounds ^ i)
            pairs.append((s * head_count + head, k * head_count + 2 * y + s // rounds))
    return pairs


def keep_in_hbm(array):
    return pltpu.with_memory_space_constraint(array, pltpu.HBM)


def pack_kernel(rounds, width, *rest):
    ins, smalls = rest[:4], rest[4:6]
    outs, small_outs, sem, small_sem = rest[6:-4], rest[-4:-2], rest[-2], rest[-1]
    turn = lax.rem(lax.axis_index("seq"), rounds)
    copies = []
    for m in range(2):
        for i in range(rounds):
            col = pl.multiple_of((turn ^ i) * width, width)
            for n in range(2):
                copy = pltpu.make_async_copy(
                    ins[2 * m + n].at[0, :, pl.ds(col, width)],
                    outs[m * rounds + i].at[n],
                    sem.at[m * rounds + i, n],
                )
                copy.start()
                copies.append(copy)
    for m in range(2):
        copy = pltpu.make_async_copy(smalls[m], small_outs[m], small_sem.at[m])
        copy.start()
        copies.append(copy)
    for copy in copies:
        copy.wait()


def pack(arrays, smalls, rounds):
    _, tokens, columns = arrays[0].shape
    width = columns // rounds
    out = jax.ShapeDtypeStruct((2, tokens, width), BF16)
    outs = pl.pallas_call(
        functools.partial(pack_kernel, rounds, width),
        out_shape=[out] * (2 * rounds)
        + [jax.ShapeDtypeStruct(a.shape, a.dtype) for a in smalls],
        in_specs=[HBM] * 6,
        out_specs=[VMEM] * (2 * rounds + 2),
        scratch_shapes=[
            pltpu.SemaphoreType.DMA((2 * rounds, 2)),
            pltpu.SemaphoreType.DMA((2,)),
        ],
        compiler_params=PACK_PARAMS,
        cost_estimate=pl.CostEstimate(
            flops=0, transcendentals=0, bytes_accessed=16 * tokens * columns
        ),
        name="pack",
    )(*[keep_in_hbm(a) for a in (*arrays, *smalls)])
    return outs[:rounds], outs[rounds:-2], outs[-2], outs[-1]


def unpack_kernel(rounds, width, *rest):
    ins, outs, sem = rest[:rounds], rest[rounds:-1], rest[-1]
    turn = lax.rem(lax.axis_index("seq"), rounds)
    copies = []
    for i in range(rounds):
        col = pl.multiple_of((turn ^ i) * width, width)
        for n in range(2):
            copy = pltpu.make_async_copy(
                ins[i].at[n], outs[n].at[0, :, pl.ds(col, width)], sem.at[i, n]
            )
            copy.start()
            copies.append(copy)
    for copy in copies:
        copy.wait()


def unpack(parts):
    rounds = len(parts)
    _, tokens, width = parts[0].shape
    out = jax.ShapeDtypeStruct((1, tokens, rounds * width), BF16)
    return pl.pallas_call(
        functools.partial(unpack_kernel, rounds, width),
        out_shape=[out] * 2,
        in_specs=[VMEM] * rounds,
        out_specs=[HBM] * 2,
        scratch_shapes=[pltpu.SemaphoreType.DMA((rounds, 2))],
        compiler_params=PARAMS,
        cost_estimate=pl.CostEstimate(
            flops=0, transcendentals=0, bytes_accessed=8 * rounds * tokens * width
        ),
        name="unpack",
    )(*parts)


def attend_kernel(
    rounds, run_blocks, picks, turns, opens, closes, mine_ref, other_table_ref, *rest
):
    rest = list(rest)
    take = lambda n: [rest.pop(0) for _ in range(n)]
    count = len(turns)
    if opens:
        (global_ref,), parts = take(1), take(2 * rounds)
    else:
        all_ref, picked_ref, _ = take(3)
    sides = take(count)
    mixes = take(count)
    if opens:
        all_ref, picked_ref = take(2)
    (acc,) = take(1)
    if closes:
        (send_ref,) = take(1)
    keep, table, table_sem = take(3)

    k, h = lax.axis_index("seq"), lax.rem(lax.axis_index("head"), 2)
    tokens = run_blocks * BLOCK
    half = rounds * tokens
    total_blocks = 2 * rounds * run_blocks
    listed = (3 + picks) * BLOCK
    flip = (h * rounds + lax.rem(k, rounds)) * run_blocks
    head = lax.rem(k, rounds)
    held_here = pltpu.make_async_copy(mine_ref, table, table_sem.at[0])
    held_there = pltpu.make_async_copy(other_table_ref, table, table_sem.at[0])
    pl.when(k // rounds == h)(held_here.start)
    pl.when(k // rounds != h)(held_there.start)
    scale = all_ref.shape[2] ** -0.5
    column = lax.broadcasted_iota(jnp.int32, (1, 4 * BLOCK), 1)

    if opens:
        shared = global_ref.shape[1]
        spots = jnp.broadcast_to(global_ref[...] ^ (flip * BLOCK), (shared, shared)).T[:, :1]
        sums = [None, None]
        for n in range(2 * rounds):
            ids = lax.broadcasted_iota(jnp.int32, (shared, tokens), 1) + n * tokens
            hot = jnp.where(ids == spots, 1.0, 0.0).astype(BF16)
            for m in range(2):
                part = parts[n][m]
                all_ref[m, n * tokens : (n + 1) * tokens] = part
                product = dot(hot, part, ((1,), (0,)))
                sums[m] = product if n == 0 else sums[m] + product
        for m in range(2):
            picked_ref[m] = sums[m].astype(BF16)
        acc[...] = jnp.zeros_like(acc)

    held_here.wait()

    def begin(n, block):
        rows_of = slice(block * BLOCK, (block + 1) * BLOCK)
        query, grad = sides[n][0, rows_of], sides[n][1, rows_of]
        index = (turns[n] * run_blocks + block) ^ flip
        named = [
            jnp.maximum(index - 1, 0),
            index,
            jnp.minimum(index + 1, total_blocks - 1),
        ]
        for m in range(picks):
            named.append(
                table[m, head, index]
            )
        rows = [pl.multiple_of((b ^ flip) * BLOCK, BLOCK) for b in named]
        keys, values = [
            jnp.concatenate(
                [all_ref[m, pl.ds(r, BLOCK)] for r in rows] + [picked_ref[m]], axis=0
            )
            for m in range(2)
        ]
        scores = dot(query, keys, ((1,), (1,))) * scale
        probs = dot(grad, values, ((1,), (1,)))
        out = ((column < BLOCK) & (index == 0)) | (
            (column >= 2 * BLOCK) & (column < 3 * BLOCK) & (index == total_blocks - 1)
        )
        near = jnp.where(out, -1e30, scores[:, : 4 * BLOCK])
        scores = jnp.concatenate([near, scores[:, 4 * BLOCK :]], axis=1)
        return n, rows_of, rows, query, grad, keys, values, scores, probs

    def finish(state):
        weighed, scored = [], []
        for n, rows_of, rows, query, grad, keys, values, scores, probs in state:
            peak = jnp.max(scores, axis=1, keepdims=True)
            powers = jnp.exp(scores - peak)
            weights = powers * (1.0 / jnp.sum(powers, axis=1, keepdims=True))
            weighed.append((weights, weights.astype(BF16)))
        for (*_, probs), (weights, weights_b) in zip(state, weighed):
            delta = jnp.sum(weights_b.astype(F32) * probs, axis=1, keepdims=True)
            scored.append((weights * (probs - delta)).astype(BF16))
        for (n, rows_of, rows, query, grad, keys, values, _, _), (_, weights_b), dscore_b in zip(
            state, weighed, scored
        ):
            mixed = dot(weights_b, values, ((1,), (0,)))
            grad_query = dot(dscore_b, keys, ((1,), (0,))) * scale
            mixes[n][0, rows_of] = mixed.astype(BF16)
            mixes[n][1, rows_of] = grad_query.astype(BF16)
            keep[n, 0, rows_of] = dscore_b[:, listed:]
            keep[n, 1, rows_of] = weights_b[:, listed:]
            key_part = dot(dscore_b[:, :listed], query, ((0,), (0,)))
            value_part = dot(weights_b[:, :listed], grad, ((0,), (0,)))
            for m, r in enumerate(rows):
                span = slice(m * BLOCK, (m + 1) * BLOCK)
                acc[0, pl.ds(r, BLOCK)] += key_part[span]
                acc[1, pl.ds(r, BLOCK)] += value_part[span]

    held = None
    for n in range(count):
        for block in range(0, run_blocks, CHUNK):
            state = [begin(n, b) for b in range(block, block + CHUNK)]
            if held is not None:
                finish(held)
            held = state
    finish(held)
    for m in range(2):
        shared = acc[m, 2 * half :]
        for n in range(count):
            shared = shared + dot(keep[n, m], sides[n][m], ((0,), (0,)))
        acc[m, 2 * half :] = shared
        if closes:
            send_ref[m, :half] = acc[m, half : 2 * half]
            send_ref[m, half:] = shared


def attend(tables, places, parts, state, sides, turns, rounds, picks, closes):
    opens = state is None
    _, tokens, width = sides[0].shape
    run_blocks = tokens // BLOCK
    shared = places.shape[1]
    entries = (3 + picks) * BLOCK + shared
    count = len(turns)
    half = rounds * tokens
    one = jax.ShapeDtypeStruct((2, tokens, width), BF16)
    acc = jax.ShapeDtypeStruct((2, 2 * half + shared, width), F32)
    out_shape = [one] * count
    if opens:
        given = [places, *parts]
        out_shape += [
            jax.ShapeDtypeStruct((2, 2 * half, width), BF16),
            jax.ShapeDtypeStruct((2, shared, width), BF16),
        ]
        aliases = {}
    else:
        given = list(state)
        aliases = {2 + len(given) - 1: count}
    out_shape += [acc]
    if closes:
        out_shape += [jax.ShapeDtypeStruct((2, half + shared, width), F32)]
    outs = pl.pallas_call(
        functools.partial(
            attend_kernel, rounds, run_blocks, picks, turns, opens, closes
        ),
        out_shape=out_shape,
        in_specs=[VMEM] * (2 + len(given) + count),
        out_specs=[VMEM] * len(out_shape),
        input_output_aliases=aliases,
        scratch_shapes=[
            pltpu.VMEM((count, 2, tokens, shared), BF16),
            pltpu.SMEM(tables[0].shape, jnp.int32),
            pltpu.SemaphoreType.DMA((1,)),
        ],
        compiler_params=PARAMS,
        cost_estimate=pl.CostEstimate(
            flops=12 * count * tokens * entries * width,
            transcendentals=count * tokens * entries,
            bytes_accessed=12 * half * width,
        ),
        name="attend",
    )(*tables, *given, *sides)
    return outs[:count], outs[count:]


def total_kernel(rounds, global_ref, acc_ref, came_ref, *outs):
    tokens, width = outs[0].shape[1:]
    half = rounds * tokens
    count = global_ref.shape[1]
    scale = width**-0.5
    k, h = lax.axis_index("seq"), lax.rem(lax.axis_index("head"), 2)
    flip = (h * rounds + lax.rem(k, rounds)) * tokens
    spots = global_ref[...] ^ flip
    halves = []
    for n in range(2):
        shared = acc_ref[n, 2 * half :] + came_ref[n, half:]
        high = shared.astype(BF16)
        halves += [high, (shared - high.astype(F32)).astype(BF16)]
    halves = jnp.concatenate(halves, axis=1)
    for i in range(rounds):
        ids = lax.broadcasted_iota(jnp.int32, (tokens, count), 0) + i * tokens
        hot = jnp.where(ids == spots, 1.0, 0.0).astype(BF16)
        spread = dot(hot, halves, ((1,), (0,)))
        mine = slice(i * tokens, (i + 1) * tokens)
        for n in range(2):
            whole = acc_ref[n, mine] + came_ref[n, mine]
            whole = whole + spread[:, 2 * n * width : (2 * n + 1) * width]
            whole = whole + spread[:, (2 * n + 1) * width : (2 * n + 2) * width]
            if n == 0:
                whole = whole * scale
            outs[i][n] = whole.astype(BF16)


def total(places, acc, came, rounds):
    rows, width = came.shape[1:]
    count = places.shape[1]
    tokens = (rows - count) // rounds
    return pl.pallas_call(
        functools.partial(total_kernel, rounds),
        out_shape=[jax.ShapeDtypeStruct((2, tokens, width), BF16)] * rounds,
        in_specs=[VMEM] * 3,
        out_specs=[VMEM] * rounds,
        compiler_params=PARAMS,
        cost_estimate=pl.CostEstimate(
            flops=4 * rows * width, transcendentals=0, bytes_accessed=20 * rows * width
        ),
        name="total",
    )(places, acc, came)


def by_heads(query_rows, key_rows, value_rows, grad_out, rand_blocks, global_pos):
    seq_count, head_count = lax.axis_size("seq"), lax.axis_size("head")
    _, rounds, _, picks = rand_blocks.shape
    sibling = [(i, i ^ 1) for i in range(head_count)]
    trades = [round_pairs(seq_count, head_count, i) for i in range(rounds)]

    order = round_order(rounds)

    def send(parts, turns=order):
        out = {}
        for n in turns:
            out[n] = lax.ppermute(parts[n], AXES, trades[n])
        return out

    def swap(parts):
        out = []
        for part in parts:
            out.append(lax.ppermute(part, "head", sibling))
        return out

    arrays = [key_rows, value_rows, query_rows, grad_out]
    smalls = [global_pos.reshape(1, -1), rand_blocks[0].transpose(2, 0, 1)]
    kv, sides, places, table = pack(arrays, smalls, rounds)
    kv = send(kv)
    sides = send(sides)
    tables = [table, *swap([table])]
    parts = [kv[n] for n in range(rounds)]
    parts += swap(parts)
    mixes, state = {}, None
    calls = attend_calls(rounds)
    for n, turns in enumerate(calls):
        mix, new = attend(
            tables,
            places,
            parts,
            state,
            [sides[t] for t in turns],
            turns,
            rounds,
            picks,
            n == len(calls) - 1,
        )
        mixes.update(send(dict(zip(turns, mix)), turns))
        state = new if state is None else (*state[:2], *new)
    _, _, acc, leaving = state
    (came,) = swap([leaving])
    grads = total(places, acc, came, rounds)
    grads = send(grads)
    attended, grad_query = unpack([mixes[n] for n in range(rounds)])
    grad_key, grad_value = unpack([grads[n] for n in range(rounds)])
    return attended, grad_query, grad_key, grad_value


def extended_2(value, sides, width):
    for axis, dim in sides:
        size, length = (lax.axis_size(axis), value.shape[dim])
        up = [(i, (i + 1) % size) for i in range(size - 1)]
        down = [(j, i) for i, j in up]
        last = lax.slice_in_dim(value, length - width, length, axis=dim)
        first = lax.slice_in_dim(value, 0, width, axis=dim)
        before = lax.ppermute(last, axis, up)
        after = lax.ppermute(first, axis, down)
        value = jnp.concatenate([before, value, after], axis=dim)
    return value


def by_blocks(query_rows, key_rows, value_rows, grad_out, rand_blocks, global_pos):
    batch_count, tok_local, columns = query_rows.shape
    seq_count = lax.axis_size("seq")
    seq_index = lax.axis_index("seq")
    heads_local = rand_blocks.shape[1]
    total_blocks = rand_blocks.shape[2]
    pick_count = rand_blocks.shape[3]
    head_dim = columns // heads_local
    blocks_local = tok_local // BLOCK
    score_scale = head_dim ** (-0.5)
    slot_count = batch_count * heads_local * blocks_local * pick_count
    capacity = (slot_count + seq_count - 1) // seq_count
    buffer_rows = seq_count * capacity
    f32 = jnp.float32
    bf16 = jnp.bfloat16

    def to_blocks(array):
        return array.reshape(batch_count, blocks_local, BLOCK, heads_local, head_dim).transpose(
            0, 3, 1, 2, 4
        )

    def from_blocks(array):
        return array.transpose(0, 2, 3, 1, 4).reshape(batch_count, tok_local, columns)

    def pair_blocks(array):
        return array.reshape(2, batch_count, blocks_local, BLOCK, heads_local, head_dim).transpose(
            0, 1, 4, 2, 3, 5
        )

    def global_sum(array):
        return lax.psum(array, "seq")

    key_value = jnp.stack([key_rows, value_rows])
    edge_rows = jnp.concatenate([key_value[:, :, :BLOCK], key_value[:, :, -BLOCK:]], axis=2)
    extended = extended_2(edge_rows, (("seq", 2),), BLOCK)
    padded = jnp.concatenate([extended[:, :, :BLOCK], key_value, extended[:, :, -BLOCK:]], axis=2)

    def shifted(start):
        return pair_blocks(padded[:, :, start : start + tok_local])

    window_lists = jnp.concatenate([shifted(0), shifted(BLOCK), shifted(2 * BLOCK)], axis=4)
    my_table = lax.dynamic_slice_in_dim(
        rand_blocks, seq_index * blocks_local, blocks_local, 2
    ).reshape(slot_count)
    holder = my_table // blocks_local
    holder_hot = (holder[:, None] == jnp.arange(seq_count)[None, :]).astype(jnp.int32)
    holder_rank = jnp.sum((jnp.cumsum(holder_hot, axis=0) - 1) * holder_hot, axis=1)
    position = holder * capacity + holder_rank
    requests = rand_blocks.reshape(batch_count, heads_local, seq_count, blocks_local, pick_count)
    requests = requests.transpose(2, 0, 1, 3, 4).reshape(seq_count, slot_count)
    wanted = (requests // blocks_local == seq_index).astype(jnp.int32)
    wanted_rank = jnp.cumsum(wanted, axis=1) - 1
    chosen = wanted[:, None, :] * (
        wanted_rank[:, None, :] == jnp.arange(capacity)[None, :, None]
    ).astype(jnp.int32)
    slot_live = (jnp.sum(chosen, axis=2) > 0).reshape(buffer_rows)
    slot_index = jnp.sum(chosen * jnp.arange(slot_count)[None, None, :], axis=2)
    which_batch = slot_index // (heads_local * blocks_local * pick_count)
    which_head = slot_index // (blocks_local * pick_count) % heads_local
    which_block = jnp.take_along_axis(requests, slot_index, axis=1) % blocks_local
    stacked = key_value.reshape(
        2, batch_count, blocks_local, BLOCK, heads_local, head_dim
    ).transpose(1, 2, 4, 0, 3, 5)
    outgoing = stacked[which_batch, which_block, which_head].reshape(
        buffer_rows, 2, BLOCK, head_dim
    )
    incoming = lax.all_to_all(outgoing, "seq", split_axis=0, concat_axis=0, tiled=True)
    fetched = incoming[position].reshape(
        batch_count, heads_local, blocks_local, pick_count, 2, BLOCK, head_dim
    )
    fetched = fetched.transpose(4, 0, 1, 2, 3, 5, 6).reshape(
        2, batch_count, heads_local, blocks_local, pick_count * BLOCK, head_dim
    )
    local_pos = global_pos - seq_index * tok_local
    pick_hot = (local_pos[:, None] == jnp.arange(tok_local)[None, :]).astype(bf16)
    owned_rows = jnp.einsum("gt,pbtc->pbgc", pick_hot, key_value, preferred_element_type=f32)
    shared = global_sum(owned_rows).astype(bf16)
    globals_count = shared.shape[2]
    global_kv = shared.reshape(2, batch_count, globals_count, heads_local, head_dim).transpose(
        0, 1, 3, 2, 4
    )
    global_kv = jnp.broadcast_to(
        global_kv[:, :, :, None],
        (2, batch_count, heads_local, blocks_local, globals_count, head_dim),
    )
    lists_all = jnp.concatenate([window_lists, fetched, global_kv], axis=4)
    key_lists = lists_all[0]
    value_lists = lists_all[1]
    key_count = key_lists.shape[3]
    block_ids = seq_index * blocks_local + jnp.arange(blocks_local)
    column_ids = jnp.arange(key_count)[None, :]
    middle_ok = jnp.where(
        (column_ids >= 2 * BLOCK) & (column_ids < 3 * BLOCK),
        (block_ids < total_blocks - 1)[:, None],
        True,
    )
    valid_mask = jnp.where(column_ids < BLOCK, (block_ids > 0)[:, None], middle_ok)
    query_blocks = to_blocks(query_rows)
    grad_blocks = to_blocks(grad_out)
    scores = (
        jnp.einsum("bhjqd,bhjkd->bhjqk", query_blocks, key_lists, preferred_element_type=f32)
        * score_scale
    )
    scores = jnp.where(valid_mask[None, None, :, None, :], scores, -1e30)
    row_max = jnp.max(scores, axis=-1, keepdims=True)
    log_total = row_max + jnp.log(jnp.sum(jnp.exp(scores - row_max), axis=-1, keepdims=True))
    weights = jnp.exp(scores - log_total)
    weights_b = weights.astype(bf16)
    mixed_rows = jnp.einsum(
        "bhjqk,bhjkd->bhjqd", weights_b, value_lists, preferred_element_type=f32
    )
    attended = from_blocks(mixed_rows.astype(bf16))
    row_delta = jnp.sum(grad_blocks.astype(f32) * mixed_rows, axis=-1, keepdims=True)
    grad_probs = jnp.einsum(
        "bhjqd,bhjkd->bhjqk", grad_blocks, value_lists, preferred_element_type=f32
    )
    dscore_b = (weights * (grad_probs - row_delta)).astype(bf16)
    grad_query = (
        jnp.einsum("bhjqk,bhjkd->bhjqd", dscore_b, key_lists, preferred_element_type=f32)
        * score_scale
    )

    def key_grads(lower, upper):
        key_part = (
            jnp.einsum(
                "bhjqk,bhjqd->bhjkd",
                dscore_b[..., lower:upper],
                query_blocks,
                preferred_element_type=f32,
            )
            * score_scale
        )
        value_part = jnp.einsum(
            "bhjqk,bhjqd->bhjkd",
            weights_b[..., lower:upper],
            grad_blocks,
            preferred_element_type=f32,
        )
        return jnp.stack([key_part, value_part])

    window_cols = 3 * BLOCK
    random_cols = pick_count * BLOCK
    window_grads = key_grads(0, window_cols).reshape(
        2, batch_count, heads_local, blocks_local, 3, BLOCK, head_dim
    )
    padded_grads = jnp.pad(
        window_grads[:, :, :, :, 0], ((0, 0), (0, 0), (0, 0), (0, 2), (0, 0), (0, 0))
    )
    padded_grads = padded_grads + jnp.pad(
        window_grads[:, :, :, :, 1], ((0, 0), (0, 0), (0, 0), (1, 1), (0, 0), (0, 0))
    )
    padded_grads = padded_grads + jnp.pad(
        window_grads[:, :, :, :, 2], ((0, 0), (0, 0), (0, 0), (2, 0), (0, 0), (0, 0))
    )
    own_grads = padded_grads[:, :, :, 1:-1]
    rim_grads = jnp.stack([padded_grads[:, :, :, 0], padded_grads[:, :, :, -1]], axis=3)
    returned = extended_2(rim_grads.astype(jnp.bfloat16), (("seq", 3),), 1).astype(rim_grads.dtype)
    own_grads = own_grads.at[:, :, :, 0].add(returned[:, :, :, 0])
    own_grads = own_grads.at[:, :, :, -1].add(returned[:, :, :, 3])
    global_grads = jnp.sum(key_grads(window_cols + random_cols, key_count), axis=3)
    global_grads = global_grads.transpose(0, 1, 3, 2, 4).reshape(
        2, batch_count, globals_count, columns
    )
    global_summed = global_sum(global_grads)
    inside = (local_pos >= 0) & (local_pos < tok_local)
    safe_pos = jnp.where(inside, local_pos, tok_local)
    global_local = (
        jnp.zeros((2, batch_count, tok_local, columns), f32)
        .at[:, :, safe_pos]
        .add(global_summed, mode="drop")
    )
    global_part = pair_blocks(global_local)
    target = ((which_batch * blocks_local + which_block) * heads_local + which_head).reshape(
        buffer_rows
    )
    random_grads = key_grads(window_cols, window_cols + random_cols)
    per_slot = random_grads.reshape(
        2, batch_count, heads_local, blocks_local, pick_count, BLOCK, head_dim
    )
    per_slot = per_slot.transpose(1, 2, 3, 4, 0, 5, 6).reshape(slot_count, 2, BLOCK, head_dim)
    sending = jnp.zeros((buffer_rows, 2, BLOCK, head_dim), f32).at[position].set(per_slot)
    arrived = lax.all_to_all(
        sending.astype(jnp.bfloat16), "seq", split_axis=0, concat_axis=0, tiled=True
    ).astype(sending.dtype)
    kept = jnp.where(slot_live[:, None, None, None], arrived, 0.0)
    summed = (
        jnp.zeros((batch_count * blocks_local * heads_local, 2, BLOCK, head_dim), f32)
        .at[target]
        .add(kept)
    )
    random_part = summed.reshape(
        batch_count, blocks_local, heads_local, 2, BLOCK, head_dim
    ).transpose(3, 0, 2, 1, 4, 5)
    total_grads = own_grads + random_part + global_part
    grad_key = from_blocks(total_grads[0].astype(bf16))
    grad_value = from_blocks(total_grads[1].astype(bf16))
    return (attended, from_blocks(grad_query.astype(bf16)), grad_key, grad_value)


def body(query_rows, key_rows, value_rows, grad_out, rand_blocks, global_pos):
    seq_count, head_count = lax.axis_size("seq"), lax.axis_size("head")
    batch_count, heads_local = rand_blocks.shape[:2]
    tokens = query_rows.shape[1]
    whole_heads = seq_count == 2 * heads_local and heads_local & (heads_local - 1) == 0
    whole_heads = whole_heads and heads_local > 1 and tokens & (tokens - 1) == 0
    whole_heads = whole_heads and head_count % 2 == 0 and batch_count == 1
    form = by_heads if whole_heads else by_blocks
    return form(query_rows, key_rows, value_rows, grad_out, rand_blocks, global_pos)


def solution(mesh):
    return jax.shard_map(
        body,
        mesh=mesh,
        in_specs=(
            P(None, "seq", "head"),
            P(None, "seq", "head"),
            P(None, "seq", "head"),
            P(None, "seq", "head"),
            P(None, "head", None, None),
            P(),
        ),
        out_specs=(
            P(None, "seq", "head"),
            P(None, "seq", "head"),
            P(None, "seq", "head"),
            P(None, "seq", "head"),
        ),
        check_vma=False,
    )
```

```python
import functools

import jax
import jax.numpy as jnp
from jax import lax
from jax.experimental import pallas as pl
from jax.experimental.pallas import tpu as pltpu
from jax.sharding import PartitionSpec as P


BLOCK = 64
AXES = ("seq", "head")
CHUNK = 4
GRANT = 24 * 1024 * 1024
VMEM = pl.BlockSpec(memory_space=pltpu.VMEM)
PARAMS = pltpu.CompilerParams(vmem_limit_bytes=GRANT)
PACK_PARAMS = pltpu.CompilerParams(vmem_limit_bytes=GRANT)
HBM = pl.BlockSpec(memory_space=pltpu.HBM)
F32 = jnp.float32
BF16 = jnp.bfloat16


def dot(a, b, dims):
    return lax.dot_general(a, b, (dims, ((), ())), preferred_element_type=F32)


def round_order(rounds):
    return (*range(rounds - 1, 0, -2), *range(0, rounds, 2))


def attend_calls(rounds):
    order = round_order(rounds)
    return [order[: rounds // 2], order[rounds // 2 :]]


def round_pairs(seq_count, head_count, i):
    rounds = seq_count // 2
    pairs = []
    for s in range(seq_count):
        for head in range(head_count):
            y, c = head // 2, head % 2
            k = rounds * c + (s % rounds ^ i)
            pairs.append((s * head_count + head, k * head_count + 2 * y + s // rounds))
    return pairs


def keep_in_hbm(array):
    return pltpu.with_memory_space_constraint(array, pltpu.HBM)


def pack_kernel(rounds, width, extra, *rest):
    ins, smalls = rest[:2], rest[2 : 2 + extra]
    outs = rest[2 + extra : 2 + extra + rounds]
    small_outs, (sem, small_sem) = rest[2 + extra + rounds : -2], rest[-2:]
    turn = lax.rem(lax.axis_index("seq"), rounds)
    copies = []
    for i in range(rounds):
        col = pl.multiple_of((turn ^ i) * width, width)
        for n in range(2):
            copy = pltpu.make_async_copy(
                ins[n].at[0, :, pl.ds(col, width)], outs[i].at[n], sem.at[i, n]
            )
            copy.start()
            copies.append(copy)
    for m in range(extra):
        copy = pltpu.make_async_copy(smalls[m], small_outs[m], small_sem.at[m])
        copy.start()
        copies.append(copy)
    for copy in copies:
        copy.wait()


def pack(arrays, smalls, rounds):
    _, tokens, columns = arrays[0].shape
    width = columns // rounds
    out = jax.ShapeDtypeStruct((2, tokens, width), BF16)
    outs = pl.pallas_call(
        functools.partial(pack_kernel, rounds, width, len(smalls)),
        out_shape=[out] * rounds
        + [jax.ShapeDtypeStruct(a.shape, a.dtype) for a in smalls],
        in_specs=[HBM] * (2 + len(smalls)),
        out_specs=[VMEM] * (rounds + len(smalls)),
        scratch_shapes=[
            pltpu.SemaphoreType.DMA((rounds, 2)),
            pltpu.SemaphoreType.DMA((2,)),
        ],
        compiler_params=PACK_PARAMS,
        cost_estimate=pl.CostEstimate(
            flops=0, transcendentals=0, bytes_accessed=16 * tokens * columns
        ),
        name="pack",
    )(*[keep_in_hbm(a) for a in (*arrays, *smalls)])
    return outs[:rounds], outs[rounds:]


def unpack_kernel(rounds, width, *rest):
    ins, outs, sem = rest[:rounds], rest[rounds:-1], rest[-1]
    turn = lax.rem(lax.axis_index("seq"), rounds)
    copies = []
    for i in range(rounds):
        col = pl.multiple_of((turn ^ i) * width, width)
        for n in range(2):
            copy = pltpu.make_async_copy(
                ins[i].at[n], outs[n].at[0, :, pl.ds(col, width)], sem.at[i, n]
            )
            copy.start()
            copies.append(copy)
    for copy in copies:
        copy.wait()


def unpack(parts):
    rounds = len(parts)
    _, tokens, width = parts[0].shape
    out = jax.ShapeDtypeStruct((1, tokens, rounds * width), BF16)
    return pl.pallas_call(
        functools.partial(unpack_kernel, rounds, width),
        out_shape=[out] * 2,
        in_specs=[VMEM] * rounds,
        out_specs=[HBM] * 2,
        scratch_shapes=[pltpu.SemaphoreType.DMA((rounds, 2))],
        compiler_params=PARAMS,
        cost_estimate=pl.CostEstimate(
            flops=0, transcendentals=0, bytes_accessed=8 * rounds * tokens * width
        ),
        name="unpack",
    )(*parts)


def attend_kernel(
    rounds, run_blocks, picks, turns, opens, closes, mine_ref, other_table_ref, *rest
):
    rest = list(rest)
    take = lambda n: [rest.pop(0) for _ in range(n)]
    count = len(turns)
    if opens:
        (global_ref,), parts = take(1), take(2 * rounds)
    else:
        all_ref, picked_ref, _ = take(3)
    sides = take(count)
    mixes = take(count)
    if opens:
        all_ref, picked_ref = take(2)
    (acc,) = take(1)
    if closes:
        (send_ref,) = take(1)
    keep, table, table_sem = take(3)

    k, h = lax.axis_index("seq"), lax.rem(lax.axis_index("head"), 2)
    tokens = run_blocks * BLOCK
    half = rounds * tokens
    total_blocks = 2 * rounds * run_blocks
    listed = (3 + picks) * BLOCK
    flip = (h * rounds + lax.rem(k, rounds)) * run_blocks
    head = lax.rem(k, rounds)
    held_here = pltpu.make_async_copy(mine_ref, table, table_sem.at[0])
    held_there = pltpu.make_async_copy(other_table_ref, table, table_sem.at[0])
    pl.when(k // rounds == h)(held_here.start)
    pl.when(k // rounds != h)(held_there.start)
    scale = all_ref.shape[2] ** -0.5
    column = lax.broadcasted_iota(jnp.int32, (1, 4 * BLOCK), 1)

    if opens:
        shared = global_ref.shape[1]
        spots = jnp.broadcast_to(global_ref[...] ^ (flip * BLOCK), (shared, shared)).T[:, :1]
        sums = [None, None]
        for n in range(2 * rounds):
            ids = lax.broadcasted_iota(jnp.int32, (shared, tokens), 1) + n * tokens
            hot = jnp.where(ids == spots, 1.0, 0.0).astype(BF16)
            for m in range(2):
                part = parts[n][m]
                all_ref[m, n * tokens : (n + 1) * tokens] = part
                product = dot(hot, part, ((1,), (0,)))
                sums[m] = product if n == 0 else sums[m] + product
        for m in range(2):
            picked_ref[m] = sums[m].astype(BF16)
        acc[...] = jnp.zeros_like(acc)

    held_here.wait()

    def begin(n, block):
        rows_of = slice(block * BLOCK, (block + 1) * BLOCK)
        query, grad = sides[n][0, rows_of], sides[n][1, rows_of]
        index = (turns[n] * run_blocks + block) ^ flip
        named = [
            jnp.maximum(index - 1, 0),
            index,
            jnp.minimum(index + 1, total_blocks - 1),
        ]
        for m in range(picks):
            named.append(
                table[m, head, index]
            )
        rows = [pl.multiple_of((b ^ flip) * BLOCK, BLOCK) for b in named]
        keys, values = [
            jnp.concatenate(
                [all_ref[m, pl.ds(r, BLOCK)] for r in rows] + [picked_ref[m]], axis=0
            )
            for m in range(2)
        ]
        scores = dot(query, keys, ((1,), (1,))) * scale
        probs = dot(grad, values, ((1,), (1,)))
        out = ((column < BLOCK) & (index == 0)) | (
            (column >= 2 * BLOCK) & (column < 3 * BLOCK) & (index == total_blocks - 1)
        )
        near = jnp.where(out, -1e30, scores[:, : 4 * BLOCK])
        scores = jnp.concatenate([near, scores[:, 4 * BLOCK :]], axis=1)
        return n, rows_of, rows, query, grad, keys, values, scores, probs

    def finish(state):
        weighed, scored = [], []
        for n, rows_of, rows, query, grad, keys, values, scores, probs in state:
            peak = jnp.max(scores, axis=1, keepdims=True)
            powers = jnp.exp(scores - peak)
            weights = powers * (1.0 / jnp.sum(powers, axis=1, keepdims=True))
            weighed.append((weights, weights.astype(BF16)))
        for (*_, probs), (weights, weights_b) in zip(state, weighed):
            delta = jnp.sum(weights_b.astype(F32) * probs, axis=1, keepdims=True)
            scored.append((weights * (probs - delta)).astype(BF16))
        for (n, rows_of, rows, query, grad, keys, values, _, _), (_, weights_b), dscore_b in zip(
            state, weighed, scored
        ):
            mixed = dot(weights_b, values, ((1,), (0,)))
            grad_query = dot(dscore_b, keys, ((1,), (0,))) * scale
            mixes[n][0, rows_of] = mixed.astype(BF16)
            mixes[n][1, rows_of] = grad_query.astype(BF16)
            keep[n, 0, rows_of] = dscore_b[:, listed:]
            keep[n, 1, rows_of] = weights_b[:, listed:]
            key_part = dot(dscore_b[:, :listed], query, ((0,), (0,)))
            value_part = dot(weights_b[:, :listed], grad, ((0,), (0,)))
            for m, r in enumerate(rows):
                span = slice(m * BLOCK, (m + 1) * BLOCK)
                acc[0, pl.ds(r, BLOCK)] += key_part[span]
                acc[1, pl.ds(r, BLOCK)] += value_part[span]

    held = None
    for n in range(count):
        for block in range(0, run_blocks, CHUNK):
            state = [begin(n, b) for b in range(block, block + CHUNK)]
            if held is not None:
                finish(held)
            held = state
    finish(held)
    for m in range(2):
        shared = acc[m, 2 * half :]
        for n in range(count):
            shared = shared + dot(keep[n, m], sides[n][m], ((0,), (0,)))
        acc[m, 2 * half :] = shared
        if closes:
            send_ref[m, :half] = acc[m, half : 2 * half]
            send_ref[m, half:] = shared


def attend(tables, places, parts, state, sides, turns, rounds, picks, closes):
    opens = state is None
    _, tokens, width = sides[0].shape
    run_blocks = tokens // BLOCK
    shared = places.shape[1]
    entries = (3 + picks) * BLOCK + shared
    count = len(turns)
    half = rounds * tokens
    one = jax.ShapeDtypeStruct((2, tokens, width), BF16)
    acc = jax.ShapeDtypeStruct((2, 2 * half + shared, width), F32)
    out_shape = [one] * count
    if opens:
        given = [places, *parts]
        out_shape += [
            jax.ShapeDtypeStruct((2, 2 * half, width), BF16),
            jax.ShapeDtypeStruct((2, shared, width), BF16),
        ]
        aliases = {}
    else:
        given = list(state)
        aliases = {2 + len(given) - 1: count}
    out_shape += [acc]
    if closes:
        out_shape += [jax.ShapeDtypeStruct((2, half + shared, width), F32)]
    outs = pl.pallas_call(
        functools.partial(
            attend_kernel, rounds, run_blocks, picks, turns, opens, closes
        ),
        out_shape=out_shape,
        in_specs=[VMEM] * (2 + len(given) + count),
        out_specs=[VMEM] * len(out_shape),
        input_output_aliases=aliases,
        scratch_shapes=[
            pltpu.VMEM((count, 2, tokens, shared), BF16),
            pltpu.SMEM(tables[0].shape, jnp.int32),
            pltpu.SemaphoreType.DMA((1,)),
        ],
        compiler_params=PARAMS,
        cost_estimate=pl.CostEstimate(
            flops=12 * count * tokens * entries * width,
            transcendentals=count * tokens * entries,
            bytes_accessed=12 * half * width,
        ),
        name="attend",
    )(*tables, *given, *sides)
    return outs[:count], outs[count:]


def total_kernel(rounds, global_ref, acc_ref, came_ref, *outs):
    tokens, width = outs[0].shape[1:]
    half = rounds * tokens
    count = global_ref.shape[1]
    scale = width**-0.5
    k, h = lax.axis_index("seq"), lax.rem(lax.axis_index("head"), 2)
    flip = (h * rounds + lax.rem(k, rounds)) * tokens
    spots = global_ref[...] ^ flip
    halves = []
    for n in range(2):
        shared = acc_ref[n, 2 * half :] + came_ref[n, half:]
        high = shared.astype(BF16)
        halves += [high, (shared - high.astype(F32)).astype(BF16)]
    halves = jnp.concatenate(halves, axis=1)
    for i in range(rounds):
        ids = lax.broadcasted_iota(jnp.int32, (tokens, count), 0) + i * tokens
        hot = jnp.where(ids == spots, 1.0, 0.0).astype(BF16)
        spread = dot(hot, halves, ((1,), (0,)))
        mine = slice(i * tokens, (i + 1) * tokens)
        for n in range(2):
            whole = acc_ref[n, mine] + came_ref[n, mine]
            whole = whole + spread[:, 2 * n * width : (2 * n + 1) * width]
            whole = whole + spread[:, (2 * n + 1) * width : (2 * n + 2) * width]
            if n == 0:
                whole = whole * scale
            outs[i][n] = whole.astype(BF16)


def total(places, acc, came, rounds):
    rows, width = came.shape[1:]
    count = places.shape[1]
    tokens = (rows - count) // rounds
    return pl.pallas_call(
        functools.partial(total_kernel, rounds),
        out_shape=[jax.ShapeDtypeStruct((2, tokens, width), BF16)] * rounds,
        in_specs=[VMEM] * 3,
        out_specs=[VMEM] * rounds,
        compiler_params=PARAMS,
        cost_estimate=pl.CostEstimate(
            flops=4 * rows * width, transcendentals=0, bytes_accessed=20 * rows * width
        ),
        name="total",
    )(places, acc, came)


def by_heads(query_rows, key_rows, value_rows, grad_out, rand_blocks, global_pos):
    seq_count, head_count = lax.axis_size("seq"), lax.axis_size("head")
    _, rounds, _, picks = rand_blocks.shape
    sibling = [(i, i ^ 1) for i in range(head_count)]
    trades = [round_pairs(seq_count, head_count, i) for i in range(rounds)]

    order = round_order(rounds)

    def send(parts, turns=order):
        out = {}
        for n in turns:
            out[n] = lax.ppermute(parts[n], AXES, trades[n])
        return out

    def swap(parts):
        out = []
        for part in parts:
            out.append(lax.ppermute(part, "head", sibling))
        return out

    smalls = [global_pos.reshape(1, -1), rand_blocks[0].transpose(2, 0, 1)]
    kv, _ = pack([key_rows, value_rows], [], rounds)
    sides, (places, table) = pack([query_rows, grad_out], smalls, rounds)
    kv = send(kv)
    sides = send(sides)
    tables = [table, *swap([table])]
    parts = [kv[n] for n in range(rounds)]
    parts += swap(parts)
    mixes, state = {}, None
    calls = attend_calls(rounds)
    for n, turns in enumerate(calls):
        mix, new = attend(
            tables,
            places,
            parts,
            state,
            [sides[t] for t in turns],
            turns,
            rounds,
            picks,
            n == len(calls) - 1,
        )
        mixes.update(send(dict(zip(turns, mix)), turns[::-1]))
        state = new if state is None else (*state[:2], *new)
    _, _, acc, leaving = state
    (came,) = swap([leaving])
    grads = total(places, acc, came, rounds)
    grads = send(grads)
    attended, grad_query = unpack([mixes[n] for n in range(rounds)])
    grad_key, grad_value = unpack([grads[n] for n in range(rounds)])
    return attended, grad_query, grad_key, grad_value


def extended_2(value, sides, width):
    for axis, dim in sides:
        size, length = (lax.axis_size(axis), value.shape[dim])
        up = [(i, (i + 1) % size) for i in range(size - 1)]
        down = [(j, i) for i, j in up]
        last = lax.slice_in_dim(value, length - width, length, axis=dim)
        first = lax.slice_in_dim(value, 0, width, axis=dim)
        before = lax.ppermute(last, axis, up)
        after = lax.ppermute(first, axis, down)
        value = jnp.concatenate([before, value, after], axis=dim)
    return value


def by_blocks(query_rows, key_rows, value_rows, grad_out, rand_blocks, global_pos):
    batch_count, tok_local, columns = query_rows.shape
    seq_count = lax.axis_size("seq")
    seq_index = lax.axis_index("seq")
    heads_local = rand_blocks.shape[1]
    total_blocks = rand_blocks.shape[2]
    pick_count = rand_blocks.shape[3]
    head_dim = columns // heads_local
    blocks_local = tok_local // BLOCK
    score_scale = head_dim ** (-0.5)
    slot_count = batch_count * heads_local * blocks_local * pick_count
    capacity = (slot_count + seq_count - 1) // seq_count
    buffer_rows = seq_count * capacity
    f32 = jnp.float32
    bf16 = jnp.bfloat16

    def to_blocks(array):
        return array.reshape(batch_count, blocks_local, BLOCK, heads_local, head_dim).transpose(
            0, 3, 1, 2, 4
        )

    def from_blocks(array):
        return array.transpose(0, 2, 3, 1, 4).reshape(batch_count, tok_local, columns)

    def pair_blocks(array):
        return array.reshape(2, batch_count, blocks_local, BLOCK, heads_local, head_dim).transpose(
            0, 1, 4, 2, 3, 5
        )

    def global_sum(array):
        return lax.psum(array, "seq")

    key_value = jnp.stack([key_rows, value_rows])
    edge_rows = jnp.concatenate([key_value[:, :, :BLOCK], key_value[:, :, -BLOCK:]], axis=2)
    extended = extended_2(edge_rows, (("seq", 2),), BLOCK)
    padded = jnp.concatenate([extended[:, :, :BLOCK], key_value, extended[:, :, -BLOCK:]], axis=2)

    def shifted(start):
        return pair_blocks(padded[:, :, start : start + tok_local])

    window_lists = jnp.concatenate([shifted(0), shifted(BLOCK), shifted(2 * BLOCK)], axis=4)
    my_table = lax.dynamic_slice_in_dim(
        rand_blocks, seq_index * blocks_local, blocks_local, 2
    ).reshape(slot_count)
    holder = my_table // blocks_local
    holder_hot = (holder[:, None] == jnp.arange(seq_count)[None, :]).astype(jnp.int32)
    holder_rank = jnp.sum((jnp.cumsum(holder_hot, axis=0) - 1) * holder_hot, axis=1)
    position = holder * capacity + holder_rank
    requests = rand_blocks.reshape(batch_count, heads_local, seq_count, blocks_local, pick_count)
    requests = requests.transpose(2, 0, 1, 3, 4).reshape(seq_count, slot_count)
    wanted = (requests // blocks_local == seq_index).astype(jnp.int32)
    wanted_rank = jnp.cumsum(wanted, axis=1) - 1
    chosen = wanted[:, None, :] * (
        wanted_rank[:, None, :] == jnp.arange(capacity)[None, :, None]
    ).astype(jnp.int32)
    slot_live = (jnp.sum(chosen, axis=2) > 0).reshape(buffer_rows)
    slot_index = jnp.sum(chosen * jnp.arange(slot_count)[None, None, :], axis=2)
    which_batch = slot_index // (heads_local * blocks_local * pick_count)
    which_head = slot_index // (blocks_local * pick_count) % heads_local
    which_block = jnp.take_along_axis(requests, slot_index, axis=1) % blocks_local
    stacked = key_value.reshape(
        2, batch_count, blocks_local, BLOCK, heads_local, head_dim
    ).transpose(1, 2, 4, 0, 3, 5)
    outgoing = stacked[which_batch, which_block, which_head].reshape(
        buffer_rows, 2, BLOCK, head_dim
    )
    incoming = lax.all_to_all(outgoing, "seq", split_axis=0, concat_axis=0, tiled=True)
    fetched = incoming[position].reshape(
        batch_count, heads_local, blocks_local, pick_count, 2, BLOCK, head_dim
    )
    fetched = fetched.transpose(4, 0, 1, 2, 3, 5, 6).reshape(
        2, batch_count, heads_local, blocks_local, pick_count * BLOCK, head_dim
    )
    local_pos = global_pos - seq_index * tok_local
    pick_hot = (local_pos[:, None] == jnp.arange(tok_local)[None, :]).astype(bf16)
    owned_rows = jnp.einsum("gt,pbtc->pbgc", pick_hot, key_value, preferred_element_type=f32)
    shared = global_sum(owned_rows).astype(bf16)
    globals_count = shared.shape[2]
    global_kv = shared.reshape(2, batch_count, globals_count, heads_local, head_dim).transpose(
        0, 1, 3, 2, 4
    )
    global_kv = jnp.broadcast_to(
        global_kv[:, :, :, None],
        (2, batch_count, heads_local, blocks_local, globals_count, head_dim),
    )
    lists_all = jnp.concatenate([window_lists, fetched, global_kv], axis=4)
    key_lists = lists_all[0]
    value_lists = lists_all[1]
    key_count = key_lists.shape[3]
    block_ids = seq_index * blocks_local + jnp.arange(blocks_local)
    column_ids = jnp.arange(key_count)[None, :]
    middle_ok = jnp.where(
        (column_ids >= 2 * BLOCK) & (column_ids < 3 * BLOCK),
        (block_ids < total_blocks - 1)[:, None],
        True,
    )
    valid_mask = jnp.where(column_ids < BLOCK, (block_ids > 0)[:, None], middle_ok)
    query_blocks = to_blocks(query_rows)
    grad_blocks = to_blocks(grad_out)
    scores = (
        jnp.einsum("bhjqd,bhjkd->bhjqk", query_blocks, key_lists, preferred_element_type=f32)
        * score_scale
    )
    scores = jnp.where(valid_mask[None, None, :, None, :], scores, -1e30)
    row_max = jnp.max(scores, axis=-1, keepdims=True)
    log_total = row_max + jnp.log(jnp.sum(jnp.exp(scores - row_max), axis=-1, keepdims=True))
    weights = jnp.exp(scores - log_total)
    weights_b = weights.astype(bf16)
    mixed_rows = jnp.einsum(
        "bhjqk,bhjkd->bhjqd", weights_b, value_lists, preferred_element_type=f32
    )
    attended = from_blocks(mixed_rows.astype(bf16))
    row_delta = jnp.sum(grad_blocks.astype(f32) * mixed_rows, axis=-1, keepdims=True)
    grad_probs = jnp.einsum(
        "bhjqd,bhjkd->bhjqk", grad_blocks, value_lists, preferred_element_type=f32
    )
    dscore_b = (weights * (grad_probs - row_delta)).astype(bf16)
    grad_query = (
        jnp.einsum("bhjqk,bhjkd->bhjqd", dscore_b, key_lists, preferred_element_type=f32)
        * score_scale
    )

    def key_grads(lower, upper):
        key_part = (
            jnp.einsum(
                "bhjqk,bhjqd->bhjkd",
                dscore_b[..., lower:upper],
                query_blocks,
                preferred_element_type=f32,
            )
            * score_scale
        )
        value_part = jnp.einsum(
            "bhjqk,bhjqd->bhjkd",
            weights_b[..., lower:upper],
            grad_blocks,
            preferred_element_type=f32,
        )
        return jnp.stack([key_part, value_part])

    window_cols = 3 * BLOCK
    random_cols = pick_count * BLOCK
    window_grads = key_grads(0, window_cols).reshape(
        2, batch_count, heads_local, blocks_local, 3, BLOCK, head_dim
    )
    padded_grads = jnp.pad(
        window_grads[:, :, :, :, 0], ((0, 0), (0, 0), (0, 0), (0, 2), (0, 0), (0, 0))
    )
    padded_grads = padded_grads + jnp.pad(
        window_grads[:, :, :, :, 1], ((0, 0), (0, 0), (0, 0), (1, 1), (0, 0), (0, 0))
    )
    padded_grads = padded_grads + jnp.pad(
        window_grads[:, :, :, :, 2], ((0, 0), (0, 0), (0, 0), (2, 0), (0, 0), (0, 0))
    )
    own_grads = padded_grads[:, :, :, 1:-1]
    rim_grads = jnp.stack([padded_grads[:, :, :, 0], padded_grads[:, :, :, -1]], axis=3)
    returned = extended_2(rim_grads.astype(jnp.bfloat16), (("seq", 3),), 1).astype(rim_grads.dtype)
    own_grads = own_grads.at[:, :, :, 0].add(returned[:, :, :, 0])
    own_grads = own_grads.at[:, :, :, -1].add(returned[:, :, :, 3])
    global_grads = jnp.sum(key_grads(window_cols + random_cols, key_count), axis=3)
    global_grads = global_grads.transpose(0, 1, 3, 2, 4).reshape(
        2, batch_count, globals_count, columns
    )
    global_summed = global_sum(global_grads)
    inside = (local_pos >= 0) & (local_pos < tok_local)
    safe_pos = jnp.where(inside, local_pos, tok_local)
    global_local = (
        jnp.zeros((2, batch_count, tok_local, columns), f32)
        .at[:, :, safe_pos]
        .add(global_summed, mode="drop")
    )
    global_part = pair_blocks(global_local)
    target = ((which_batch * blocks_local + which_block) * heads_local + which_head).reshape(
        buffer_rows
    )
    random_grads = key_grads(window_cols, window_cols + random_cols)
    per_slot = random_grads.reshape(
        2, batch_count, heads_local, blocks_local, pick_count, BLOCK, head_dim
    )
    per_slot = per_slot.transpose(1, 2, 3, 4, 0, 5, 6).reshape(slot_count, 2, BLOCK, head_dim)
    sending = jnp.zeros((buffer_rows, 2, BLOCK, head_dim), f32).at[position].set(per_slot)
    arrived = lax.all_to_all(
        sending.astype(jnp.bfloat16), "seq", split_axis=0, concat_axis=0, tiled=True
    ).astype(sending.dtype)
    kept = jnp.where(slot_live[:, None, None, None], arrived, 0.0)
    summed = (
        jnp.zeros((batch_count * blocks_local * heads_local, 2, BLOCK, head_dim), f32)
        .at[target]
        .add(kept)
    )
    random_part = summed.reshape(
        batch_count, blocks_local, heads_local, 2, BLOCK, head_dim
    ).transpose(3, 0, 2, 1, 4, 5)
    total_grads = own_grads + random_part + global_part
    grad_key = from_blocks(total_grads[0].astype(bf16))
    grad_value = from_blocks(total_grads[1].astype(bf16))
    return (attended, from_blocks(grad_query.astype(bf16)), grad_key, grad_value)


def body(query_rows, key_rows, value_rows, grad_out, rand_blocks, global_pos):
    seq_count, head_count = lax.axis_size("seq"), lax.axis_size("head")
    batch_count, heads_local = rand_blocks.shape[:2]
    tokens = query_rows.shape[1]
    whole_heads = seq_count == 2 * heads_local and heads_local & (heads_local - 1) == 0
    whole_heads = whole_heads and heads_local > 1 and tokens & (tokens - 1) == 0
    whole_heads = whole_heads and head_count % 2 == 0 and batch_count == 1
    form = by_heads if whole_heads else by_blocks
    return form(query_rows, key_rows, value_rows, grad_out, rand_blocks, global_pos)


def solution(mesh):
    return jax.shard_map(
        body,
        mesh=mesh,
        in_specs=(
            P(None, "seq", "head"),
            P(None, "seq", "head"),
            P(None, "seq", "head"),
            P(None, "seq", "head"),
            P(None, "head", None, None),
            P(),
        ),
        out_specs=(
            P(None, "seq", "head"),
            P(None, "seq", "head"),
            P(None, "seq", "head"),
            P(None, "seq", "head"),
        ),
        check_vma=False,
    )
```
